32 devices in a mesh: dp: 16 (over z, y, x), tensor: 2 (over core).
Axes of the slice: x: 2, y: 2, z: 4, core: 2. Of those that a mesh axis runs over, the one named last changes fastest.
Arguments:
- tokens: bfloat16 [32768, 768], P(('dp', 'tensor')), may hold values from -6 to 6
- lengths: int32 [64], P('dp'), may hold values from 64 to 512, as said below
- qkv_weight: bfloat16 [3, 768, 768], P(None, None, 'tensor'), may hold values from -0.21875 to 0.21875
- qv_bias: float32 [2, 768], P(None, 'tensor'), may hold values from -3 to 3
- out_weight: bfloat16 [768, 768], P('tensor'), may hold values from -0.625 to 0.625
- out_bias: float32 [768], replicated, may hold values from -2 to 2
- first_gain: float32 [768], replicated, may hold values from 0.5 to 1.5
- first_shift: float32 [768], replicated, may hold values from -2 to 2
- up_weight: bfloat16 [768, 3072], P(None, 'tensor'), may hold values from -0.21875 to 0.21875
- up_bias: float32 [3072], P('tensor'), may hold values from -3 to 3
- down_weight: bfloat16 [3072, 768], P('tensor'), may hold values from -0.109375 to 0.109375
- down_bias: float32 [768], replicated, may hold values from -2 to 2
- second_gain: float32 [768], replicated, may hold values from 0.5 to 1.5
- second_shift: float32 [768], replicated, may hold values from -2 to 2
- cotangent: bfloat16 [32768, 768], P(('dp', 'tensor')), may hold values from -6 to 6
Outputs:
- layer_out: float32 [32768, 768], P(('dp', 'tensor'))
- grad_tokens: float32 [32768, 768], P(('dp', 'tensor'))
- grad_qkv_weight: float32 [3, 768, 768], P(None, None, 'tensor')
- grad_qv_bias: float32 [2, 768], P(None, 'tensor')
- grad_out_weight: float32 [768, 768], P('tensor')
- grad_out_bias: float32 [768], replicated
- grad_first_gain: float32 [768], replicated
- grad_first_shift: float32 [768], replicated
- grad_up_weight: float32 [768, 3072], P(None, 'tensor')
- grad_up_bias: float32 [3072], P('tensor')
- grad_down_weight: float32 [3072, 768], P('tensor')
- grad_down_bias: float32 [768], replicated
- grad_second_gain: float32 [768], replicated
- grad_second_shift: float32 [768], replicated
The draws below stay inside these ranges and needn't reach their ends.
Inputs may be any that keep to these rules, and one draw needn't show every extreme that they name: The valid positions of a sequence are its first lengths[s]; in every draw some sequence has all 512 positions valid.
All inputs are finite; a program needn't handle non-finite values.
Results may differ from the reference program's by a relative error of at most 0.019.
The reference program's roundings to bfloat16 on the way count: a program that leaves them out, or rounds other values in their place, can miss the bound.
Values may be sent and summed in bfloat16 or wider, within the bound.
A program may use at most 192 MiB of HBM per device.

```python
import jax
import jax.numpy as jnp
from jax import lax

D = 768
H = 12
HD = 64
FF = 3072
LEN = 512
SEQ_DEV = 4
SEQS = 64
TOKENS = 32768
N_DP = 16
N_TENSOR = 2


def draw_lengths(key, part):
    first_key, second_key = jax.random.split(jax.random.fold_in(key, 11))
    values = jax.random.randint(first_key, (SEQS,), max(1, LEN // 8), LEN + 1)
    place = jax.random.randint(second_key, (), 0, SEQS)
    return jnp.where(jnp.arange(SEQS) == place, LEN, values).astype(jnp.int32)


def block_scale(key, shape, cuts, low, top_value):
    def one(dim, blocks):
        draws = jax.random.uniform(jax.random.fold_in(jax.random.fold_in(key, 6), dim), (blocks,), jnp.float32, low / len(cuts), top_value / len(cuts))
        return jnp.repeat(jnp.exp(draws), shape[dim] // blocks).reshape((-1,) + (1,) * (len(shape) - dim - 1))

    level = one(*cuts[0])
    for cut in cuts[1:]:
        level = level * one(*cut)
    return level


def scatter_about(stream_key, shape, deviation, reach, shards=(), held_as=jnp.bfloat16):
    drawn = deviation * jax.random.normal(stream_key, shape, jnp.float32)
    if shards:
        drawn = drawn * block_scale(stream_key, shape, shards, -0.22, 0.18)
    return jnp.clip(drawn, -reach, reach).astype(held_as)


def setup_inputs(seed: int = 0) -> dict:
    splits = jax.random.split(jax.random.key(seed), 16)
    return {
        "tokens": scatter_about(splits[0], (TOKENS, D), 1.0, 6.0, ((0, 32),)),
        "lengths": draw_lengths(jax.random.fold_in(splits[15], 71), 0),
        "qkv_weight": scatter_about(splits[2], (3, D, D), D ** -0.5, 0.21875, ((2, 2),)),
        "qv_bias": scatter_about(splits[3], (2, D), 0.5, 3.0, ((1, 2),), jnp.float32),
        "out_weight": scatter_about(splits[4], (D, D), (D // 8) ** -0.5, 0.625, ((0, 2),)),
        "out_bias": scatter_about(splits[5], (D,), 0.3, 2.0, (), jnp.float32),
        "first_gain": jnp.clip(1.0 + 0.1 * jax.random.normal(splits[6], (D,), jnp.float32), 0.5, 1.5),
        "first_shift": scatter_about(splits[7], (D,), 0.3, 2.0, (), jnp.float32),
        "up_weight": scatter_about(splits[8], (D, FF), D ** -0.5, 0.21875, ((1, 2),)),
        "up_bias": scatter_about(splits[9], (FF,), 0.5, 3.0, ((0, 2),), jnp.float32),
        "down_weight": scatter_about(splits[10], (FF, D), FF ** -0.5, 0.109375, ((0, 2),)),
        "down_bias": scatter_about(splits[11], (D,), 0.3, 2.0, (), jnp.float32),
        "second_gain": jnp.clip(1.0 + 0.1 * jax.random.normal(splits[12], (D,), jnp.float32), 0.5, 1.5),
        "second_shift": scatter_about(splits[13], (D,), 0.3, 2.0, (), jnp.float32),
        "cotangent": scatter_about(splits[14], (TOKENS, D), 1.0, 6.0, ((0, 32),)),
    }


@jax.custom_vjp
def low(v):
    return lax.optimization_barrier(v.astype(jnp.bfloat16)).astype(jnp.float32)

@jax.custom_vjp
def low_back(v):
    return v

def low_keep(v):
    return (low(v), None)

def low_pass(kept, grad):
    return (grad,)

def back_keep(v):
    return (v, None)

def back_low(kept, grad):
    return (low(grad),)
low.defvjp(low_keep, low_pass)
low_back.defvjp(back_keep, back_low)
EPS = 1e-06
HIGH = lax.Precision.HIGHEST

def both_ways(value):
    return low(low_back(value))

def layer_norm(inputs, gain, shift):
    centre = inputs - lax.optimization_barrier(jnp.mean(inputs, axis=-1, keepdims=True))
    spread = lax.optimization_barrier(jnp.mean(centre * centre, axis=-1, keepdims=True))
    return centre * lax.rsqrt(spread + EPS) * gain + shift

def gelu_exact(inputs):
    return jax.nn.gelu(inputs, approximate=False)

def group_forward(rows_in, seq_lengths, qkv_weight, qv_bias, out_weight, out_bias, first_gain, first_shift, up_weight, up_bias, down_weight, down_bias, second_gain, second_shift):
    width = D // N_TENSOR
    hidden_width = FF // N_TENSOR
    pieces = []
    for group in range(N_TENSOR):
        copy_rows = low_back(rows_in)
        pieces.append(jnp.einsum('rd,kde->kre', copy_rows, qkv_weight[:, :, group * width:(group + 1) * width], precision=HIGH))
    projected = jnp.concatenate(pieces, axis=2)
    queries = both_ways(projected[0] + qv_bias[0])
    key_rows = both_ways(projected[1])
    value_rows = both_ways(projected[2] + qv_bias[1])
    shape_four = (SEQ_DEV, LEN, H, HD)
    raw_scores = jnp.einsum('sqhe,skhe->shqk', queries.reshape(shape_four), key_rows.reshape(shape_four), precision=HIGH)
    scores = low_back(raw_scores * HD ** (-0.5))
    is_valid = jnp.arange(LEN)[None, :] < seq_lengths[:, None]
    scores = jnp.where(is_valid[:, None, None, :], scores, -1000000000.0)
    attn_weights = jax.nn.softmax(scores, axis=-1)
    context = jnp.einsum('shqk,skhe->sqhe', low(attn_weights), value_rows.reshape(shape_four), precision=HIGH)
    context = both_ways(context).reshape(SEQ_DEV * LEN, D)
    attn_sum = jnp.zeros((SEQ_DEV * LEN, D), jnp.float32)
    for group in range(N_TENSOR):
        part_out = jnp.dot(context[:, group * width:(group + 1) * width], out_weight[group * width:(group + 1) * width], precision=HIGH)
        attn_sum = attn_sum + low(part_out)
    first_in = rows_in + low_back(attn_sum) + out_bias
    first_out = layer_norm(first_in, first_gain, first_shift)
    middle = low(first_out)
    ffn_sum = jnp.zeros((SEQ_DEV * LEN, D), jnp.float32)
    for group in range(N_TENSOR):
        copy_middle = low_back(middle)
        cols = slice(group * hidden_width, (group + 1) * hidden_width)
        up_act = low_back(jnp.dot(copy_middle, up_weight[:, cols], precision=HIGH) + up_bias[cols])
        hidden = low(gelu_exact(up_act))
        ffn_sum = ffn_sum + low(jnp.dot(hidden, down_weight[cols], precision=HIGH))
    second_in = first_out + low_back(ffn_sum) + down_bias
    return layer_norm(second_in, second_gain, second_shift)

def reference(tokens, lengths, qkv_weight, qv_bias, out_weight, out_bias, first_gain, first_shift, up_weight, up_bias, down_weight, down_bias, second_gain, second_shift, cotangent):
    params = tuple((item.astype(jnp.float32) for item in (qkv_weight, qv_bias, out_weight, out_bias, first_gain, first_shift, up_weight, up_bias, down_weight, down_bias, second_gain, second_shift)))
    grouped = tokens.astype(jnp.float32).reshape(N_DP, SEQ_DEV * LEN, D)
    group_lengths = lengths.reshape(N_DP, SEQ_DEV).astype(jnp.int32)
    checked = jax.checkpoint(group_forward)

    def whole(rows_all, *weights):

        def step(carry, element):
            return (carry, checked(element[0], element[1], *weights))
        unused, outputs = lax.scan(step, jnp.zeros((), jnp.float32), (rows_all, group_lengths))
        return outputs
    outputs, backward = jax.vjp(whole, grouped, *params)
    grads = backward(cotangent.astype(jnp.float32).reshape(N_DP, SEQ_DEV * LEN, D))
    return (outputs.reshape(TOKENS, D), grads[0].reshape(TOKENS, D), grads[1], grads[2], grads[3], grads[4], grads[5], grads[6], grads[7], grads[8], grads[9], grads[10], grads[11], grads[12])
```

```python
import functools

import jax
import jax.numpy as jnp
from jax import lax
from jax.experimental import pallas as pl
from jax.experimental.pallas import tpu as pltpu
from jax.sharding import PartitionSpec as P

HD = 64
EPS = 1e-06
BF = jnp.bfloat16
F32 = jnp.float32
NEG = -1000000000.0
JR, JC = 256, 384


def dot(a, b):
    return lax.dot_general(a, b, (((1,), (0,)), ((), ())), preferred_element_type=F32)


def dot_nt(a, b):
    return lax.dot_general(a, b, (((1,), (1,)), ((), ())), preferred_element_type=F32)


def dot_tn(a, b):
    return lax.dot_general(a, b, (((0,), (0,)), ((), ())), preferred_element_type=F32)


def half_masks(shape, dim):
    low = lax.broadcasted_iota(jnp.int32, shape, dim) % (2 * HD) < HD
    return low


def attn_kernel(qb, lens_ref, x_ref, w_ref, b_ref, q_ref, k_ref, v_ref, c_ref):
    length = lens_ref[pl.program_id(0)]
    x = x_ref[...]
    rows, width = q_ref.shape
    scale = HD ** (-0.5)
    q_ref[...] = (dot(x, w_ref[0]) + b_ref[0:1, :]).astype(BF) * jnp.asarray(scale, BF)
    k_ref[...] = dot(x, w_ref[1]).astype(BF)
    v_ref[...] = (dot(x, w_ref[2]) + b_ref[1:2, :]).astype(BF)
    for pair in range(width // 128):
        lanes = slice(pair * 128, pair * 128 + 128)
        k = k_ref[:, lanes]
        v_t = v_ref[:, lanes].T
        for block in range(rows // qb):
            span = slice(block * qb, block * qb + qb)
            q = q_ref[span, lanes]
            low = half_masks(q.shape, 1)
            zero = jnp.zeros_like(q)
            parts = []
            for head in range(2):
                q_head = jnp.where(low, q, zero) if head == 0 else jnp.where(low, zero, q)
                s = dot_nt(k, q_head)
                is_valid = lax.broadcasted_iota(jnp.int32, s.shape, 0) < length
                s = jnp.where(is_valid, s, NEG)
                top = jnp.max(s, axis=0, keepdims=True)
                e = jnp.exp(s - top)
                total = jnp.sum(e, axis=0, keepdims=True)
                c_t = dot(v_t[head * HD:(head + 1) * HD], e.astype(BF))
                parts.append(c_t * (1.0 / total))
            c_ref[span, lanes] = jnp.concatenate(parts, axis=0).T.astype(BF)


def attention(lens, x, weight, bias, qb=256):
    rows, depth = x.shape
    seqs = lens.shape[0]
    seq_len = rows // seqs
    width = weight.shape[2]
    row_spec = pl.BlockSpec((seq_len, width), lambda s, _: (s, 0))
    out = jax.ShapeDtypeStruct((rows, width), BF)
    flops = 2 * rows * depth * width * 3 + 4 * rows * seq_len * width
    return pl.pallas_call(
        functools.partial(attn_kernel, qb),
        out_shape=(out, out, out, out),
        grid_spec=pltpu.PrefetchScalarGridSpec(
            num_scalar_prefetch=1,
            grid=(seqs,),
            in_specs=[
                pl.BlockSpec((seq_len, depth), lambda s, _: (s, 0)),
                pl.BlockSpec(weight.shape, lambda s, _: (0, 0, 0)),
                pl.BlockSpec(bias.shape, lambda s, _: (0, 0)),
            ],
            out_specs=[row_spec] * 4,
        ),
        compiler_params=pltpu.CompilerParams(vmem_limit_bytes=56 << 20),
        cost_estimate=pl.CostEstimate(flops=flops * 3, bytes_accessed=12 << 20, transcendentals=rows * seq_len * width // HD),
        name="attend",
    )(lens, x, weight, bias)


def norm_stats(rows_in):
    centre = rows_in - jnp.mean(rows_in, axis=-1, keepdims=True)
    spread = jnp.mean(centre * centre, axis=-1, keepdims=True)
    root = lax.rsqrt(spread + EPS)
    return centre * root, root


def norm_back(grad, normed, root):
    first = jnp.mean(grad, axis=-1, keepdims=True)
    second = jnp.mean(grad * normed, axis=-1, keepdims=True)
    return root * (grad - first - normed * second)


def gelu_both(u):
    z = jnp.abs(u) * (0.5 ** 0.5)
    t = 1.0 / (1.0 + 0.3275911 * z)
    poly = 1.061405429 * t - 1.453152027
    poly = poly * t + 1.421413741
    poly = poly * t - 0.284496736
    poly = poly * t + 0.254829592
    bell = jnp.exp(-0.5 * (u * u))
    tail = 0.5 * (poly * t) * bell
    phi_cdf = jnp.where(u < 0.0, tail, 1.0 - tail)
    return u * phi_cdf, phi_cdf + u * (bell * 0.3989422804014327)


def ffn_kernel(
    chunk,
    c_own, c_peer, x_ref, cot_ref, wo_own, wo_peer, wu_own, wu_peer, bu_own, bu_peer, wd_own, wd_peer, vec_ref,
    out_ref, h_own, h_peer, gu_own, gu_peer, mid_ref, glow_ref, flow_ref, gctx_ref, gf_ref, small_ref,
    gp_ref,
):
    step = pl.program_id(0)
    wide = wu_own.shape[1]
    out_bias, gain1, shift1, down_bias, gain2, shift2 = (vec_ref[i:i + 1, :] for i in range(6))

    @pl.when(step == 0)
    def _():
        small_ref[...] = jnp.zeros_like(small_ref)

    def colsum(index, value):
        small_ref[index:index + 1, :] += jnp.sum(value, axis=0, keepdims=True)

    attn_sum = dot(c_own[...], wo_own[...]) + dot(c_peer[...], wo_peer[...])
    n1, root1 = norm_stats(x_ref[...].astype(F32) + attn_sum + out_bias)
    first_out = n1 * gain1 + shift1
    middle = first_out.astype(BF)
    mid_ref[...] = middle
    ffn_sum = jnp.zeros_like(first_out)
    groups = ((wu_own, bu_own, wd_own, h_own, gu_own, 0), (wu_peer, bu_peer, wd_peer, h_peer, gu_peer, wide))
    for wu, bu, wd, h_ref, _, base in groups:
        for at in range(0, wide, chunk):
            cols = slice(at, at + chunk)
            u = dot(middle, wu[:, cols]) + bu[:, cols]
            act, slope = gelu_both(u)
            act = act.astype(BF)
            h_ref[:, cols] = act
            gp_ref[:, base + at:base + at + chunk] = slope
            ffn_sum = ffn_sum + dot(act, wd[cols, :])
    n2, root2 = norm_stats(first_out + ffn_sum + down_bias)
    out_ref[...] = n2 * gain2 + shift2
    cot = cot_ref[...].astype(F32)
    colsum(4, cot * n2)
    colsum(5, cot)
    grad_second = norm_back(cot * gain2, n2, root2)
    colsum(3, grad_second)
    glow = grad_second.astype(BF)
    glow_ref[...] = glow
    grad_first_out = grad_second
    for wu, _, wd, _, gu_ref, base in groups:
        for at in range(0, wide, chunk):
            cols = slice(at, at + chunk)
            grad_hidden = dot_nt(glow, wd[cols, :])
            gu = (grad_hidden * gp_ref[:, base + at:base + at + chunk]).astype(BF)
            gu_ref[:, cols] = gu
            colsum(8 + (base + at) // chunk, gu.astype(F32))
            grad_first_out = grad_first_out + dot_nt(gu, wu[:, cols])
    colsum(1, grad_first_out * n1)
    colsum(2, grad_first_out)
    grad_first = norm_back(grad_first_out * gain1, n1, root1)
    colsum(0, grad_first)
    gf_ref[...] = grad_first
    flow = grad_first.astype(BF)
    flow_ref[...] = flow
    half = wo_own.shape[0]
    gctx_ref[:, :half] = dot_nt(flow, wo_own[...]).astype(BF)
    gctx_ref[:, half:] = dot_nt(flow, wo_peer[...]).astype(BF)


def ffn(c_own, c_peer, x, cot, wo_own, wo_peer, wu_own, wu_peer, bu_own, bu_peer, wd_own, wd_peer, vecs, tile=256):
    rows, depth = x.shape
    half = c_own.shape[1]
    wide = wu_own.shape[1]
    chunk = depth

    def tiled(cols):
        return pl.BlockSpec((tile, cols), lambda i: (i, 0))

    def fixed(shape):
        return pl.BlockSpec(shape, lambda i: (0, 0), pipeline_mode=pl.Buffered(1))

    def sds(cols, dtype):
        return jax.ShapeDtypeStruct((rows, cols), dtype)

    fixed_in = (wo_own, wo_peer, wu_own, wu_peer, bu_own, bu_peer, wd_own, wd_peer, vecs)
    return pl.pallas_call(
        functools.partial(ffn_kernel, chunk),
        grid=(rows // tile,),
        out_shape=(
            sds(depth, F32), sds(wide, BF), sds(wide, BF), sds(wide, BF), sds(wide, BF),
            sds(depth, BF), sds(depth, BF), sds(depth, BF), sds(2 * half, BF), sds(depth, F32),
            jax.ShapeDtypeStruct((16, depth), F32),
        ),
        in_specs=[tiled(half), tiled(half), tiled(depth), tiled(depth)] + [fixed(a.shape) for a in fixed_in],
        out_specs=[
            tiled(depth), tiled(wide), tiled(wide), tiled(wide), tiled(wide),
            tiled(depth), tiled(depth), tiled(depth), tiled(2 * half), tiled(depth),
            pl.BlockSpec((16, depth), lambda i: (0, 0)),
        ],
        scratch_shapes=[pltpu.VMEM((tile, 2 * wide), F32)],
        compiler_params=pltpu.CompilerParams(vmem_limit_bytes=60 << 20),
        cost_estimate=pl.CostEstimate(flops=rows * depth * (8 * 2 * wide + 8 * depth), bytes_accessed=48 << 20, transcendentals=rows * wide * 2),
        name="feed",
    )(c_own, c_peer, x, cot, *fixed_in)


LAGS = (1, 3, 5, 6, 8, 10, 11, 12, 14)
GROUPS = 12
JOBS = 3 * GROUPS


def back_kernel(
    levels,
    lens_ref, h_own, h_peer, gu_own, gu_peer, glow_in, mid_in, flow_in, c_own, c_peer, q_own, q_peer, k_own, k_peer, v_own, v_peer, gctx_in, x_in, w_own, w_peer, small_in,
    job_out, dx_out, small_out,
    buf, ring, prec, rbuf, blocks, glow, mid, flow, ctx, qv, kv, vv, dov, xv, wv, dq, dk, dv, dxs, small, small_sum, small_send, small_recv,
    load_sem, blk_sem, core_send, core_recv, hop_send, hop_recv, out_sem, dx_sem, small_sem, sum_send, sum_recv,
):
    dp = lax.axis_index("dp")
    core = lax.axis_index("tensor")
    half = ctx.shape[1] // 2
    rows, depth = glow.shape
    seqs = lens_ref.shape[0]
    seq_len = rows // seqs
    pairs = qv.shape[1] // 128
    scale = HD ** (-0.5)
    other = (dp, 1 - core)

    def partner(level, job):
        flip = job % 2
        mask = (1 + flip, 4, 2 - flip, 8)[level]
        bit = (dp // mask) % 2
        return bit, (dp + mask * (1 - 2 * bit), core)

    def loads():
        return (
            (glow_in, glow, 0), (mid_in, mid, 1), (c_own, ctx.at[:, :half], 2), (c_peer, ctx.at[:, half:], 3), (flow_in, flow, 4),
            (q_own, qv.at[:, :half], 5), (q_peer, qv.at[:, half:], 6), (k_own, kv.at[:, :half], 7), (k_peer, kv.at[:, half:], 8),
            (v_own, vv.at[:, :half], 9), (v_peer, vv.at[:, half:], 10), (gctx_in, dov, 11), (x_in, xv, 12), (w_own, wv.at[0], 13), (w_peer, wv.at[1], 14), (small_in, small, 15),
        )

    def load(index):
        src, dst, sem = loads()[index]
        return pltpu.make_async_copy(src, dst, load_sem.at[sem])

    def block_copies(src_own, src_peer, index, slot):
        cols = pl.ds(pl.multiple_of(index * JC, 128), JC)
        return (
            pltpu.make_async_copy(src_own.at[:, cols], blocks.at[slot, 0], blk_sem.at[slot, 0]),
            pltpu.make_async_copy(src_peer.at[:, cols], blocks.at[slot, 1], blk_sem.at[slot, 1]),
        )

    def start_blocks(index):
        @pl.when(index < 4)
        def _():
            for copy in block_copies(h_own, h_peer, index, index % 2):
                copy.start()

        @pl.when((index >= 4) & (index < 8))
        def _():
            for copy in block_copies(gu_own, gu_peer, index - 4, index % 2):
                copy.start()

    def core_copy(job):
        return pltpu.make_async_remote_copy(
            src_ref=ring.at[job % 9], dst_ref=prec.at[job], send_sem=core_send.at[job], recv_sem=core_recv.at[job],
            device_id=other, device_id_type=pl.DeviceIdType.MESH,
        )

    def offsets(job):
        spots = [0]
        for level in range(levels):
            bit, _ = partner(level, job)
            spots.append(spots[-1] + bit * (JR >> (level + 1)))
        return spots

    def hop(job, stage):
        if stage < levels:
            level = stage
            size = JR >> (level + 1)
            bit, device = partner(level, job)
            at = pl.multiple_of(offsets(job)[level] + (1 - bit) * size, 16)
            src = buf.at[job, pl.ds(at, size)]
            begin = JR - (JR >> level)
            dst = rbuf.at[job, begin:begin + size]
        else:
            level = 2 * levels - 1 - stage
            size = JR >> (level + 1)
            bit, device = partner(level, job)
            at = pl.multiple_of(offsets(job)[level + 1], 16)
            src = prec.at[job, pl.ds(at, size)]
            dst = prec.at[job, pl.ds(at, size)]
        return pltpu.make_async_remote_copy(
            src_ref=src, dst_ref=dst, send_sem=hop_send.at[stage, job], recv_sem=hop_recv.at[stage, job],
            device_id=device, device_id_type=pl.DeviceIdType.MESH,
        )

    def stage_op(stage, job):
        if stage == 0:
            core_copy(job).wait_recv()
            buf[job] = (buf[job].astype(F32) + prec[job].astype(F32)).astype(BF)
            hop(job, 0).start()
            return
        before = hop(job, stage - 1)
        before.wait_recv()
        before.wait_send()
        if stage <= levels:
            level = stage - 1
            size = JR >> stage
            at = pl.multiple_of(offsets(job)[stage], 16)
            begin = JR - (JR >> level)
            keep = buf[job, pl.ds(at, size)].astype(F32) + rbuf[job, begin:begin + size].astype(F32)
            target = prec if stage == levels else buf
            target[job, pl.ds(at, size)] = keep.astype(BF)
        if stage < 2 * levels:
            hop(job, stage).start()
        else:
            pltpu.make_async_copy(prec.at[job], job_out.at[job], out_sem.at[job]).start()

    def emit(group, own, peer):
        for which, pieces in ((0, own), (1, peer)):
            for i, (top, bottom) in enumerate(pieces):
                job = group * 3 + i
                if which == 0:
                    target = buf.at[job]
                else:
                    target = ring.at[job % 9]
                cut = top.shape[0]
                target[:cut, :] = top.astype(BF)
                if bottom is not None:
                    target[cut:, :] = bottom.astype(BF)
                if which == 1:
                    core_copy(job).start()

    def free_ring(group):
        @pl.when(group >= 3)
        def _():
            for i in range(3):
                core_copy((group - 3) * 3 + i).wait_send()

    def slabs(block):
        return [(block[i * 128:(i + 1) * 128, :JC], block[i * 128:(i + 1) * 128, JC:]) for i in range(3)]

    def tall(block):
        return [(block[i * JR:(i + 1) * JR], None) for i in range(3)]

    def down_phase(index):
        @pl.when(index == 0)
        def _():
            load(0).wait()

        for copy in block_copies(h_own, h_peer, index, index % 2):
            copy.wait()
        free_ring(index)
        right = glow[...]
        slot = index % 2
        emit(index, slabs(dot_tn(blocks[slot, 0], right)), slabs(dot_tn(blocks[slot, 1], right)))
        start_blocks(index + 2)

    def up_phase(index):
        @pl.when(index == 0)
        def _():
            load(1).wait()

        slot = index % 2
        for copy in block_copies(gu_own, gu_peer, index, slot):
            copy.wait()
        free_ring(index + 4)
        left = mid[...]
        emit(index + 4, tall(dot_tn(left, blocks[slot, 0])), tall(dot_tn(left, blocks[slot, 1])))
        start_blocks(index + 6)

    def out_phase():
        for i in (2, 3, 4):
            load(i).wait()
        free_ring(8)
        right = flow[...]
        emit(8, slabs(dot_tn(ctx[:, :half], right)), slabs(dot_tn(ctx[:, half:], right)))

    def add_bias(pair, offset, value):
        total = jnp.sum(value.astype(F32), axis=0, keepdims=True)
        for side in range(2):
            @pl.when(pair // (pairs // 2) == side)
            def _():
                lanes = pl.ds(pl.multiple_of(offset + (pair - side * (pairs // 2)) * 128, 128), 128)
                small[12 + side:13 + side, lanes] += total

    def sum_hop(stage):
        if stage == 0:
            src, device = small_send, other
        else:
            src, device = small_sum.at[stage - 1], partner(stage - 1, 0)[1]
        return pltpu.make_async_remote_copy(
            src_ref=src, dst_ref=small_recv.at[stage], send_sem=sum_send.at[stage], recv_sem=sum_recv.at[stage],
            device_id=device, device_id_type=pl.DeviceIdType.MESH,
        )

    def sum_phase(stage):
        if stage == 0:
            small_send[0:8, :] = small[0:8, :]
            small_send[8:10, :] = small[10:12, :]
            small_send[10:11, :] = small[13:14, :]
            small_send[11:16, :] = jnp.zeros((5, depth), F32)
        else:
            sum_hop(stage - 1).wait_recv()
            sum_hop(stage - 1).wait_send()
            if stage == 1:
                got = small_recv[0]
                small_sum[0, 0:8, :] = small[0:8, :] + got[0:8, :]
                small_sum[0, 8:10, :] = small[8:10, :] + got[8:10, :]
                small_sum[0, 10:11, :] = small[12:13, :] + got[10:11, :]
                small_sum[0, 11:16, :] = jnp.zeros((5, depth), F32)
            else:
                small_sum[stage - 1] = small_sum[stage - 2] + small_recv[stage - 1]
        if stage <= levels:
            sum_hop(stage).start()
        else:
            pltpu.make_async_copy(small_sum.at[levels], small_out, small_sem).start()

    def attend_phase(unit):
        @pl.when(unit == 0)
        def _():
            for i in range(5, 12):
                load(i).wait()
            load(15).wait()
            small[12:14, :] = jnp.zeros((2, depth), F32)

        seq = unit // pairs
        pair = unit % pairs
        length = lens_ref[seq]
        span = pl.ds(pl.multiple_of(seq * seq_len, seq_len), seq_len)
        lanes = pl.ds(pl.multiple_of(pair * 128, 128), 128)
        k = kv[span, lanes]
        v = vv[span, lanes]
        k_t = k.T
        low = half_masks((1, 128), 1)
        qb = seq_len // 2
        grad_k = jnp.zeros((seq_len, 128), F32)
        grad_v = jnp.zeros((seq_len, 128), F32)
        for block in range(2):
            part = pl.ds(pl.multiple_of(seq * seq_len + block * qb, qb), qb)
            q = qv[part, lanes]
            do = dov[part, lanes]
            grad_q = []
            for head in range(2):
                pick = low if head == 0 else jnp.logical_not(low)
                q_head = jnp.where(pick, q, jnp.zeros_like(q))
                do_head = jnp.where(pick, do, jnp.zeros_like(do))
                s = dot_nt(k, q_head)
                is_valid = lax.broadcasted_iota(jnp.int32, s.shape, 0) < length
                s = jnp.where(is_valid, s, NEG)
                e = jnp.exp(s - jnp.max(s, axis=0, keepdims=True))
                weights = e * (1.0 / jnp.sum(e, axis=0, keepdims=True))
                grad_probs = dot_nt(v, do_head)
                grad_v = grad_v + dot(weights.astype(BF), do_head)
                row_terms = jnp.sum(weights * grad_probs, axis=0, keepdims=True)
                grad_s = (weights * (grad_probs - row_terms)).astype(BF)
                grad_k = grad_k + dot(grad_s, q_head)
                grad_q.append(dot(k_t[head * HD:(head + 1) * HD], grad_s) * scale)
            grad_q = jnp.concatenate(grad_q, axis=0).T.astype(BF)
            dq[part, lanes] = grad_q
            add_bias(pair, 0, grad_q)
        grad_v = grad_v.astype(BF)
        dk[span, lanes] = grad_k.astype(BF)
        dv[span, lanes] = grad_v
        add_bias(pair, half, grad_v)

    def proj_phase(index):
        if index == 0:
            load(12).wait()
        free_ring(jnp.int32(index + 9))
        left = xv[...]
        grad = (dq, dk, dv)[index]
        emit(index + 9, tall(dot_tn(left, grad[:, :half])), tall(dot_tn(left, grad[:, half:])))

    def dx_copy(index):
        span = pl.ds(pl.multiple_of(index * JR, JR), JR)
        return pltpu.make_async_copy(dxs.at[index % 2], dx_out.at[span], dx_sem.at[index % 2])

    def dx_phase(index):
        @pl.when(index == 0)
        def _():
            load(13).wait()
            load(14).wait()

        @pl.when(index >= 2)
        def _():
            dx_copy(index - 2).wait()

        span = pl.ds(pl.multiple_of(index * JR, JR), JR)
        total = jnp.zeros((JR, depth), F32)
        for side in range(2):
            cols = slice(side * half, side * half + half)
            part = jnp.zeros((JR, depth), F32)
            for i, grad in enumerate((dq, dk, dv)):
                part = part + dot_nt(grad[span, cols], wv[side, i])
            total = total + part
        dxs[index % 2] = total
        dx_copy(index).start()

    barrier = pltpu.get_barrier_semaphore()
    pl.semaphore_signal(barrier, inc=1, device_id=other, device_id_type=pl.DeviceIdType.MESH)
    for level in range(levels):
        pl.semaphore_signal(barrier, inc=1, device_id=partner(level, 0)[1], device_id_type=pl.DeviceIdType.MESH)
    load(0).start()
    start_blocks(0)
    start_blocks(1)
    for i in range(1, 16):
        load(i).start()
    pl.semaphore_wait(barrier, levels + 1)

    units = seqs * pairs
    first = 9 + units
    ticks = max(JOBS + LAGS[2 * levels], first + 3 + rows // JR)

    def tick(t, carry):
        for stage in range(2 * levels, -1, -1):
            job = t - LAGS[stage]

            @pl.when((job >= 0) & (job < JOBS))
            def _():
                stage_op(stage, job)

        @pl.when(t < 4)
        def _():
            down_phase(t)

        @pl.when((t >= 4) & (t < 8))
        def _():
            up_phase(t - 4)

        @pl.when(t == 8)
        def _():
            out_phase()

        @pl.when((t >= 9) & (t < first))
        def _():
            attend_phase(t - 9)

        for i in range(3):
            @pl.when(t == first + i)
            def _():
                proj_phase(i)

        @pl.when((t >= first + 3) & (t < first + 3 + rows // JR))
        def _():
            dx_phase(t - first - 3)

        for stage in range(levels + 2):
            @pl.when(t == first + 1 + 2 * stage)
            def _():
                sum_phase(stage)

        return carry

    lax.fori_loop(0, ticks, tick, 0)
    for group in (GROUPS - 3, GROUPS - 2, GROUPS - 1):
        for i in range(3):
            core_copy(group * 3 + i).wait_send()
    dx_copy(rows // JR - 2).wait()
    dx_copy(rows // JR - 1).wait()

    def finish(job, carry):
        pltpu.make_async_copy(prec.at[job], job_out.at[job], out_sem.at[job]).wait()
        return carry

    lax.fori_loop(0, JOBS, finish, 0)
    pltpu.make_async_copy(small_sum.at[levels], small_out, small_sem).wait()


def backward(levels, lens, arrays):
    h_own, glow, c_own, x = arrays[0], arrays[4], arrays[7], arrays[16]
    rows, depth = glow.shape
    half = c_own.shape[1]
    hbm = pl.BlockSpec(memory_space=pl.ANY)
    square = pltpu.VMEM((rows, depth), BF)
    dma = pltpu.SemaphoreType.DMA
    return pl.pallas_call(
        functools.partial(back_kernel, levels),
        out_shape=(
            jax.ShapeDtypeStruct((JOBS, JR, JC), BF),
            jax.ShapeDtypeStruct((rows, depth), F32),
            jax.ShapeDtypeStruct((16, depth), F32),
        ),
        in_specs=[pl.BlockSpec(memory_space=pltpu.SMEM)] + [hbm] * len(arrays),
        out_specs=(hbm, hbm, hbm),
        scratch_shapes=[
            pltpu.VMEM((JOBS, JR, JC), BF), pltpu.VMEM((9, JR, JC), BF), pltpu.VMEM((JOBS, JR, JC), BF),
            pltpu.VMEM((JOBS, JR - (JR >> levels), JC), BF), pltpu.VMEM((2, 2, rows, JC), BF),
            square, square, square, square, square, square, square, square, square,
            pltpu.VMEM((2, 3, depth, half), BF), square, square, square,
            pltpu.VMEM((2, JR, depth), F32), pltpu.VMEM((16, depth), F32),
            pltpu.VMEM((levels + 1, 16, depth), F32), pltpu.VMEM((16, depth), F32), pltpu.VMEM((levels + 1, 16, depth), F32),
            dma((16,)), dma((2, 2)), dma((JOBS,)), dma((JOBS,)), dma((2 * levels, JOBS)), dma((2 * levels, JOBS)), dma((JOBS,)), dma((2,)), dma(()), dma((levels + 1,)), dma((levels + 1,)),
        ],
        compiler_params=pltpu.CompilerParams(vmem_limit_bytes=67043328, collective_id=1, has_side_effects=True),
        cost_estimate=pl.CostEstimate(flops=60 << 30, bytes_accessed=64 << 20, transcendentals=8 << 20),
        name="backward",
    )(lens, *arrays)


def unpack_kernel(jobs_ref, gf_ref, dx_ref, small_ref, tok_ref, qkv_ref, qvb_ref, out_ref, up_ref, upb_ref, down_ref, *vec_refs):
    step = pl.program_id(0)

    def unslab(target):
        for i in range(3):
            rows = slice(i * 128, i * 128 + 128)
            target[rows, :JC] = jobs_ref[i, :128, :].astype(F32)
            target[rows, JC:] = jobs_ref[i, 128:, :].astype(F32)

    def tall(store):
        for i in range(3):
            store(i, jobs_ref[i].astype(F32))

    @pl.when(step < 4)
    def _():
        unslab(down_ref)
        tok_ref[...] = gf_ref[...] + dx_ref[...]

    @pl.when((step >= 4) & (step < 8))
    def _():
        for i in range(3):
            up_ref[i * JR:(i + 1) * JR, :] = jobs_ref[i].astype(F32)

    @pl.when(step == 8)
    def _():
        unslab(out_ref)
        for i, ref in enumerate(vec_refs):
            ref[...] = small_ref[i:i + 1, :]
        upb_ref[...] = small_ref[8:10, :]
        qvb_ref[0:1, :] = small_ref[10:11, :JC]
        qvb_ref[1:2, :] = small_ref[10:11, JC:]

    @pl.when(step >= 9)
    def _():
        for i in range(3):
            qkv_ref[0, i * JR:(i + 1) * JR, :] = jobs_ref[i].astype(F32)


def unpack(jobs, grad_first, dx, small, wide):
    rows, depth = grad_first.shape

    def rows_at(i):
        return (jnp.minimum(i, 3), 0)

    quarter = pl.BlockSpec((rows // 4, depth), rows_at)

    def whole(shape):
        return pl.BlockSpec(shape, lambda i: (0, 0))

    vec = jax.ShapeDtypeStruct((1, depth), F32)
    return pl.pallas_call(
        unpack_kernel,
        grid=(GROUPS,),
        out_shape=(
            jax.ShapeDtypeStruct((rows, depth), F32), jax.ShapeDtypeStruct((3, depth, JC), F32), jax.ShapeDtypeStruct((2, JC), F32),
            jax.ShapeDtypeStruct((JC, depth), F32), jax.ShapeDtypeStruct((depth, wide), F32), jax.ShapeDtypeStruct((2, depth), F32),
            jax.ShapeDtypeStruct((wide, depth), F32), vec, vec, vec, vec, vec, vec,
        ),
        in_specs=[pl.BlockSpec((3, JR, JC), lambda i: (i, 0, 0)), quarter, quarter, whole((16, depth))],
        out_specs=[
            quarter, pl.BlockSpec((1, depth, JC), lambda i: (jnp.clip(i - 9, 0, 2), 0, 0)), whole((2, JC)), whole((JC, depth)),
            pl.BlockSpec((depth, JC), lambda i: (0, jnp.clip(i - 4, 0, 3))), whole((2, depth)), pl.BlockSpec((JC, depth), rows_at),
        ] + [whole((1, depth))] * 6,
        name="unpack",
    )(jobs, grad_first, dx, small)


def body(tokens, lengths, qkv_weight, qv_bias, out_weight, out_bias, first_gain, first_shift, up_weight, up_bias, down_weight, down_bias, second_gain, second_shift, cotangent):
    n_tensor = lax.axis_size("tensor")
    n_dp = lax.axis_size("dp")
    core = lax.axis_index("tensor")
    seqs = lengths.shape[0] // n_tensor
    lens = lax.dynamic_slice(lengths, (core * seqs,), (seqs,))
    levels = 4

    def swap(value):
        return lax.ppermute(value, "tensor", [(0, 1), (1, 0)])

    up_row = up_bias.reshape(1, -1)
    peer_qkv, peer_qv_bias = swap(qkv_weight), swap(qv_bias)
    peer_out, peer_up, peer_up_row, peer_down = swap(out_weight), swap(up_weight), swap(up_row), swap(down_weight)
    q_own, k_own, v_own, c_own = attention(lens, tokens, qkv_weight, qv_bias)
    q_peer, k_peer, v_peer, c_peer = attention(lens, tokens, peer_qkv, peer_qv_bias)
    vecs = jnp.stack([out_bias, first_gain, first_shift, down_bias, second_gain, second_shift, out_bias, out_bias])
    layer_out, h_own, h_peer, gu_own, gu_peer, mid, glow, flow, gctx, grad_first, sums = ffn(
        c_own, c_peer, tokens, cotangent, out_weight, peer_out, up_weight, peer_up, up_row, peer_up_row, down_weight, peer_down, vecs
    )
    jobs, dx, sums = backward(
        levels, lens,
        (h_own, h_peer, gu_own, gu_peer, glow, mid, flow, c_own, c_peer, q_own, q_peer, k_own, k_peer, v_own, v_peer, gctx, tokens, qkv_weight, peer_qkv, sums),
    )
    inner = 1 << levels
    if n_dp > inner:
        groups = [[i + inner * g for g in range(n_dp // inner)] for i in range(inner)]
        jobs, sums = lax.psum((jobs, sums), "dp", axis_index_groups=groups)
    grad_tokens, grad_qkv, grad_qv_bias, grad_out, grad_up, grad_up_bias, grad_down, *vectors = unpack(jobs, grad_first, dx, sums, up_bias.shape[0])
    vectors = [item.reshape(-1) for item in vectors]
    return (
        layer_out, grad_tokens, grad_qkv, grad_qv_bias, grad_out, vectors[0], vectors[1], vectors[2],
        grad_up, grad_up_bias.reshape(-1), grad_down, vectors[3], vectors[4], vectors[5],
    )


def solution(mesh):
    tokens = P(("dp", "tensor"), None)
    columns = P(None, "tensor")
    cube = P(None, None, "tensor")
    split = P("tensor", None)
    return jax.shard_map(
        body,
        mesh=mesh,
        in_specs=(tokens, P("dp"), cube, columns, split, P(), P(), P(), columns, P("tensor"), split, P(), P(), P(), tokens),
        out_specs=(tokens, tokens, cube, columns, split, P(), P(), P(), columns, P("tensor"), split, P(), P(), P()),
        check_vma=False,
    )
```

```python
import functools

import jax
import jax.numpy as jnp
from jax import lax
from jax.experimental import pallas as pl
from jax.experimental.pallas import tpu as pltpu
from jax.sharding import PartitionSpec as P

HD = 64
EPS = 1e-06
BF = jnp.bfloat16
F32 = jnp.float32
NEG = -1000000000.0
JR, JC = 256, 384


def dot(a, b):
    return lax.dot_general(a, b, (((1,), (0,)), ((), ())), preferred_element_type=F32)


def dot_nt(a, b):
    return lax.dot_general(a, b, (((1,), (1,)), ((), ())), preferred_element_type=F32)


def dot_tn(a, b):
    return lax.dot_general(a, b, (((0,), (0,)), ((), ())), preferred_element_type=F32)


def half_masks(shape, dim):
    low = lax.broadcasted_iota(jnp.int32, shape, dim) % (2 * HD) < HD
    return low


def attn_kernel(qb, lens_ref, x_ref, w_ref, b_ref, q_ref, k_ref, v_ref, c_ref):
    length = lens_ref[pl.program_id(0)]
    x = x_ref[...]
    rows, width = q_ref.shape
    scale = HD ** (-0.5)
    q_ref[...] = (dot(x, w_ref[0]) + b_ref[0:1, :]).astype(BF) * jnp.asarray(scale, BF)
    k_ref[...] = dot(x, w_ref[1]).astype(BF)
    v_ref[...] = (dot(x, w_ref[2]) + b_ref[1:2, :]).astype(BF)
    for pair in range(width // 128):
        lanes = slice(pair * 128, pair * 128 + 128)
        k = k_ref[:, lanes]
        v_t = v_ref[:, lanes].T
        for block in range(rows // qb):
            span = slice(block * qb, block * qb + qb)
            q = q_ref[span, lanes]
            low = half_masks(q.shape, 1)
            zero = jnp.zeros_like(q)
            parts = []
            for head in range(2):
                q_head = jnp.where(low, q, zero) if head == 0 else jnp.where(low, zero, q)
                s = dot_nt(k, q_head)
                is_valid = lax.broadcasted_iota(jnp.int32, s.shape, 0) < length
                s = jnp.where(is_valid, s, NEG)
                top = jnp.max(s, axis=0, keepdims=True)
                e = jnp.exp(s - top)
                total = jnp.sum(e, axis=0, keepdims=True)
                c_t = dot(v_t[head * HD:(head + 1) * HD], e.astype(BF))
                parts.append(c_t * (1.0 / total))
            c_ref[span, lanes] = jnp.concatenate(parts, axis=0).T.astype(BF)


def attention(lens, x, weight, bias, qb=512):
    rows, depth = x.shape
    seqs = lens.shape[0]
    seq_len = rows // seqs
    width = weight.shape[2]
    row_spec = pl.BlockSpec((seq_len, width), lambda s, _: (s, 0))
    out = jax.ShapeDtypeStruct((rows, width), BF)
    flops = 2 * rows * depth * width * 3 + 4 * rows * seq_len * width
    return pl.pallas_call(
        functools.partial(attn_kernel, qb),
        out_shape=(out, out, out, out),
        grid_spec=pltpu.PrefetchScalarGridSpec(
            num_scalar_prefetch=1,
            grid=(seqs,),
            in_specs=[
                pl.BlockSpec((seq_len, depth), lambda s, _: (s, 0)),
                pl.BlockSpec(weight.shape, lambda s, _: (0, 0, 0)),
                pl.BlockSpec(bias.shape, lambda s, _: (0, 0)),
            ],
            out_specs=[row_spec] * 4,
        ),
        compiler_params=pltpu.CompilerParams(vmem_limit_bytes=56 << 20),
        cost_estimate=pl.CostEstimate(flops=flops * 3, bytes_accessed=12 << 20, transcendentals=rows * seq_len * width // HD),
        name="attend",
    )(lens, x, weight, bias)


def norm_stats(rows_in):
    centre = rows_in - jnp.mean(rows_in, axis=-1, keepdims=True)
    spread = jnp.mean(centre * centre, axis=-1, keepdims=True)
    root = lax.rsqrt(spread + EPS)
    return centre * root, root


def norm_back(grad, normed, root):
    first = jnp.mean(grad, axis=-1, keepdims=True)
    second = jnp.mean(grad * normed, axis=-1, keepdims=True)
    return root * (grad - first - normed * second)


def gelu_both(u):
    z = jnp.abs(u) * (0.5 ** 0.5)
    t = 1.0 / (1.0 + 0.3275911 * z)
    poly = 1.061405429 * t - 1.453152027
    poly = poly * t + 1.421413741
    poly = poly * t - 0.284496736
    poly = poly * t + 0.254829592
    bell = jnp.exp(-0.5 * (u * u))
    tail = 0.5 * (poly * t) * bell
    phi_cdf = jnp.where(u < 0.0, tail, 1.0 - tail)
    return u * phi_cdf, phi_cdf + u * (bell * 0.3989422804014327)


def ffn_kernel(
    chunk,
    c_own, c_peer, x_ref, cot_ref, wo_own, wo_peer, wu_own, wu_peer, bu_own, bu_peer, wd_own, wd_peer, vec_ref,
    out_ref, h_own, h_peer, gu_own, gu_peer, mid_ref, glow_ref, flow_ref, gctx_ref, gf_ref, small_ref,
    gp_ref,
):
    step = pl.program_id(0)
    wide = wu_own.shape[1]
    out_bias, gain1, shift1, down_bias, gain2, shift2 = (vec_ref[i:i + 1, :] for i in range(6))

    @pl.when(step == 0)
    def _():
        small_ref[...] = jnp.zeros_like(small_ref)

    def colsum(index, value):
        small_ref[index:index + 1, :] += jnp.sum(value, axis=0, keepdims=True)

    attn_sum = dot(c_own[...], wo_own[...]) + dot(c_peer[...], wo_peer[...])
    n1, root1 = norm_stats(x_ref[...].astype(F32) + attn_sum + out_bias)
    first_out = n1 * gain1 + shift1
    middle = first_out.astype(BF)
    mid_ref[...] = middle
    ffn_sum = jnp.zeros_like(first_out)
    groups = ((wu_own, bu_own, wd_own, h_own, gu_own, 0), (wu_peer, bu_peer, wd_peer, h_peer, gu_peer, wide))
    for wu, bu, wd, h_ref, _, base in groups:
        for at in range(0, wide, chunk):
            cols = slice(at, at + chunk)
            u = dot(middle, wu[:, cols]) + bu[:, cols]
            act, slope = gelu_both(u)
            act = act.astype(BF)
            h_ref[:, cols] = act
            gp_ref[:, base + at:base + at + chunk] = slope
            ffn_sum = ffn_sum + dot(act, wd[cols, :])
    n2, root2 = norm_stats(first_out + ffn_sum + down_bias)
    out_ref[...] = n2 * gain2 + shift2
    cot = cot_ref[...].astype(F32)
    colsum(4, cot * n2)
    colsum(5, cot)
    grad_second = norm_back(cot * gain2, n2, root2)
    colsum(3, grad_second)
    glow = grad_second.astype(BF)
    glow_ref[...] = glow
    grad_first_out = grad_second
    for wu, _, wd, _, gu_ref, base in groups:
        for at in range(0, wide, chunk):
            cols = slice(at, at + chunk)
            grad_hidden = dot_nt(glow, wd[cols, :])
            gu = (grad_hidden * gp_ref[:, base + at:base + at + chunk]).astype(BF)
            gu_ref[:, cols] = gu
            colsum(8 + (base + at) // chunk, gu.astype(F32))
            grad_first_out = grad_first_out + dot_nt(gu, wu[:, cols])
    colsum(1, grad_first_out * n1)
    colsum(2, grad_first_out)
    grad_first = norm_back(grad_first_out * gain1, n1, root1)
    colsum(0, grad_first)
    gf_ref[...] = grad_first
    flow = grad_first.astype(BF)
    flow_ref[...] = flow
    half = wo_own.shape[0]
    gctx_ref[:, :half] = dot_nt(flow, wo_own[...]).astype(BF)
    gctx_ref[:, half:] = dot_nt(flow, wo_peer[...]).astype(BF)


def ffn(c_own, c_peer, x, cot, wo_own, wo_peer, wu_own, wu_peer, bu_own, bu_peer, wd_own, wd_peer, vecs, tile=256):
    rows, depth = x.shape
    half = c_own.shape[1]
    wide = wu_own.shape[1]
    chunk = depth

    def tiled(cols):
        return pl.BlockSpec((tile, cols), lambda i: (i, 0))

    def fixed(shape):
        return pl.BlockSpec(shape, lambda i: (0, 0), pipeline_mode=pl.Buffered(1))

    def sds(cols, dtype):
        return jax.ShapeDtypeStruct((rows, cols), dtype)

    fixed_in = (wo_own, wo_peer, wu_own, wu_peer, bu_own, bu_peer, wd_own, wd_peer, vecs)
    return pl.pallas_call(
        functools.partial(ffn_kernel, chunk),
        grid=(rows // tile,),
        out_shape=(
            sds(depth, F32), sds(wide, BF), sds(wide, BF), sds(wide, BF), sds(wide, BF),
            sds(depth, BF), sds(depth, BF), sds(depth, BF), sds(2 * half, BF), sds(depth, F32),
            jax.ShapeDtypeStruct((16, depth), F32),
        ),
        in_specs=[tiled(half), tiled(half), tiled(depth), tiled(depth)] + [fixed(a.shape) for a in fixed_in],
        out_specs=[
            tiled(depth), tiled(wide), tiled(wide), tiled(wide), tiled(wide),
            tiled(depth), tiled(depth), tiled(depth), tiled(2 * half), tiled(depth),
            pl.BlockSpec((16, depth), lambda i: (0, 0)),
        ],
        scratch_shapes=[pltpu.VMEM((tile, 2 * wide), F32)],
        compiler_params=pltpu.CompilerParams(vmem_limit_bytes=60 << 20),
        cost_estimate=pl.CostEstimate(flops=rows * depth * (8 * 2 * wide + 8 * depth), bytes_accessed=48 << 20, transcendentals=rows * wide * 2),
        name="feed",
    )(c_own, c_peer, x, cot, *fixed_in)


LAGS = (1, 4, 7, 9, 12, 15, 17, 19, 22)
GROUPS = 12
BLOCKS = 1
JOBS = 3 * GROUPS


def back_kernel(
    levels,
    lens_ref, h_own, h_peer, gu_own, gu_peer, glow_in, mid_in, flow_in, c_own, c_peer, q_own, q_peer, k_own, k_peer, v_own, v_peer, gctx_in, x_in, w_own, w_peer, small_in,
    job_out, dx_out, small_out,
    buf, ring, prec, rbuf, blocks, glow, mid, flow, ctx, qv, kv, vv, dov, xv, wv, dq, dk, dv, dxs, small, small_sum, small_send, small_recv,
    load_sem, blk_sem, core_send, core_recv, hop_send, hop_recv, out_sem, dx_sem, small_sem, sum_send, sum_recv,
):
    dp = lax.axis_index("dp")
    core = lax.axis_index("tensor")
    half = ctx.shape[1] // 2
    rows, depth = glow.shape
    seqs = lens_ref.shape[0]
    seq_len = rows // seqs
    pairs = qv.shape[1] // 128
    scale = HD ** (-0.5)
    other = (dp, 1 - core)

    def partner(level, job):
        flip = job % 2
        mask = (1 + flip, 4, 2 - flip, 8)[level]
        bit = (dp // mask) % 2
        return bit, (dp + mask * (1 - 2 * bit), core)

    def loads():
        return (
            (glow_in, glow, 0), (mid_in, mid, 1), (c_own, ctx.at[:, :half], 2), (c_peer, ctx.at[:, half:], 3), (flow_in, flow, 4),
            (q_own, qv.at[:, :half], 5), (q_peer, qv.at[:, half:], 6), (k_own, kv.at[:, :half], 7), (k_peer, kv.at[:, half:], 8),
            (v_own, vv.at[:, :half], 9), (v_peer, vv.at[:, half:], 10), (gctx_in, dov, 11), (x_in, xv, 12), (w_own, wv.at[0], 13), (w_peer, wv.at[1], 14), (small_in, small, 15),
        )

    def load(index):
        src, dst, sem = loads()[index]
        return pltpu.make_async_copy(src, dst, load_sem.at[sem])

    def block_copies(src_own, src_peer, index, slot):
        cols = pl.ds(pl.multiple_of(index * JC, 128), JC)
        return (
            pltpu.make_async_copy(src_own.at[:, cols], blocks.at[slot, 0], blk_sem.at[slot, 0]),
            pltpu.make_async_copy(src_peer.at[:, cols], blocks.at[slot, 1], blk_sem.at[slot, 1]),
        )

    def start_blocks(index):
        @pl.when(index < 4)
        def _():
            for copy in block_copies(h_own, h_peer, index, index % 2):
                copy.start()

        @pl.when((index >= 4) & (index < 8))
        def _():
            for copy in block_copies(gu_own, gu_peer, index - 4, index % 2):
                copy.start()

    def core_copy(job):
        return pltpu.make_async_remote_copy(
            src_ref=ring.at[job % 9], dst_ref=prec.at[job], send_sem=core_send.at[job], recv_sem=core_recv.at[job],
            device_id=other, device_id_type=pl.DeviceIdType.MESH,
        )

    def offsets(job):
        spots = [0]
        for level in range(levels):
            bit, _ = partner(level, job)
            spots.append(spots[-1] + bit * (JR >> (level + 1)))
        return spots

    def hop(job, stage):
        if stage < levels:
            level = stage
            size = JR >> (level + 1)
            bit, device = partner(level, job)
            at = pl.multiple_of(offsets(job)[level] + (1 - bit) * size, 16)
            src = buf.at[job, pl.ds(at, size)]
            begin = JR - (JR >> level)
            dst = rbuf.at[job, begin:begin + size]
        else:
            level = 2 * levels - 1 - stage
            size = JR >> (level + 1)
            bit, device = partner(level, job)
            at = pl.multiple_of(offsets(job)[level + 1], 16)
            src = prec.at[job, pl.ds(at, size)]
            dst = prec.at[job, pl.ds(at, size)]
        return pltpu.make_async_remote_copy(
            src_ref=src, dst_ref=dst, send_sem=hop_send.at[stage, job], recv_sem=hop_recv.at[stage, job],
            device_id=device, device_id_type=pl.DeviceIdType.MESH,
        )

    def stage_op(stage, job):
        if stage == 0:
            core_copy(job).wait_recv()
            buf[job] = buf[job] + prec[job]
            hop(job, 0).start()
            return
        before = hop(job, stage - 1)
        before.wait_recv()
        before.wait_send()
        if stage <= levels:
            level = stage - 1
            size = JR >> stage
            at = pl.multiple_of(offsets(job)[stage], 16)
            begin = JR - (JR >> level)
            keep = buf[job, pl.ds(at, size)] + rbuf[job, begin:begin + size]
            target = prec if stage == levels else buf
            target[job, pl.ds(at, size)] = keep
        if stage < 2 * levels:
            hop(job, stage).start()
        else:
            pltpu.make_async_copy(prec.at[job], job_out.at[job], out_sem.at[job]).start()

    def emit(group, own, peer):
        for which, pieces in ((0, own), (1, peer)):
            for i, (top, bottom) in enumerate(pieces):
                job = group * 3 + i
                if which == 0:
                    target = buf.at[job]
                else:
                    target = ring.at[job % 9]
                cut = top.shape[0]
                target[:cut, :] = top.astype(BF)
                if bottom is not None:
                    target[cut:, :] = bottom.astype(BF)
                if which == 1:
                    core_copy(job).start()

    def free_ring(group):
        @pl.when(group >= 3)
        def _():
            for i in range(3):
                core_copy((group - 3) * 3 + i).wait_send()

    def slabs(block):
        return [(block[i * 128:(i + 1) * 128, :JC], block[i * 128:(i + 1) * 128, JC:]) for i in range(3)]

    def tall(block):
        return [(block[i * JR:(i + 1) * JR], None) for i in range(3)]

    def down_phase(index):
        @pl.when(index == 0)
        def _():
            load(0).wait()

        for copy in block_copies(h_own, h_peer, index, index % 2):
            copy.wait()
        free_ring(index)
        right = glow[...]
        slot = index % 2
        emit(index, slabs(dot_tn(blocks[slot, 0], right)), slabs(dot_tn(blocks[slot, 1], right)))
        start_blocks(index + 2)

    def up_phase(index):
        @pl.when(index == 0)
        def _():
            load(1).wait()

        slot = index % 2
        for copy in block_copies(gu_own, gu_peer, index, slot):
            copy.wait()
        free_ring(index + 4)
        left = mid[...]
        emit(index + 4, tall(dot_tn(left, blocks[slot, 0])), tall(dot_tn(left, blocks[slot, 1])))
        start_blocks(index + 6)

    def out_phase():
        for i in (2, 3, 4):
            load(i).wait()
        free_ring(8)
        right = flow[...]
        emit(8, slabs(dot_tn(ctx[:, :half], right)), slabs(dot_tn(ctx[:, half:], right)))

    def add_bias(pair, offset, value):
        total = jnp.sum(value.astype(F32), axis=0, keepdims=True)
        for side in range(2):
            @pl.when(pair // (pairs // 2) == side)
            def _():
                lanes = pl.ds(pl.multiple_of(offset + (pair - side * (pairs // 2)) * 128, 128), 128)
                small[12 + side:13 + side, lanes] += total

    def sum_hop(stage):
        if stage == 0:
            src, device = small_send, other
        else:
            src, device = small_sum.at[stage - 1], partner(stage - 1, 0)[1]
        return pltpu.make_async_remote_copy(
            src_ref=src, dst_ref=small_recv.at[stage], send_sem=sum_send.at[stage], recv_sem=sum_recv.at[stage],
            device_id=device, device_id_type=pl.DeviceIdType.MESH,
        )

    def sum_phase(stage):
        if stage == 0:
            small_send[0:8, :] = small[0:8, :]
            small_send[8:10, :] = small[10:12, :]
            small_send[10:11, :] = small[13:14, :]
            small_send[11:16, :] = jnp.zeros((5, depth), F32)
        else:
            sum_hop(stage - 1).wait_recv()
            sum_hop(stage - 1).wait_send()
            if stage == 1:
                got = small_recv[0]
                small_sum[0, 0:8, :] = small[0:8, :] + got[0:8, :]
                small_sum[0, 8:10, :] = small[8:10, :] + got[8:10, :]
                small_sum[0, 10:11, :] = small[12:13, :] + got[10:11, :]
                small_sum[0, 11:16, :] = jnp.zeros((5, depth), F32)
            else:
                small_sum[stage - 1] = small_sum[stage - 2] + small_recv[stage - 1]
        if stage <= levels:
            sum_hop(stage).start()
        else:
            pltpu.make_async_copy(small_sum.at[levels], small_out, small_sem).start()

    def attend_phase(unit):
        @pl.when(unit == 0)
        def _():
            for i in range(5, 12):
                load(i).wait()
            load(15).wait()
            small[12:14, :] = jnp.zeros((2, depth), F32)

        seq = unit // pairs
        pair = unit % pairs
        length = lens_ref[seq]
        span = pl.ds(pl.multiple_of(seq * seq_len, seq_len), seq_len)
        lanes = pl.ds(pl.multiple_of(pair * 128, 128), 128)
        k = kv[span, lanes]
        v = vv[span, lanes]
        k_t = k.T
        low = half_masks((1, 128), 1)
        qb = seq_len // BLOCKS
        grad_k = jnp.zeros((seq_len, 128), F32)
        grad_v = jnp.zeros((seq_len, 128), F32)
        for block in range(BLOCKS):
            part = pl.ds(pl.multiple_of(seq * seq_len + block * qb, qb), qb)
            q = qv[part, lanes]
            do = dov[part, lanes]
            grad_q = []
            for head in range(2):
                pick = low if head == 0 else jnp.logical_not(low)
                q_head = jnp.where(pick, q, jnp.zeros_like(q))
                do_head = jnp.where(pick, do, jnp.zeros_like(do))
                s = dot_nt(k, q_head)
                is_valid = lax.broadcasted_iota(jnp.int32, s.shape, 0) < length
                s = jnp.where(is_valid, s, NEG)
                e = jnp.exp(s - jnp.max(s, axis=0, keepdims=True))
                weights = e * (1.0 / jnp.sum(e, axis=0, keepdims=True))
                grad_probs = dot_nt(v, do_head)
                grad_v = grad_v + dot(weights.astype(BF), do_head)
                row_terms = jnp.sum(weights * grad_probs, axis=0, keepdims=True)
                grad_s = (weights * (grad_probs - row_terms)).astype(BF)
                grad_k = grad_k + dot(grad_s, q_head)
                grad_q.append(dot(k_t[head * HD:(head + 1) * HD], grad_s) * scale)
            grad_q = jnp.concatenate(grad_q, axis=0).T.astype(BF)
            dq[part, lanes] = grad_q
            add_bias(pair, 0, grad_q)
        grad_v = grad_v.astype(BF)
        dk[span, lanes] = grad_k.astype(BF)
        dv[span, lanes] = grad_v
        add_bias(pair, half, grad_v)

    def proj_phase(index):
        if index == 0:
            load(12).wait()
        free_ring(jnp.int32(index + 9))
        left = xv[...]
        grad = (dq, dk, dv)[index]
        emit(index + 9, tall(dot_tn(left, grad[:, :half])), tall(dot_tn(left, grad[:, half:])))

    def dx_copy(index):
        span = pl.ds(pl.multiple_of(index * JR, JR), JR)
        return pltpu.make_async_copy(dxs.at[index % 2], dx_out.at[span], dx_sem.at[index % 2])

    def dx_phase(index):
        @pl.when(index == 0)
        def _():
            load(13).wait()
            load(14).wait()

        @pl.when(index >= 2)
        def _():
            dx_copy(index - 2).wait()

        span = pl.ds(pl.multiple_of(index * JR, JR), JR)
        total = jnp.zeros((JR, depth), F32)
        for side in range(2):
            cols = slice(side * half, side * half + half)
            part = jnp.zeros((JR, depth), F32)
            for i, grad in enumerate((dq, dk, dv)):
                part = part + dot_nt(grad[span, cols], wv[side, i])
            total = total + part
        dxs[index % 2] = total.astype(BF)
        dx_copy(index).start()

    barrier = pltpu.get_barrier_semaphore()
    pl.semaphore_signal(barrier, inc=1, device_id=other, device_id_type=pl.DeviceIdType.MESH)
    for level in range(levels):
        pl.semaphore_signal(barrier, inc=1, device_id=partner(level, 0)[1], device_id_type=pl.DeviceIdType.MESH)
    load(0).start()
    start_blocks(0)
    start_blocks(1)
    for i in range(1, 16):
        load(i).start()
    pl.semaphore_wait(barrier, levels + 1)

    units = seqs * pairs
    first = 9 + units
    ticks = max(JOBS + LAGS[2 * levels], first + 3 + rows // JR)

    def tick(t, carry):
        for stage in range(2 * levels, -1, -1):
            job = t - LAGS[stage]

            @pl.when((job >= 0) & (job < JOBS))
            def _():
                stage_op(stage, job)

        @pl.when(t < 4)
        def _():
            down_phase(t)

        @pl.when((t >= 4) & (t < 8))
        def _():
            up_phase(t - 4)

        @pl.when(t == 8)
        def _():
            out_phase()

        @pl.when((t >= 9) & (t < first))
        def _():
            attend_phase(t - 9)

        for i in range(3):
            @pl.when(t == first + i)
            def _():
                proj_phase(i)

        @pl.when((t >= first + 3) & (t < first + 3 + rows // JR))
        def _():
            dx_phase(t - first - 3)

        for stage in range(levels + 2):
            @pl.when(t == first + 1 + 2 * stage)
            def _():
                sum_phase(stage)

        return carry

    lax.fori_loop(0, ticks, tick, 0)
    for group in (GROUPS - 3, GROUPS - 2, GROUPS - 1):
        for i in range(3):
            core_copy(group * 3 + i).wait_send()
    dx_copy(rows // JR - 2).wait()
    dx_copy(rows // JR - 1).wait()

    def finish(job, carry):
        pltpu.make_async_copy(prec.at[job], job_out.at[job], out_sem.at[job]).wait()
        return carry

    lax.fori_loop(0, JOBS, finish, 0)
    pltpu.make_async_copy(small_sum.at[levels], small_out, small_sem).wait()


def backward(levels, lens, arrays):
    h_own, glow, c_own, x = arrays[0], arrays[4], arrays[7], arrays[16]
    rows, depth = glow.shape
    half = c_own.shape[1]
    hbm = pl.BlockSpec(memory_space=pl.ANY)
    square = pltpu.VMEM((rows, depth), BF)
    dma = pltpu.SemaphoreType.DMA
    return pl.pallas_call(
        functools.partial(back_kernel, levels),
        out_shape=(
            jax.ShapeDtypeStruct((JOBS, JR, JC), BF),
            jax.ShapeDtypeStruct((rows, depth), BF),
            jax.ShapeDtypeStruct((16, depth), F32),
        ),
        in_specs=[pl.BlockSpec(memory_space=pltpu.SMEM)] + [hbm] * len(arrays),
        out_specs=(hbm, hbm, hbm),
        scratch_shapes=[
            pltpu.VMEM((JOBS, JR, JC), BF), pltpu.VMEM((9, JR, JC), BF), pltpu.VMEM((JOBS, JR, JC), BF),
            pltpu.VMEM((JOBS, JR - (JR >> levels), JC), BF), pltpu.VMEM((2, 2, rows, JC), BF),
            square, square, square, square, square, square, square, square, square,
            pltpu.VMEM((2, 3, depth, half), BF), square, square, square,
            pltpu.VMEM((2, JR, depth), BF), pltpu.VMEM((16, depth), F32),
            pltpu.VMEM((levels + 1, 16, depth), F32), pltpu.VMEM((16, depth), F32), pltpu.VMEM((levels + 1, 16, depth), F32),
            dma((16,)), dma((2, 2)), dma((JOBS,)), dma((JOBS,)), dma((2 * levels, JOBS)), dma((2 * levels, JOBS)), dma((JOBS,)), dma((2,)), dma(()), dma((levels + 1,)), dma((levels + 1,)),
        ],
        compiler_params=pltpu.CompilerParams(vmem_limit_bytes=67043328, collective_id=1, has_side_effects=True),
        cost_estimate=pl.CostEstimate(flops=60 << 30, bytes_accessed=64 << 20, transcendentals=8 << 20),
        name="backward",
    )(lens, *arrays)


def unpack_kernel(jobs_ref, gf_ref, dx_ref, small_ref, tok_ref, qkv_ref, qvb_ref, out_ref, up_ref, upb_ref, down_ref, *vec_refs):
    step = pl.program_id(0)
    depth = small_ref.shape[1]

    def unslab(target):
        for i in range(3):
            rows = slice(i * 128, i * 128 + 128)
            target[rows, :JC] = jobs_ref[i, :128, :].astype(F32)
            target[rows, JC:] = jobs_ref[i, 128:, :].astype(F32)

    def tall(store):
        for i in range(3):
            store(i, jobs_ref[i].astype(F32))

    @pl.when(step < 4)
    def _():
        unslab(down_ref)
        tok_ref[...] = gf_ref[...] + dx_ref[...].astype(F32)

    @pl.when((step >= 4) & (step < 8))
    def _():
        for i in range(3):
            up_ref[i * JR:(i + 1) * JR, :] = jobs_ref[i].astype(F32)

    @pl.when(step == 8)
    def _():
        unslab(out_ref)
        for i, ref in enumerate(vec_refs):
            ref[...] = small_ref[i]
        upb_ref[:depth] = small_ref[8]
        upb_ref[depth:] = small_ref[9]
        qvb_ref[0:1, :] = small_ref[10:11, :JC]
        qvb_ref[1:2, :] = small_ref[10:11, JC:]

    @pl.when(step >= 9)
    def _():
        for i in range(3):
            qkv_ref[0, i * JR:(i + 1) * JR, :] = jobs_ref[i].astype(F32)


def unpack(jobs, grad_first, dx, small, wide):
    rows, depth = grad_first.shape

    def rows_at(i):
        return (jnp.minimum(i, 3), 0)

    quarter = pl.BlockSpec((rows // 4, depth), rows_at)

    def whole(shape):
        return pl.BlockSpec(shape, lambda i: (0, 0))

    def flat(size):
        return pl.BlockSpec((size,), lambda i: (0,))

    vec = jax.ShapeDtypeStruct((depth,), F32)
    return pl.pallas_call(
        unpack_kernel,
        grid=(GROUPS,),
        out_shape=(
            jax.ShapeDtypeStruct((rows, depth), F32), jax.ShapeDtypeStruct((3, depth, JC), F32), jax.ShapeDtypeStruct((2, JC), F32),
            jax.ShapeDtypeStruct((JC, depth), F32), jax.ShapeDtypeStruct((depth, wide), F32), jax.ShapeDtypeStruct((wide,), F32),
            jax.ShapeDtypeStruct((wide, depth), F32), vec, vec, vec, vec, vec, vec,
        ),
        in_specs=[pl.BlockSpec((3, JR, JC), lambda i: (i, 0, 0)), quarter, quarter, whole((16, depth))],
        out_specs=[
            quarter, pl.BlockSpec((1, depth, JC), lambda i: (jnp.clip(i - 9, 0, 2), 0, 0)), whole((2, JC)), whole((JC, depth)),
            pl.BlockSpec((depth, JC), lambda i: (0, jnp.clip(i - 4, 0, 3))), flat(wide), pl.BlockSpec((JC, depth), rows_at),
        ] + [flat(depth)] * 6,
        compiler_params=pltpu.CompilerParams(vmem_limit_bytes=62 << 20),
        name="unpack",
    )(jobs, grad_first, dx, small)


def body(tokens, lengths, qkv_weight, qv_bias, out_weight, out_bias, first_gain, first_shift, up_weight, up_bias, down_weight, down_bias, second_gain, second_shift, cotangent):
    n_tensor = lax.axis_size("tensor")
    n_dp = lax.axis_size("dp")
    core = lax.axis_index("tensor")
    seqs = lengths.shape[0] // n_tensor
    lens = lax.dynamic_slice(lengths, (core * seqs,), (seqs,))
    levels = 4

    def swap(value):
        return lax.ppermute(value, "tensor", [(0, 1), (1, 0)])

    up_row = up_bias.reshape(1, -1)
    peer_qkv, peer_qv_bias = swap(qkv_weight), swap(qv_bias)
    peer_out, peer_up, peer_up_row, peer_down = swap(out_weight), swap(up_weight), swap(up_row), swap(down_weight)
    q_own, k_own, v_own, c_own = attention(lens, tokens, qkv_weight, qv_bias)
    q_peer, k_peer, v_peer, c_peer = attention(lens, tokens, peer_qkv, peer_qv_bias)
    vecs = jnp.stack([out_bias, first_gain, first_shift, down_bias, second_gain, second_shift, out_bias, out_bias])
    layer_out, h_own, h_peer, gu_own, gu_peer, mid, glow, flow, gctx, grad_first, sums = ffn(
        c_own, c_peer, tokens, cotangent, out_weight, peer_out, up_weight, peer_up, up_row, peer_up_row, down_weight, peer_down, vecs
    )
    jobs, dx, sums = backward(
        levels, lens,
        (h_own, h_peer, gu_own, gu_peer, glow, mid, flow, c_own, c_peer, q_own, q_peer, k_own, k_peer, v_own, v_peer, gctx, tokens, qkv_weight, peer_qkv, sums),
    )
    inner = 1 << levels
    if n_dp > inner:
        groups = [[i + inner * g for g in range(n_dp // inner)] for i in range(inner)]
        jobs, sums = lax.psum((jobs, sums), "dp", axis_index_groups=groups)
    grad_tokens, grad_qkv, grad_qv_bias, grad_out, grad_up, grad_up_bias, grad_down, *vectors = unpack(jobs, grad_first, dx, sums, up_bias.shape[0])
    return (
        layer_out, grad_tokens, grad_qkv, grad_qv_bias, grad_out, vectors[0], vectors[1], vectors[2],
        grad_up, grad_up_bias, grad_down, vectors[3], vectors[4], vectors[5],
    )


def solution(mesh):
    tokens = P(("dp", "tensor"), None)
    columns = P(None, "tensor")
    cube = P(None, None, "tensor")
    split = P("tensor", None)
    return jax.shard_map(
        body,
        mesh=mesh,
        in_specs=(tokens, P("dp"), cube, columns, split, P(), P(), P(), columns, P("tensor"), split, P(), P(), P(), tokens),
        out_specs=(tokens, tokens, cube, columns, split, P(), P(), P(), columns, P("tensor"), split, P(), P(), P()),
        check_vma=False,
    )
```

```python
import functools

import jax
import jax.numpy as jnp
from jax import lax
from jax.experimental import pallas as pl
from jax.experimental.pallas import tpu as pltpu
from jax.sharding import PartitionSpec as P

HD = 64
EPS = 1e-06
BF = jnp.bfloat16
F32 = jnp.float32
NEG = -1000000000.0
JR, JC = 256, 384


def dot(a, b):
    return lax.dot_general(a, b, (((1,), (0,)), ((), ())), preferred_element_type=F32)


def dot_nt(a, b):
    return lax.dot_general(a, b, (((1,), (1,)), ((), ())), preferred_element_type=F32)


def dot_tn(a, b):
    return lax.dot_general(a, b, (((0,), (0,)), ((), ())), preferred_element_type=F32)


def half_masks(shape, dim):
    low = lax.broadcasted_iota(jnp.int32, shape, dim) % (2 * HD) < HD
    return low


def attn_kernel(qb, lens_ref, x_ref, w_ref, b_ref, q_ref, k_ref, v_ref, c_ref):
    length = lens_ref[pl.program_id(0)]
    x = x_ref[...]
    rows, width = q_ref.shape
    scale = HD ** (-0.5)
    q_ref[...] = (dot(x, w_ref[0]) + b_ref[0:1, :]).astype(BF) * jnp.asarray(scale, BF)
    k_ref[...] = dot(x, w_ref[1]).astype(BF)
    v_ref[...] = (dot(x, w_ref[2]) + b_ref[1:2, :]).astype(BF)
    for pair in range(width // 128):
        lanes = slice(pair * 128, pair * 128 + 128)
        k = k_ref[:, lanes]
        v_t = v_ref[:, lanes].T
        for block in range(rows // qb):
            span = slice(block * qb, block * qb + qb)
            q = q_ref[span, lanes]
            low = half_masks(q.shape, 1)
            zero = jnp.zeros_like(q)
            parts = []
            for head in range(2):
                q_head = jnp.where(low, q, zero) if head == 0 else jnp.where(low, zero, q)
                s = dot_nt(k, q_head)
                is_valid = lax.broadcasted_iota(jnp.int32, s.shape, 0) < length
                s = jnp.where(is_valid, s, NEG)
                top = jnp.max(s, axis=0, keepdims=True)
                e = jnp.exp(s - top)
                total = jnp.sum(e, axis=0, keepdims=True)
                c_t = dot(v_t[head * HD:(head + 1) * HD], e.astype(BF))
                parts.append(c_t * (1.0 / total))
            c_ref[span, lanes] = jnp.concatenate(parts, axis=0).T.astype(BF)


def attention(lens, x, weight, bias, qb=512):
    rows, depth = x.shape
    seqs = lens.shape[0]
    seq_len = rows // seqs
    width = weight.shape[2]
    row_spec = pl.BlockSpec((seq_len, width), lambda s, _: (s, 0))
    out = jax.ShapeDtypeStruct((rows, width), BF)
    flops = 2 * rows * depth * width * 3 + 4 * rows * seq_len * width
    return pl.pallas_call(
        functools.partial(attn_kernel, qb),
        out_shape=(out, out, out, out),
        grid_spec=pltpu.PrefetchScalarGridSpec(
            num_scalar_prefetch=1,
            grid=(seqs,),
            in_specs=[
                pl.BlockSpec((seq_len, depth), lambda s, _: (s, 0)),
                pl.BlockSpec(weight.shape, lambda s, _: (0, 0, 0)),
                pl.BlockSpec(bias.shape, lambda s, _: (0, 0)),
            ],
            out_specs=[row_spec] * 4,
        ),
        compiler_params=pltpu.CompilerParams(vmem_limit_bytes=56 << 20),
        cost_estimate=pl.CostEstimate(flops=flops * 3, bytes_accessed=12 << 20, transcendentals=rows * seq_len * width // HD),
        name="attend",
    )(lens, x, weight, bias)


def norm_stats(rows_in):
    centre = rows_in - jnp.mean(rows_in, axis=-1, keepdims=True)
    spread = jnp.mean(centre * centre, axis=-1, keepdims=True)
    root = lax.rsqrt(spread + EPS)
    return centre * root, root


def norm_back(grad, normed, root):
    first = jnp.mean(grad, axis=-1, keepdims=True)
    second = jnp.mean(grad * normed, axis=-1, keepdims=True)
    return root * (grad - first - normed * second)


def gelu_both(u):
    z = jnp.abs(u) * (0.5 ** 0.5)
    t = 1.0 / (1.0 + 0.3275911 * z)
    poly = 1.061405429 * t - 1.453152027
    poly = poly * t + 1.421413741
    poly = poly * t - 0.284496736
    poly = poly * t + 0.254829592
    bell = jnp.exp(-0.5 * (u * u))
    tail = 0.5 * (poly * t) * bell
    phi_cdf = jnp.where(u < 0.0, tail, 1.0 - tail)
    return u * phi_cdf, phi_cdf + u * (bell * 0.3989422804014327)


def ffn_kernel(
    chunk,
    c_own, c_peer, x_ref, cot_ref, wo_own, wo_peer, wu_own, wu_peer, bu_own, bu_peer, wd_own, wd_peer, vec_ref,
    out_ref, h_own, h_peer, gu_own, gu_peer, mid_ref, glow_ref, flow_ref, gctx_ref, gf_ref, small_ref,
    gp_ref,
):
    step = pl.program_id(0)
    wide = wu_own.shape[1]
    out_bias, gain1, shift1, down_bias, gain2, shift2 = (vec_ref[i:i + 1, :] for i in range(6))

    @pl.when(step == 0)
    def _():
        small_ref[...] = jnp.zeros_like(small_ref)

    def colsum(index, value):
        small_ref[index:index + 1, :] += jnp.sum(value, axis=0, keepdims=True)

    attn_sum = dot(c_own[...], wo_own[...]) + dot(c_peer[...], wo_peer[...])
    n1, root1 = norm_stats(x_ref[...].astype(F32) + attn_sum + out_bias)
    first_out = n1 * gain1 + shift1
    middle = first_out.astype(BF)
    mid_ref[...] = middle
    ffn_sum = jnp.zeros_like(first_out)
    groups = ((wu_own, bu_own, wd_own, h_own, gu_own, 0), (wu_peer, bu_peer, wd_peer, h_peer, gu_peer, wide))
    for wu, bu, wd, h_ref, _, base in groups:
        for at in range(0, wide, chunk):
            cols = slice(at, at + chunk)
            u = dot(middle, wu[:, cols]) + bu[:, cols]
            act, slope = gelu_both(u)
            act = act.astype(BF)
            h_ref[:, cols] = act
            gp_ref[:, base + at:base + at + chunk] = slope
            ffn_sum = ffn_sum + dot(act, wd[cols, :])
    n2, root2 = norm_stats(first_out + ffn_sum + down_bias)
    out_ref[...] = n2 * gain2 + shift2
    cot = cot_ref[...].astype(F32)
    colsum(4, cot * n2)
    colsum(5, cot)
    grad_second = norm_back(cot * gain2, n2, root2)
    colsum(3, grad_second)
    glow = grad_second.astype(BF)
    glow_ref[...] = glow
    grad_first_out = grad_second
    for wu, _, wd, _, gu_ref, base in groups:
        for at in range(0, wide, chunk):
            cols = slice(at, at + chunk)
            grad_hidden = dot_nt(glow, wd[cols, :])
            gu = (grad_hidden * gp_ref[:, base + at:base + at + chunk]).astype(BF)
            gu_ref[:, cols] = gu
            colsum(8 + (base + at) // chunk, gu.astype(F32))
            grad_first_out = grad_first_out + dot_nt(gu, wu[:, cols])
    colsum(1, grad_first_out * n1)
    colsum(2, grad_first_out)
    grad_first = norm_back(grad_first_out * gain1, n1, root1)
    colsum(0, grad_first)
    gf_ref[...] = grad_first
    flow = grad_first.astype(BF)
    flow_ref[...] = flow
    half = wo_own.shape[0]
    gctx_ref[:, :half] = dot_nt(flow, wo_own[...]).astype(BF)
    gctx_ref[:, half:] = dot_nt(flow, wo_peer[...]).astype(BF)


def ffn(c_own, c_peer, x, cot, wo_own, wo_peer, wu_own, wu_peer, bu_own, bu_peer, wd_own, wd_peer, vecs, tile=256):
    rows, depth = x.shape
    half = c_own.shape[1]
    wide = wu_own.shape[1]
    chunk = depth

    def tiled(cols):
        return pl.BlockSpec((tile, cols), lambda i: (i, 0))

    def fixed(shape):
        return pl.BlockSpec(shape, lambda i: (0, 0), pipeline_mode=pl.Buffered(1))

    def sds(cols, dtype):
        return jax.ShapeDtypeStruct((rows, cols), dtype)

    fixed_in = (wo_own, wo_peer, wu_own, wu_peer, bu_own, bu_peer, wd_own, wd_peer, vecs)
    return pl.pallas_call(
        functools.partial(ffn_kernel, chunk),
        grid=(rows // tile,),
        out_shape=(
            sds(depth, F32), sds(wide, BF), sds(wide, BF), sds(wide, BF), sds(wide, BF),
            sds(depth, BF), sds(depth, BF), sds(depth, BF), sds(2 * half, BF), sds(depth, F32),
            jax.ShapeDtypeStruct((16, depth), F32),
        ),
        in_specs=[tiled(half), tiled(half), tiled(depth), tiled(depth)] + [fixed(a.shape) for a in fixed_in],
        out_specs=[
            tiled(depth), tiled(wide), tiled(wide), tiled(wide), tiled(wide),
            tiled(depth), tiled(depth), tiled(depth), tiled(2 * half), tiled(depth),
            pl.BlockSpec((16, depth), lambda i: (0, 0)),
        ],
        scratch_shapes=[pltpu.VMEM((tile, 2 * wide), F32)],
        compiler_params=pltpu.CompilerParams(vmem_limit_bytes=60 << 20),
        cost_estimate=pl.CostEstimate(flops=rows * depth * (8 * 2 * wide + 8 * depth), bytes_accessed=48 << 20, transcendentals=rows * wide * 2),
        name="feed",
    )(c_own, c_peer, x, cot, *fixed_in)


LAGS = (1, 4, 7, 9, 12, 15, 17, 19, 22)
GROUPS = 12
BLOCKS = 1
JOBS = 3 * GROUPS


def back_kernel(
    levels,
    lens_ref, h_own, h_peer, gu_own, gu_peer, glow_in, mid_in, flow_in, c_own, c_peer, q_own, q_peer, k_own, k_peer, v_own, v_peer, gctx_in, x_in, w_own, w_peer, small_in,
    job_out, dx_out, small_out,
    buf, ring, prec, rbuf, blocks, glow, mid, flow, ctx, qv, kv, vv, dov, xv, wv, dq, dk, dv, dxs, small, small_sum, small_send, small_recv,
    load_sem, blk_sem, core_send, core_recv, hop_send, hop_recv, out_sem, dx_sem, small_sem, sum_send, sum_recv,
):
    dp = lax.axis_index("dp")
    core = lax.axis_index("tensor")
    half = ctx.shape[1] // 2
    rows, depth = glow.shape
    seqs = lens_ref.shape[0]
    seq_len = rows // seqs
    pairs = qv.shape[1] // 128
    scale = HD ** (-0.5)
    other = (dp, 1 - core)

    def partner(level, job):
        flip = job % 2
        mask = (1 + flip, 4, 2 - flip, 8)[level]
        bit = (dp // mask) % 2
        return bit, (dp + mask * (1 - 2 * bit), core)

    def loads():
        return (
            (glow_in, glow, 0), (mid_in, mid, 1), (c_own, ctx.at[:, :half], 2), (c_peer, ctx.at[:, half:], 3), (flow_in, flow, 4),
            (q_own, qv.at[:, :half], 5), (q_peer, qv.at[:, half:], 6), (k_own, kv.at[:, :half], 7), (k_peer, kv.at[:, half:], 8),
            (v_own, vv.at[:, :half], 9), (v_peer, vv.at[:, half:], 10), (gctx_in, dov, 11), (x_in, xv, 12), (w_own, wv.at[0], 13), (w_peer, wv.at[1], 14), (small_in, small, 15),
        )

    def load(index):
        src, dst, sem = loads()[index]
        return pltpu.make_async_copy(src, dst, load_sem.at[sem])

    def block_copies(src_own, src_peer, index, slot):
        cols = pl.ds(pl.multiple_of(index * JC, 128), JC)
        return (
            pltpu.make_async_copy(src_own.at[:, cols], blocks.at[slot, 0], blk_sem.at[slot, 0]),
            pltpu.make_async_copy(src_peer.at[:, cols], blocks.at[slot, 1], blk_sem.at[slot, 1]),
        )

    def start_blocks(index):
        @pl.when(index < 4)
        def _():
            for copy in block_copies(h_own, h_peer, index, index % 2):
                copy.start()

        @pl.when((index >= 4) & (index < 8))
        def _():
            for copy in block_copies(gu_own, gu_peer, index - 4, index % 2):
                copy.start()

    def core_copy(job):
        return pltpu.make_async_remote_copy(
            src_ref=ring.at[job % 9], dst_ref=prec.at[job], send_sem=core_send.at[job], recv_sem=core_recv.at[job],
            device_id=other, device_id_type=pl.DeviceIdType.MESH,
        )

    def offsets(job):
        spots = [0]
        for level in range(levels):
            bit, _ = partner(level, job)
            spots.append(spots[-1] + bit * (JR >> (level + 1)))
        return spots

    def hop(job, stage):
        if stage < levels:
            level = stage
            size = JR >> (level + 1)
            bit, device = partner(level, job)
            at = pl.multiple_of(offsets(job)[level] + (1 - bit) * size, 16)
            src = buf.at[job, pl.ds(at, size)]
            begin = JR - (JR >> level)
            dst = rbuf.at[job, begin:begin + size]
        else:
            level = 2 * levels - 1 - stage
            size = JR >> (level + 1)
            bit, device = partner(level, job)
            at = pl.multiple_of(offsets(job)[level + 1], 16)
            src = prec.at[job, pl.ds(at, size)]
            dst = prec.at[job, pl.ds(at, size)]
        return pltpu.make_async_remote_copy(
            src_ref=src, dst_ref=dst, send_sem=hop_send.at[stage, job], recv_sem=hop_recv.at[stage, job],
            device_id=device, device_id_type=pl.DeviceIdType.MESH,
        )

    def stage_op(stage, job):
        if stage == 0:
            core_copy(job).wait_recv()
            buf[job] = buf[job] + prec[job]
            hop(job, 0).start()
            return
        before = hop(job, stage - 1)
        before.wait_recv()
        before.wait_send()
        if stage <= levels:
            level = stage - 1
            size = JR >> stage
            at = pl.multiple_of(offsets(job)[stage], 16)
            begin = JR - (JR >> level)
            keep = buf[job, pl.ds(at, size)] + rbuf[job, begin:begin + size]
            target = prec if stage == levels else buf
            target[job, pl.ds(at, size)] = keep
        if stage < 2 * levels:
            hop(job, stage).start()
        else:
            pltpu.make_async_copy(prec.at[job], job_out.at[job], out_sem.at[job]).start()

    def emit(group, own, peer):
        for which, pieces in ((0, own), (1, peer)):
            for i, (top, bottom) in enumerate(pieces):
                job = group * 3 + i
                if which == 0:
                    target = buf.at[job]
                else:
                    target = ring.at[job % 9]
                cut = top.shape[0]
                target[:cut, :] = top.astype(BF)
                if bottom is not None:
                    target[cut:, :] = bottom.astype(BF)
                if which == 1:
                    core_copy(job).start()

    def free_ring(group):
        @pl.when(group >= 3)
        def _():
            for i in range(3):
                core_copy((group - 3) * 3 + i).wait_send()

    def slabs(block):
        return [(block[i * 128:(i + 1) * 128, :JC], block[i * 128:(i + 1) * 128, JC:]) for i in range(3)]

    def tall(block):
        return [(block[i * JR:(i + 1) * JR], None) for i in range(3)]

    def down_phase(index):
        @pl.when(index == 0)
        def _():
            load(0).wait()

        for copy in block_copies(h_own, h_peer, index, index % 2):
            copy.wait()
        free_ring(index)
        right = glow[...]
        slot = index % 2
        emit(index, slabs(dot_tn(blocks[slot, 0], right)), slabs(dot_tn(blocks[slot, 1], right)))
        start_blocks(index + 2)

    def up_phase(index):
        @pl.when(index == 0)
        def _():
            load(1).wait()

        slot = index % 2
        for copy in block_copies(gu_own, gu_peer, index, slot):
            copy.wait()
        free_ring(index + 4)
        left = mid[...]
        emit(index + 4, tall(dot_tn(left, blocks[slot, 0])), tall(dot_tn(left, blocks[slot, 1])))
        start_blocks(index + 6)

    def out_phase():
        for i in (2, 3, 4):
            load(i).wait()
        free_ring(8)
        right = flow[...]
        emit(8, slabs(dot_tn(ctx[:, :half], right)), slabs(dot_tn(ctx[:, half:], right)))

    def add_bias(pair, offset, value):
        total = jnp.sum(value.astype(F32), axis=0, keepdims=True)
        for side in range(2):
            @pl.when(pair // (pairs // 2) == side)
            def _():
                lanes = pl.ds(pl.multiple_of(offset + (pair - side * (pairs // 2)) * 128, 128), 128)
                small[12 + side:13 + side, lanes] += total

    def sum_hop(stage):
        if stage == 0:
            src, device = small_send, other
        else:
            src, device = small_sum.at[stage - 1], partner(stage - 1, 0)[1]
        return pltpu.make_async_remote_copy(
            src_ref=src, dst_ref=small_recv.at[stage], send_sem=sum_send.at[stage], recv_sem=sum_recv.at[stage],
            device_id=device, device_id_type=pl.DeviceIdType.MESH,
        )

    def sum_phase(stage):
        if stage == 0:
            small_send[0:8, :] = small[0:8, :]
            small_send[8:10, :] = small[10:12, :]
            small_send[10:11, :] = small[13:14, :]
            small_send[11:16, :] = jnp.zeros((5, depth), F32)
        else:
            sum_hop(stage - 1).wait_recv()
            sum_hop(stage - 1).wait_send()
            if stage == 1:
                got = small_recv[0]
                small_sum[0, 0:8, :] = small[0:8, :] + got[0:8, :]
                small_sum[0, 8:10, :] = small[8:10, :] + got[8:10, :]
                small_sum[0, 10:11, :] = small[12:13, :] + got[10:11, :]
                small_sum[0, 11:16, :] = jnp.zeros((5, depth), F32)
            else:
                small_sum[stage - 1] = small_sum[stage - 2] + small_recv[stage - 1]
        if stage <= levels:
            sum_hop(stage).start()
        else:
            pltpu.make_async_copy(small_sum.at[levels], small_out, small_sem).start()

    def attend_phase(unit):
        @pl.when(unit == 0)
        def _():
            for i in range(5, 12):
                load(i).wait()
            load(15).wait()
            small[12:14, :] = jnp.zeros((2, depth), F32)

        seq = unit // pairs
        pair = unit % pairs
        length = lens_ref[seq]
        span = pl.ds(pl.multiple_of(seq * seq_len, seq_len), seq_len)
        lanes = pl.ds(pl.multiple_of(pair * 128, 128), 128)
        k = kv[span, lanes]
        v = vv[span, lanes]
        k_t = k.T
        low = half_masks((1, 128), 1)
        qb = seq_len // BLOCKS
        grad_k = jnp.zeros((seq_len, 128), F32)
        grad_v = jnp.zeros((seq_len, 128), F32)
        for block in range(BLOCKS):
            part = pl.ds(pl.multiple_of(seq * seq_len + block * qb, qb), qb)
            q = qv[part, lanes]
            do = dov[part, lanes]
            grad_q = []
            for head in range(2):
                pick = low if head == 0 else jnp.logical_not(low)
                q_head = jnp.where(pick, q, jnp.zeros_like(q))
                do_head = jnp.where(pick, do, jnp.zeros_like(do))
                s = dot_nt(k, q_head)
                is_valid = lax.broadcasted_iota(jnp.int32, s.shape, 0) < length
                s = jnp.where(is_valid, s, NEG)
                e = jnp.exp(s - jnp.max(s, axis=0, keepdims=True))
                weights = e * (1.0 / jnp.sum(e, axis=0, keepdims=True))
                grad_probs = dot_nt(v, do_head)
                grad_v = grad_v + dot(weights.astype(BF), do_head)
                row_terms = jnp.sum(weights * grad_probs, axis=0, keepdims=True)
                grad_s = (weights * (grad_probs - row_terms)).astype(BF)
                grad_k = grad_k + dot(grad_s, q_head)
                grad_q.append(dot(k_t[head * HD:(head + 1) * HD], grad_s) * scale)
            grad_q = jnp.concatenate(grad_q, axis=0).T.astype(BF)
            dq[part, lanes] = grad_q
            add_bias(pair, 0, grad_q)
        grad_v = grad_v.astype(BF)
        dk[span, lanes] = grad_k.astype(BF)
        dv[span, lanes] = grad_v
        add_bias(pair, half, grad_v)

    def proj_phase(index):
        if index == 0:
            load(12).wait()
        free_ring(jnp.int32(index + 9))
        left = xv[...]
        grad = (dq, dk, dv)[index]
        emit(index + 9, tall(dot_tn(left, grad[:, :half])), tall(dot_tn(left, grad[:, half:])))

    def dx_copy(index):
        span = pl.ds(pl.multiple_of(index * JR, JR), JR)
        return pltpu.make_async_copy(dxs.at[index % 2], dx_out.at[span], dx_sem.at[index % 2])

    def dx_phase(index):
        @pl.when(index == 0)
        def _():
            load(13).wait()
            load(14).wait()

        @pl.when(index >= 2)
        def _():
            dx_copy(index - 2).wait()

        span = pl.ds(pl.multiple_of(index * JR, JR), JR)
        total = jnp.zeros((JR, depth), F32)
        for side in range(2):
            cols = slice(side * half, side * half + half)
            part = jnp.zeros((JR, depth), F32)
            for i, grad in enumerate((dq, dk, dv)):
                part = part + dot_nt(grad[span, cols], wv[side, i])
            total = total + part
        dxs[index % 2] = total.astype(BF)
        dx_copy(index).start()

    barrier = pltpu.get_barrier_semaphore()
    pl.semaphore_signal(barrier, inc=1, device_id=other, device_id_type=pl.DeviceIdType.MESH)
    for level in range(levels):
        pl.semaphore_signal(barrier, inc=1, device_id=partner(level, 0)[1], device_id_type=pl.DeviceIdType.MESH)
    load(0).start()
    start_blocks(0)
    start_blocks(1)
    for i in range(1, 16):
        load(i).start()
    pl.semaphore_wait(barrier, levels + 1)

    units = seqs * pairs

    def comm(step):
        for stage in range(2 * levels, -1, -1):
            job = step - LAGS[stage]

            @pl.when((job >= 0) & (job < JOBS))
            def _():
                stage_op(stage, job)

    def early(t, carry):
        comm(t)

        @pl.when(t < 4)
        def _():
            down_phase(t)

        @pl.when((t >= 4) & (t < 8))
        def _():
            up_phase(t - 4)

        @pl.when(t == 8)
        def _():
            out_phase()

        return carry

    lax.fori_loop(0, 9, early, 0)

    def middle(i, carry):
        comm(9 + 3 * i)
        attend_phase(2 * i)
        comm(10 + 3 * i)
        attend_phase(2 * i + 1)
        comm(11 + 3 * i)
        return carry

    lax.fori_loop(0, units // 2, middle, 0)
    at = 9 + 3 * (units // 2)

    def late(t, carry):
        comm(at + t)
        for i in range(3):
            @pl.when(t == i)
            def _():
                proj_phase(i)

        @pl.when((t >= 3) & (t < 3 + rows // JR))
        def _():
            dx_phase(t - 3)

        for stage in range(levels + 2):
            @pl.when(t == 1 + 2 * stage)
            def _():
                sum_phase(stage)

        return carry

    lax.fori_loop(0, max(JOBS + LAGS[2 * levels] - at, 2 * levels + 4), late, 0)
    for group in (GROUPS - 3, GROUPS - 2, GROUPS - 1):
        for i in range(3):
            core_copy(group * 3 + i).wait_send()
    dx_copy(rows // JR - 2).wait()
    dx_copy(rows // JR - 1).wait()

    def finish(job, carry):
        pltpu.make_async_copy(prec.at[job], job_out.at[job], out_sem.at[job]).wait()
        return carry

    lax.fori_loop(0, JOBS, finish, 0)
    pltpu.make_async_copy(small_sum.at[levels], small_out, small_sem).wait()


def backward(levels, lens, arrays):
    h_own, glow, c_own, x = arrays[0], arrays[4], arrays[7], arrays[16]
    rows, depth = glow.shape
    half = c_own.shape[1]
    hbm = pl.BlockSpec(memory_space=pl.ANY)
    square = pltpu.VMEM((rows, depth), BF)
    dma = pltpu.SemaphoreType.DMA
    return pl.pallas_call(
        functools.partial(back_kernel, levels),
        out_shape=(
            jax.ShapeDtypeStruct((JOBS, JR, JC), BF),
            jax.ShapeDtypeStruct((rows, depth), BF),
            jax.ShapeDtypeStruct((16, depth), F32),
        ),
        in_specs=[pl.BlockSpec(memory_space=pltpu.SMEM)] + [hbm] * len(arrays),
        out_specs=(hbm, hbm, hbm),
        scratch_shapes=[
            pltpu.VMEM((JOBS, JR, JC), BF), pltpu.VMEM((9, JR, JC), BF), pltpu.VMEM((JOBS, JR, JC), BF),
            pltpu.VMEM((JOBS, JR - (JR >> levels), JC), BF), pltpu.VMEM((2, 2, rows, JC), BF),
            square, square, square, square, square, square, square, square, square,
            pltpu.VMEM((2, 3, depth, half), BF), square, square, square,
            pltpu.VMEM((2, JR, depth), BF), pltpu.VMEM((16, depth), F32),
            pltpu.VMEM((levels + 1, 16, depth), F32), pltpu.VMEM((16, depth), F32), pltpu.VMEM((levels + 1, 16, depth), F32),
            dma((16,)), dma((2, 2)), dma((JOBS,)), dma((JOBS,)), dma((2 * levels, JOBS)), dma((2 * levels, JOBS)), dma((JOBS,)), dma((2,)), dma(()), dma((levels + 1,)), dma((levels + 1,)),
        ],
        compiler_params=pltpu.CompilerParams(vmem_limit_bytes=67043328, collective_id=1, has_side_effects=True),
        cost_estimate=pl.CostEstimate(flops=60 << 30, bytes_accessed=64 << 20, transcendentals=8 << 20),
        name="backward",
    )(lens, *arrays)


def unpack_kernel(jobs_ref, gf_ref, dx_ref, small_ref, tok_ref, qkv_ref, qvb_ref, out_ref, up_ref, upb_ref, down_ref, *vec_refs):
    step = pl.program_id(0)
    depth = small_ref.shape[1]

    def unslab(target):
        for i in range(3):
            rows = slice(i * 128, i * 128 + 128)
            target[rows, :JC] = jobs_ref[i, :128, :].astype(F32)
            target[rows, JC:] = jobs_ref[i, 128:, :].astype(F32)

    def tall(store):
        for i in range(3):
            store(i, jobs_ref[i].astype(F32))

    @pl.when(step < 4)
    def _():
        unslab(down_ref)
        tok_ref[...] = gf_ref[...] + dx_ref[...].astype(F32)

    @pl.when((step >= 4) & (step < 8))
    def _():
        for i in range(3):
            up_ref[i * JR:(i + 1) * JR, :] = jobs_ref[i].astype(F32)

    @pl.when(step == 8)
    def _():
        unslab(out_ref)
        for i, ref in enumerate(vec_refs):
            ref[...] = small_ref[i]
        upb_ref[:depth] = small_ref[8]
        upb_ref[depth:] = small_ref[9]
        qvb_ref[0:1, :] = small_ref[10:11, :JC]
        qvb_ref[1:2, :] = small_ref[10:11, JC:]

    @pl.when(step >= 9)
    def _():
        for i in range(3):
            qkv_ref[0, i * JR:(i + 1) * JR, :] = jobs_ref[i].astype(F32)


def unpack(jobs, grad_first, dx, small, wide):
    rows, depth = grad_first.shape

    def rows_at(i):
        return (jnp.minimum(i, 3), 0)

    quarter = pl.BlockSpec((rows // 4, depth), rows_at)

    def whole(shape):
        return pl.BlockSpec(shape, lambda i: (0, 0))

    def flat(size):
        return pl.BlockSpec((size,), lambda i: (0,))

    vec = jax.ShapeDtypeStruct((depth,), F32)
    return pl.pallas_call(
        unpack_kernel,
        grid=(GROUPS,),
        out_shape=(
            jax.ShapeDtypeStruct((rows, depth), F32), jax.ShapeDtypeStruct((3, depth, JC), F32), jax.ShapeDtypeStruct((2, JC), F32),
            jax.ShapeDtypeStruct((JC, depth), F32), jax.ShapeDtypeStruct((depth, wide), F32), jax.ShapeDtypeStruct((wide,), F32),
            jax.ShapeDtypeStruct((wide, depth), F32), vec, vec, vec, vec, vec, vec,
        ),
        in_specs=[pl.BlockSpec((3, JR, JC), lambda i: (i, 0, 0)), quarter, quarter, whole((16, depth))],
        out_specs=[
            quarter, pl.BlockSpec((1, depth, JC), lambda i: (jnp.clip(i - 9, 0, 2), 0, 0)), whole((2, JC)), whole((JC, depth)),
            pl.BlockSpec((depth, JC), lambda i: (0, jnp.clip(i - 4, 0, 3))), flat(wide), pl.BlockSpec((JC, depth), rows_at),
        ] + [flat(depth)] * 6,
        compiler_params=pltpu.CompilerParams(vmem_limit_bytes=62 << 20),
        name="unpack",
    )(jobs, grad_first, dx, small)


def body(tokens, lengths, qkv_weight, qv_bias, out_weight, out_bias, first_gain, first_shift, up_weight, up_bias, down_weight, down_bias, second_gain, second_shift, cotangent):
    n_tensor = lax.axis_size("tensor")
    n_dp = lax.axis_size("dp")
    core = lax.axis_index("tensor")
    seqs = lengths.shape[0] // n_tensor
    lens = lax.dynamic_slice(lengths, (core * seqs,), (seqs,))
    levels = 4

    def swap(value):
        return lax.ppermute(value, "tensor", [(0, 1), (1, 0)])

    up_row = up_bias.reshape(1, -1)
    peer_qkv, peer_qv_bias = swap(qkv_weight), swap(qv_bias)
    peer_out, peer_up, peer_up_row, peer_down = swap(out_weight), swap(up_weight), swap(up_row), swap(down_weight)
    q_own, k_own, v_own, c_own = attention(lens, tokens, qkv_weight, qv_bias)
    q_peer, k_peer, v_peer, c_peer = attention(lens, tokens, peer_qkv, peer_qv_bias)
    vecs = jnp.stack([out_bias, first_gain, first_shift, down_bias, second_gain, second_shift, out_bias, out_bias])
    layer_out, h_own, h_peer, gu_own, gu_peer, mid, glow, flow, gctx, grad_first, sums = ffn(
        c_own, c_peer, tokens, cotangent, out_weight, peer_out, up_weight, peer_up, up_row, peer_up_row, down_weight, peer_down, vecs
    )
    jobs, dx, sums = backward(
        levels, lens,
        (h_own, h_peer, gu_own, gu_peer, glow, mid, flow, c_own, c_peer, q_own, q_peer, k_own, k_peer, v_own, v_peer, gctx, tokens, qkv_weight, peer_qkv, sums),
    )
    inner = 1 << levels
    if n_dp > inner:
        groups = [[i + inner * g for g in range(n_dp // inner)] for i in range(inner)]
        jobs, sums = lax.psum((jobs, sums), "dp", axis_index_groups=groups)
    grad_tokens, grad_qkv, grad_qv_bias, grad_out, grad_up, grad_up_bias, grad_down, *vectors = unpack(jobs, grad_first, dx, sums, up_bias.shape[0])
    return (
        layer_out, grad_tokens, grad_qkv, grad_qv_bias, grad_out, vectors[0], vectors[1], vectors[2],
        grad_up, grad_up_bias, grad_down, vectors[3], vectors[4], vectors[5],
    )


def solution(mesh):
    tokens = P(("dp", "tensor"), None)
    columns = P(None, "tensor")
    cube = P(None, None, "tensor")
    split = P("tensor", None)
    return jax.shard_map(
        body,
        mesh=mesh,
        in_specs=(tokens, P("dp"), cube, columns, split, P(), P(), P(), columns, P("tensor"), split, P(), P(), P(), tokens),
        out_specs=(tokens, tokens, cube, columns, split, P(), P(), P(), columns, P("tensor"), split, P(), P(), P()),
        check_vma=False,
    )
```

```python
import functools

import jax
import jax.numpy as jnp
from jax import lax
from jax.experimental import pallas as pl
from jax.experimental.pallas import tpu as pltpu
from jax.sharding import PartitionSpec as P

HD = 64
EPS = 1e-06
BF = jnp.bfloat16
F32 = jnp.float32
NEG = -1000000000.0
JR, JC = 256, 384


def dot(a, b):
    return lax.dot_general(a, b, (((1,), (0,)), ((), ())), preferred_element_type=F32)


def dot_nt(a, b):
    return lax.dot_general(a, b, (((1,), (1,)), ((), ())), preferred_element_type=F32)


def dot_tn(a, b):
    return lax.dot_general(a, b, (((0,), (0,)), ((), ())), preferred_element_type=F32)


def half_masks(shape, dim):
    low = lax.broadcasted_iota(jnp.int32, shape, dim) % (2 * HD) < HD
    return low


def attn_kernel(qb, lens_ref, x_ref, w_ref, b_ref, q_ref, k_ref, v_ref, c_ref):
    length = lens_ref[pl.program_id(0)]
    x = x_ref[...]
    rows, width = q_ref.shape
    scale = HD ** (-0.5)
    q_ref[...] = (dot(x, w_ref[0]) + b_ref[0:1, :]).astype(BF) * jnp.asarray(scale, BF)
    k_ref[...] = dot(x, w_ref[1]).astype(BF)
    v_ref[...] = (dot(x, w_ref[2]) + b_ref[1:2, :]).astype(BF)
    for pair in range(width // 128):
        lanes = slice(pair * 128, pair * 128 + 128)
        k = k_ref[:, lanes]
        v_t = v_ref[:, lanes].T
        for block in range(rows // qb):
            span = slice(block * qb, block * qb + qb)
            q = q_ref[span, lanes]
            low = half_masks(q.shape, 1)
            zero = jnp.zeros_like(q)
            parts = []
            for head in range(2):
                q_head = jnp.where(low, q, zero) if head == 0 else jnp.where(low, zero, q)
                s = dot_nt(k, q_head)
                is_valid = lax.broadcasted_iota(jnp.int32, s.shape, 0) < length
                s = jnp.where(is_valid, s, NEG)
                top = jnp.max(s, axis=0, keepdims=True)
                e = jnp.exp(s - top)
                total = jnp.sum(e, axis=0, keepdims=True)
                c_t = dot(v_t[head * HD:(head + 1) * HD], e.astype(BF))
                parts.append(c_t * (1.0 / total))
            c_ref[span, lanes] = jnp.concatenate(parts, axis=0).T.astype(BF)


def attention(lens, x, weight, bias, qb=512):
    rows, depth = x.shape
    seqs = lens.shape[0]
    seq_len = rows // seqs
    width = weight.shape[2]
    row_spec = pl.BlockSpec((seq_len, width), lambda s, _: (s, 0))
    out = jax.ShapeDtypeStruct((rows, width), BF)
    flops = 2 * rows * depth * width * 3 + 4 * rows * seq_len * width
    return pl.pallas_call(
        functools.partial(attn_kernel, qb),
        out_shape=(out, out, out, out),
        grid_spec=pltpu.PrefetchScalarGridSpec(
            num_scalar_prefetch=1,
            grid=(seqs,),
            in_specs=[
                pl.BlockSpec((seq_len, depth), lambda s, _: (s, 0)),
                pl.BlockSpec(weight.shape, lambda s, _: (0, 0, 0)),
                pl.BlockSpec(bias.shape, lambda s, _: (0, 0)),
            ],
            out_specs=[row_spec] * 4,
        ),
        compiler_params=pltpu.CompilerParams(vmem_limit_bytes=56 << 20),
        cost_estimate=pl.CostEstimate(flops=flops * 3, bytes_accessed=12 << 20, transcendentals=rows * seq_len * width // HD),
        name="attend",
    )(lens, x, weight, bias)


def norm_stats(rows_in):
    centre = rows_in - jnp.mean(rows_in, axis=-1, keepdims=True)
    spread = jnp.mean(centre * centre, axis=-1, keepdims=True)
    root = lax.rsqrt(spread + EPS)
    return centre * root, root


def norm_back(grad, normed, root):
    first = jnp.mean(grad, axis=-1, keepdims=True)
    second = jnp.mean(grad * normed, axis=-1, keepdims=True)
    return root * (grad - first - normed * second)


def gelu_both(u):
    z = jnp.abs(u) * (0.5 ** 0.5)
    t = 1.0 / (1.0 + 0.3275911 * z)
    poly = 1.061405429 * t - 1.453152027
    poly = poly * t + 1.421413741
    poly = poly * t - 0.284496736
    poly = poly * t + 0.254829592
    bell = jnp.exp(-0.5 * (u * u))
    tail = 0.5 * (poly * t) * bell
    phi_cdf = jnp.where(u < 0.0, tail, 1.0 - tail)
    return u * phi_cdf, phi_cdf + u * (bell * 0.3989422804014327)


def ffn_kernel(
    chunk,
    c_own, c_peer, x_ref, cot_ref, wo_own, wo_peer, wu_own, wu_peer, bu_own, bu_peer, wd_own, wd_peer, vec_ref,
    out_ref, h_own, h_peer, gp_own, gp_peer, mid_ref, glow_ref, gs_ref, fin_ref, small_ref,
):
    step = pl.program_id(0)
    wide = wu_own.shape[1]
    out_bias, gain1, shift1, down_bias, gain2, shift2 = (vec_ref[i:i + 1, :] for i in range(6))

    @pl.when(step == 0)
    def _():
        small_ref[...] = jnp.zeros_like(small_ref)

    def colsum(index, value):
        small_ref[index:index + 1, :] += jnp.sum(value, axis=0, keepdims=True)

    attn_sum = dot(c_own[...], wo_own[...]) + dot(c_peer[...], wo_peer[...])
    first_in = x_ref[...].astype(F32) + attn_sum + out_bias
    fin_ref[...] = first_in
    n1, _ = norm_stats(first_in)
    first_out = n1 * gain1 + shift1
    middle = first_out.astype(BF)
    mid_ref[...] = middle
    ffn_sum = jnp.zeros_like(first_out)
    for wu, bu, wd, h_ref, gp_ref in ((wu_own, bu_own, wd_own, h_own, gp_own), (wu_peer, bu_peer, wd_peer, h_peer, gp_peer)):
        for at in range(0, wide, chunk):
            cols = slice(at, at + chunk)
            u = dot(middle, wu[:, cols]) + bu[:, cols]
            act, slope = gelu_both(u)
            act = act.astype(BF)
            h_ref[:, cols] = act
            gp_ref[:, cols] = slope.astype(BF)
            ffn_sum = ffn_sum + dot(act, wd[cols, :])
    n2, root2 = norm_stats(first_out + ffn_sum + down_bias)
    out_ref[...] = n2 * gain2 + shift2
    cot = cot_ref[...].astype(F32)
    colsum(4, cot * n2)
    colsum(5, cot)
    grad_second = norm_back(cot * gain2, n2, root2)
    colsum(3, grad_second)
    glow_ref[...] = grad_second.astype(BF)
    gs_ref[...] = grad_second


def ffn(c_own, c_peer, x, cot, wo_own, wo_peer, wu_own, wu_peer, bu_own, bu_peer, wd_own, wd_peer, vecs, tile=256):
    rows, depth = x.shape
    half = c_own.shape[1]
    wide = wu_own.shape[1]
    chunk = depth

    def tiled(cols):
        return pl.BlockSpec((tile, cols), lambda i: (i, 0))

    def fixed(shape):
        return pl.BlockSpec(shape, lambda i: (0, 0), pipeline_mode=pl.Buffered(1))

    def sds(cols, dtype):
        return jax.ShapeDtypeStruct((rows, cols), dtype)

    fixed_in = (wo_own, wo_peer, wu_own, wu_peer, bu_own, bu_peer, wd_own, wd_peer, vecs)
    return pl.pallas_call(
        functools.partial(ffn_kernel, chunk),
        grid=(rows // tile,),
        out_shape=(
            sds(depth, F32), sds(wide, BF), sds(wide, BF), sds(wide, BF), sds(wide, BF),
            sds(depth, BF), sds(depth, BF), sds(depth, F32), sds(depth, F32),
            jax.ShapeDtypeStruct((16, depth), F32),
        ),
        in_specs=[tiled(half), tiled(half), tiled(depth), tiled(depth)] + [fixed(a.shape) for a in fixed_in],
        out_specs=[
            tiled(depth), tiled(wide), tiled(wide), tiled(wide), tiled(wide),
            tiled(depth), tiled(depth), tiled(depth), tiled(depth),
            pl.BlockSpec((16, depth), lambda i: (0, 0)),
        ],
        compiler_params=pltpu.CompilerParams(vmem_limit_bytes=60 << 20),
        cost_estimate=pl.CostEstimate(flops=rows * depth * (4 * 2 * wide + 4 * depth), bytes_accessed=48 << 20, transcendentals=rows * wide * 2),
        name="feed",
    )(c_own, c_peer, x, cot, *fixed_in)


LAGS = (1, 4, 7, 9, 12, 15, 17, 19, 22)
GROUPS = 12
BLOCKS = 1
JOBS = 3 * GROUPS


def back_kernel(
    levels,
    lens_ref, h_own, h_peer, gp_own, gp_peer, glow_in, mid_in, gs_in, fin_in, c_own, c_peer, q_own, q_peer, k_own, k_peer, v_own, v_peer, x_in, w_own, w_peer, small_in,
    wu_own, wu_peer, wd_own, wd_peer, wo_own, wo_peer, vec_in,
    job_out, dx_out, small_out,
    buf, ring, prec, rbuf, blocks, glow, mid, flow, ctx, qv, kv, vv, dov, wv, wdb, acc, fin, vec, dq, dk, dv, dxs, small, small_sum, small_send, small_recv,
    load_sem, blk_sem, wt_sem, core_send, core_recv, hop_send, hop_recv, out_sem, dx_sem, small_sem, sum_send, sum_recv,
):
    dp = lax.axis_index("dp")
    core = lax.axis_index("tensor")
    half = ctx.shape[1] // 2
    rows, depth = glow.shape
    seqs = lens_ref.shape[0]
    seq_len = rows // seqs
    pairs = qv.shape[1] // 128
    scale = HD ** (-0.5)
    other = (dp, 1 - core)

    def partner(level, job):
        flip = job % 2
        mask = (1 + flip, 4, 2 - flip, 8)[level]
        bit = (dp // mask) % 2
        return bit, (dp + mask * (1 - 2 * bit), core)

    def loads():
        return (
            (glow_in, glow, 0), (mid_in, mid, 1), (c_own, ctx.at[:, :half], 2), (c_peer, ctx.at[:, half:], 3), (gs_in, acc, 4),
            (q_own, qv.at[:, :half], 5), (q_peer, qv.at[:, half:], 6), (k_own, kv.at[:, :half], 7), (k_peer, kv.at[:, half:], 8),
            (v_own, vv.at[:, :half], 9), (v_peer, vv.at[:, half:], 10), (fin_in, fin, 11), (x_in, mid, 12), (w_own, wv.at[0], 13), (w_peer, wv.at[1], 14), (small_in, small, 15),
            (vec_in, vec, 16), (wo_own, wdb.at[0, 0], 17), (wo_peer, wdb.at[0, 1], 18),
        )

    def load(index):
        src, dst, sem = loads()[index]
        return pltpu.make_async_copy(src, dst, load_sem.at[sem])

    def block_copies(src_own, src_peer, index, slot):
        cols = pl.ds(pl.multiple_of(index * JC, 128), JC)
        return (
            pltpu.make_async_copy(src_own.at[:, cols], blocks.at[slot, 0], blk_sem.at[slot, 0]),
            pltpu.make_async_copy(src_peer.at[:, cols], blocks.at[slot, 1], blk_sem.at[slot, 1]),
        )

    def start_blocks(index):
        @pl.when(index < 4)
        def _():
            for copy in block_copies(h_own, h_peer, index, index % 2):
                copy.start()

        @pl.when((index >= 4) & (index < 8))
        def _():
            for copy in block_copies(gp_own, gp_peer, index - 4, index % 2):
                copy.start()

    def weight_copies(index, side):
        slot = index % 2
        span = pl.ds(pl.multiple_of(index * JC, 128), JC)
        up, down = ((wu_own, wd_own), (wu_peer, wd_peer))[side]
        return (
            pltpu.make_async_copy(up.at[:, span], wv.at[side, slot], wt_sem.at[0, slot, side]),
            pltpu.make_async_copy(down.at[span], wdb.at[slot, side], wt_sem.at[1, slot, side]),
        )

    def start_weights(index):
        for side in range(2):
            for copy in weight_copies(index, side):
                copy.start()

    def core_copy(job):
        return pltpu.make_async_remote_copy(
            src_ref=ring.at[job % 9], dst_ref=prec.at[job], send_sem=core_send.at[job], recv_sem=core_recv.at[job],
            device_id=other, device_id_type=pl.DeviceIdType.MESH,
        )

    def offsets(job):
        spots = [0]
        for level in range(levels):
            bit, _ = partner(level, job)
            spots.append(spots[-1] + bit * (JR >> (level + 1)))
        return spots

    def hop(job, stage):
        if stage < levels:
            level = stage
            size = JR >> (level + 1)
            bit, device = partner(level, job)
            at = pl.multiple_of(offsets(job)[level] + (1 - bit) * size, 16)
            src = buf.at[job, pl.ds(at, size)]
            begin = JR - (JR >> level)
            dst = rbuf.at[job, begin:begin + size]
        else:
            level = 2 * levels - 1 - stage
            size = JR >> (level + 1)
            bit, device = partner(level, job)
            at = pl.multiple_of(offsets(job)[level + 1], 16)
            src = prec.at[job, pl.ds(at, size)]
            dst = prec.at[job, pl.ds(at, size)]
        return pltpu.make_async_remote_copy(
            src_ref=src, dst_ref=dst, send_sem=hop_send.at[stage, job], recv_sem=hop_recv.at[stage, job],
            device_id=device, device_id_type=pl.DeviceIdType.MESH,
        )

    def stage_op(stage, job):
        if stage == 0:
            core_copy(job).wait_recv()
            buf[job] = buf[job] + prec[job]
            hop(job, 0).start()
            return
        before = hop(job, stage - 1)
        before.wait_recv()
        before.wait_send()
        if stage <= levels:
            level = stage - 1
            size = JR >> stage
            at = pl.multiple_of(offsets(job)[stage], 16)
            begin = JR - (JR >> level)
            keep = buf[job, pl.ds(at, size)] + rbuf[job, begin:begin + size]
            target = prec if stage == levels else buf
            target[job, pl.ds(at, size)] = keep
        if stage < 2 * levels:
            hop(job, stage).start()
        else:
            pltpu.make_async_copy(prec.at[job], job_out.at[job], out_sem.at[job]).start()

    def emit_side(group, which, pieces):
        for i, (top, bottom) in enumerate(pieces):
            job = group * 3 + i
            target = buf.at[job] if which == 0 else ring.at[job % 9]
            cut = top.shape[0]
            target[:cut, :] = top.astype(BF)
            if bottom is not None:
                target[cut:, :] = bottom.astype(BF)
            if which == 1:
                core_copy(job).start()

    def emit(group, own, peer):
        emit_side(group, 0, own)
        emit_side(group, 1, peer)

    def free_ring(group):
        @pl.when(group >= 3)
        def _():
            for i in range(3):
                core_copy((group - 3) * 3 + i).wait_send()

    def slabs(block):
        return [(block[i * 128:(i + 1) * 128, :JC], block[i * 128:(i + 1) * 128, JC:]) for i in range(3)]

    def tall(block):
        return [(block[i * JR:(i + 1) * JR], None) for i in range(3)]

    def down_phase(index):
        @pl.when(index == 0)
        def _():
            load(0).wait()

        for copy in block_copies(h_own, h_peer, index, index % 2):
            copy.wait()
        free_ring(index)
        right = glow[...]
        slot = index % 2
        emit(index, slabs(dot_tn(blocks[slot, 0], right)), slabs(dot_tn(blocks[slot, 1], right)))
        start_blocks(index + 2)

    def up_phase(index, side):
        slot = index % 2
        if side == 0:
            @pl.when(index == 0)
            def _():
                for i in (1, 4, 15):
                    load(i).wait()

            free_ring(index + 4)
        block_copies(gp_own, gp_peer, index, slot)[side].wait()
        for copy in weight_copies(index, side):
            copy.wait()
        grad_up = (dot_nt(glow[...], wdb[slot, side]) * blocks[slot, side].astype(F32)).astype(BF)
        total = jnp.sum(grad_up.astype(F32), axis=0, keepdims=True)
        for row in range(2):
            @pl.when(index // 2 == row)
            def _():
                lanes = pl.ds(pl.multiple_of((index % 2) * JC, 128), JC)
                small[8 + 2 * side + row:9 + 2 * side + row, lanes] = total
        emit_side(index + 4, side, tall(dot_tn(mid[...], grad_up)))
        acc[...] = acc[...] + dot_nt(grad_up, wv[side, slot])
        if side == 1:
            start_blocks(index + 6)

            @pl.when(index < 2)
            def _():
                start_weights(index + 2)

            @pl.when(index == 2)
            def _():
                load(17).start()
                load(18).start()

            @pl.when(index == 3)
            def _():
                for i in (12, 13, 14):
                    load(i).start()

    def norm_phase(index):
        @pl.when(index == 0)
        def _():
            for i in (11, 16, 17, 18):
                load(i).wait()
            small[0:3, :] = jnp.zeros((3, depth), F32)

        gain1 = vec[1:2, :]

        def piece(i, carry):
            span = pl.ds(pl.multiple_of(index * (rows // 2) + i * JR, JR), JR)
            n1, root1 = norm_stats(fin[span, :])
            grad = acc[span, :]
            small[1:2, :] += jnp.sum(grad * n1, axis=0, keepdims=True)
            small[2:3, :] += jnp.sum(grad, axis=0, keepdims=True)
            grad_first = norm_back(grad * gain1, n1, root1)
            small[0:1, :] += jnp.sum(grad_first, axis=0, keepdims=True)
            acc[span, :] = grad_first
            low = grad_first.astype(BF)
            flow[span, :] = low
            dov[span, :half] = dot_nt(low, wdb[0, 0]).astype(BF)
            dov[span, half:] = dot_nt(low, wdb[0, 1]).astype(BF)
            return carry

        lax.fori_loop(0, rows // 2 // JR, piece, 0)

    def out_phase():
        for i in (2, 3):
            load(i).wait()
        free_ring(8)
        right = flow[...]
        emit(8, slabs(dot_tn(ctx[:, :half], right)), slabs(dot_tn(ctx[:, half:], right)))

    def add_bias(pair, offset, value):
        total = jnp.sum(value.astype(F32), axis=0, keepdims=True)
        for side in range(2):
            @pl.when(pair // (pairs // 2) == side)
            def _():
                lanes = pl.ds(pl.multiple_of(offset + (pair - side * (pairs // 2)) * 128, 128), 128)
                small[12 + side:13 + side, lanes] += total

    def sum_hop(stage):
        if stage == 0:
            src, device = small_send, other
        else:
            src, device = small_sum.at[stage - 1], partner(stage - 1, 0)[1]
        return pltpu.make_async_remote_copy(
            src_ref=src, dst_ref=small_recv.at[stage], send_sem=sum_send.at[stage], recv_sem=sum_recv.at[stage],
            device_id=device, device_id_type=pl.DeviceIdType.MESH,
        )

    def sum_phase(stage):
        if stage == 0:
            small_send[0:8, :] = small[0:8, :]
            small_send[8:10, :] = small[10:12, :]
            small_send[10:11, :] = small[13:14, :]
            small_send[11:16, :] = jnp.zeros((5, depth), F32)
        else:
            sum_hop(stage - 1).wait_recv()
            sum_hop(stage - 1).wait_send()
            if stage == 1:
                got = small_recv[0]
                small_sum[0, 0:8, :] = small[0:8, :] + got[0:8, :]
                small_sum[0, 8:10, :] = small[8:10, :] + got[8:10, :]
                small_sum[0, 10:11, :] = small[12:13, :] + got[10:11, :]
                small_sum[0, 11:16, :] = jnp.zeros((5, depth), F32)
            else:
                small_sum[stage - 1] = small_sum[stage - 2] + small_recv[stage - 1]
        if stage <= levels:
            sum_hop(stage).start()
        else:
            pltpu.make_async_copy(small_sum.at[levels], small_out, small_sem).start()

    def attend_phase(unit):
        @pl.when(unit == 0)
        def _():
            for i in range(5, 11):
                load(i).wait()
            small[12:14, :] = jnp.zeros((2, depth), F32)

        inner = unit % (2 * seqs)
        seq = inner % seqs
        pair = unit // (2 * seqs) + (inner // seqs) * (pairs // 2)
        length = lens_ref[seq]
        span = pl.ds(pl.multiple_of(seq * seq_len, seq_len), seq_len)
        lanes = pl.ds(pl.multiple_of(pair * 128, 128), 128)
        k = kv[span, lanes]
        v = vv[span, lanes]
        k_t = k.T
        low = half_masks((1, 128), 1)
        qb = seq_len // BLOCKS
        grad_k = jnp.zeros((seq_len, 128), F32)
        grad_v = jnp.zeros((seq_len, 128), F32)
        for block in range(BLOCKS):
            part = pl.ds(pl.multiple_of(seq * seq_len + block * qb, qb), qb)
            q = qv[part, lanes]
            do = dov[part, lanes]
            grad_q = []
            for head in range(2):
                pick = low if head == 0 else jnp.logical_not(low)
                q_head = jnp.where(pick, q, jnp.zeros_like(q))
                do_head = jnp.where(pick, do, jnp.zeros_like(do))
                s = dot_nt(k, q_head)
                is_valid = lax.broadcasted_iota(jnp.int32, s.shape, 0) < length
                s = jnp.where(is_valid, s, NEG)
                e = jnp.exp(s - jnp.max(s, axis=0, keepdims=True))
                weights = e * (1.0 / jnp.sum(e, axis=0, keepdims=True))
                grad_probs = dot_nt(v, do_head)
                grad_v = grad_v + dot(weights.astype(BF), do_head)
                row_terms = jnp.sum(weights * grad_probs, axis=0, keepdims=True)
                grad_s = (weights * (grad_probs - row_terms)).astype(BF)
                grad_k = grad_k + dot(grad_s, q_head)
                grad_q.append(dot(k_t[head * HD:(head + 1) * HD], grad_s) * scale)
            grad_q = jnp.concatenate(grad_q, axis=0).T.astype(BF)
            dq[part, lanes] = grad_q
            add_bias(pair, 0, grad_q)
        grad_v = grad_v.astype(BF)
        dk[span, lanes] = grad_k.astype(BF)
        dv[span, lanes] = grad_v
        add_bias(pair, half, grad_v)

    def proj_phase(index):
        @pl.when(index == 0)
        def _():
            load(12).wait()

        free_ring(index + 9)
        left = mid[...]
        for side in range(2):
            lanes = pl.ds(pl.multiple_of(side * half + index * 128, 128), 128)
            right = jnp.concatenate([dq[:, lanes], dk[:, lanes], dv[:, lanes]], axis=1)
            emit_side(index + 9, side, tall(dot_tn(left, right)))

    def dx_copy(index):
        span = pl.ds(pl.multiple_of(index * JR, JR), JR)
        return pltpu.make_async_copy(dxs.at[index % 2], dx_out.at[span], dx_sem.at[index % 2])

    def dx_phase(index):
        @pl.when(index == 0)
        def _():
            load(13).wait()
            load(14).wait()

        @pl.when(index >= 2)
        def _():
            dx_copy(index - 2).wait()

        span = pl.ds(pl.multiple_of(index * JR, JR), JR)
        total = jnp.zeros((JR, depth), F32)
        for side in range(2):
            cols = slice(side * half, side * half + half)
            part = jnp.zeros((JR, depth), F32)
            for i, grad in enumerate((dq, dk, dv)):
                part = part + dot_nt(grad[span, cols], wv[side, i])
            total = total + part
        dxs[index % 2] = total + acc[span, :]
        dx_copy(index).start()

    barrier = pltpu.get_barrier_semaphore()
    pl.semaphore_signal(barrier, inc=1, device_id=other, device_id_type=pl.DeviceIdType.MESH)
    for level in range(levels):
        pl.semaphore_signal(barrier, inc=1, device_id=partner(level, 0)[1], device_id_type=pl.DeviceIdType.MESH)
    load(0).start()
    start_blocks(0)
    start_blocks(1)
    load(1).start()
    start_weights(0)
    start_weights(1)
    for i in (4, 15, 11, 16, 2, 3, 5, 6, 7, 8, 9, 10):
        load(i).start()
    pl.semaphore_wait(barrier, levels + 1)

    units = seqs * pairs

    def comm(step):
        for stage in range(2 * levels, -1, -1):
            job = step - LAGS[stage]

            @pl.when((job >= 0) & (job < JOBS))
            def _():
                stage_op(stage, job)

    first = 4 + 2 * 4 + 3
    after = first + 3 * (units // 2)
    turn = 2 * seqs // 2 * 3

    def tick(t, carry):
        comm(t)

        @pl.when(t < 4)
        def _():
            down_phase(t)

        for side in range(2):
            @pl.when((t >= 4) & (t < 12) & (t % 2 == side))
            def _():
                up_phase((t - 4) // 2, side)

        @pl.when((t >= 12) & (t < 14))
        def _():
            norm_phase(t - 12)

        @pl.when(t == 14)
        def _():
            out_phase()

        spot = t - first

        @pl.when((spot > 0) & (spot <= after - first) & (spot % turn == 0))
        def _():
            proj_phase(spot // turn - 1)

        @pl.when((spot >= 0) & (t < after) & (spot % 3 < 2))
        def _():
            attend_phase(spot // 3 * 2 + spot % 3)

        @pl.when((t > after) & (t <= after + rows // JR))
        def _():
            dx_phase(t - after - 1)

        for stage in range(levels + 2):
            @pl.when(t == after + 1 + 2 * stage)
            def _():
                sum_phase(stage)

        return carry

    lax.fori_loop(0, max(JOBS + LAGS[2 * levels], after + 2 * levels + 4), tick, 0)
    for group in (GROUPS - 3, GROUPS - 2, GROUPS - 1):
        for i in range(3):
            core_copy(group * 3 + i).wait_send()
    dx_copy(rows // JR - 2).wait()
    dx_copy(rows // JR - 1).wait()

    def finish(job, carry):
        pltpu.make_async_copy(prec.at[job], job_out.at[job], out_sem.at[job]).wait()
        return carry

    lax.fori_loop(0, JOBS, finish, 0)
    pltpu.make_async_copy(small_sum.at[levels], small_out, small_sem).wait()


def backward(levels, lens, arrays):
    glow, c_own = arrays[4], arrays[8]
    rows, depth = glow.shape
    half = c_own.shape[1]
    hbm = pl.BlockSpec(memory_space=pl.ANY)
    square = pltpu.VMEM((rows, depth), BF)
    dma = pltpu.SemaphoreType.DMA
    return pl.pallas_call(
        functools.partial(back_kernel, levels),
        out_shape=(
            jax.ShapeDtypeStruct((JOBS, JR, JC), BF),
            jax.ShapeDtypeStruct((rows, depth), F32),
            jax.ShapeDtypeStruct((16, depth), F32),
        ),
        in_specs=[pl.BlockSpec(memory_space=pltpu.SMEM)] + [hbm] * len(arrays),
        out_specs=(hbm, hbm, hbm),
        scratch_shapes=[
            pltpu.VMEM((JOBS, JR, JC), BF), pltpu.VMEM((9, JR, JC), BF), pltpu.VMEM((JOBS, JR, JC), BF),
            pltpu.VMEM((JOBS, JR - (JR >> levels), JC), BF), pltpu.VMEM((2, 2, rows, JC), BF),
            square, square, square, square, square, square, square, square,
            pltpu.VMEM((2, 3, depth, half), BF), pltpu.VMEM((2, 2, JC, depth), BF), pltpu.VMEM((rows, depth), F32), pltpu.VMEM((rows, depth), F32), pltpu.VMEM((8, depth), F32), square, square, square,
            pltpu.VMEM((2, JR, depth), F32), pltpu.VMEM((16, depth), F32),
            pltpu.VMEM((levels + 1, 16, depth), F32), pltpu.VMEM((16, depth), F32), pltpu.VMEM((levels + 1, 16, depth), F32),
            dma((19,)), dma((2, 2)), dma((2, 2, 2)), dma((JOBS,)), dma((JOBS,)), dma((2 * levels, JOBS)), dma((2 * levels, JOBS)), dma((JOBS,)), dma((2,)), dma(()), dma((levels + 1,)), dma((levels + 1,)),
        ],
        compiler_params=pltpu.CompilerParams(vmem_limit_bytes=67043328, collective_id=1, has_side_effects=True),
        cost_estimate=pl.CostEstimate(flops=60 << 30, bytes_accessed=64 << 20, transcendentals=8 << 20),
        name="backward",
    )(lens, *arrays)


def unpack_kernel(jobs_ref, dx_ref, small_ref, tok_ref, qkv_ref, qvb_ref, out_ref, up_ref, upb_ref, down_ref, *vec_refs):
    step = pl.program_id(0)
    depth = small_ref.shape[1]

    def unslab(target):
        for i in range(3):
            rows = slice(i * 128, i * 128 + 128)
            target[rows, :JC] = jobs_ref[i, :128, :].astype(F32)
            target[rows, JC:] = jobs_ref[i, 128:, :].astype(F32)

    def tall(store):
        for i in range(3):
            store(i, jobs_ref[i].astype(F32))

    @pl.when(step < 4)
    def _():
        unslab(down_ref)
        tok_ref[...] = dx_ref[...]

    @pl.when((step >= 4) & (step < 8))
    def _():
        for i in range(3):
            up_ref[i * JR:(i + 1) * JR, :] = jobs_ref[i].astype(F32)

    @pl.when(step == 8)
    def _():
        unslab(out_ref)
        for i, ref in enumerate(vec_refs):
            ref[...] = small_ref[i]
        upb_ref[:depth] = small_ref[8]
        upb_ref[depth:] = small_ref[9]
        qvb_ref[0:1, :] = small_ref[10:11, :JC]
        qvb_ref[1:2, :] = small_ref[10:11, JC:]

    @pl.when(step >= 9)
    def _():
        for i in range(3):
            for c in range(3):
                qkv_ref[c, i * JR:(i + 1) * JR, :] = jobs_ref[i, :, c * 128:c * 128 + 128].astype(F32)


def unpack(jobs, dx, small, wide):
    rows, depth = dx.shape

    def rows_at(i):
        return (jnp.minimum(i, 3), 0)

    quarter = pl.BlockSpec((rows // 4, depth), rows_at)

    def whole(shape):
        return pl.BlockSpec(shape, lambda i: (0, 0))

    def flat(size):
        return pl.BlockSpec((size,), lambda i: (0,))

    vec = jax.ShapeDtypeStruct((depth,), F32)
    return pl.pallas_call(
        unpack_kernel,
        grid=(GROUPS,),
        out_shape=(
            jax.ShapeDtypeStruct((rows, depth), F32), jax.ShapeDtypeStruct((3, depth, JC), F32), jax.ShapeDtypeStruct((2, JC), F32),
            jax.ShapeDtypeStruct((JC, depth), F32), jax.ShapeDtypeStruct((depth, wide), F32), jax.ShapeDtypeStruct((wide,), F32),
            jax.ShapeDtypeStruct((wide, depth), F32), vec, vec, vec, vec, vec, vec,
        ),
        in_specs=[pl.BlockSpec((3, JR, JC), lambda i: (i, 0, 0)), quarter, whole((16, depth))],
        out_specs=[
            quarter, pl.BlockSpec((3, depth, 128), lambda i: (0, 0, jnp.clip(i - 9, 0, 2))), whole((2, JC)), whole((JC, depth)),
            pl.BlockSpec((depth, JC), lambda i: (0, jnp.clip(i - 4, 0, 3))), flat(wide), pl.BlockSpec((JC, depth), rows_at),
        ] + [flat(depth)] * 6,
        compiler_params=pltpu.CompilerParams(vmem_limit_bytes=62 << 20),
        name="unpack",
    )(jobs, dx, small)


def body(tokens, lengths, qkv_weight, qv_bias, out_weight, out_bias, first_gain, first_shift, up_weight, up_bias, down_weight, down_bias, second_gain, second_shift, cotangent):
    n_tensor = lax.axis_size("tensor")
    n_dp = lax.axis_size("dp")
    core = lax.axis_index("tensor")
    seqs = lengths.shape[0] // n_tensor
    lens = lax.dynamic_slice(lengths, (core * seqs,), (seqs,))
    levels = 4

    def swap(value):
        return lax.ppermute(value, "tensor", [(0, 1), (1, 0)])

    up_row = up_bias.reshape(1, -1)
    peer_qkv, peer_qv_bias = swap(qkv_weight), swap(qv_bias)
    peer_out, peer_up, peer_up_row, peer_down = swap(out_weight), swap(up_weight), swap(up_row), swap(down_weight)
    q_own, k_own, v_own, c_own = attention(lens, tokens, qkv_weight, qv_bias)
    q_peer, k_peer, v_peer, c_peer = attention(lens, tokens, peer_qkv, peer_qv_bias)
    vecs = jnp.stack([out_bias, first_gain, first_shift, down_bias, second_gain, second_shift, out_bias, out_bias])
    layer_out, h_own, h_peer, gp_own, gp_peer, mid, glow, grad_second, first_in, sums = ffn(
        c_own, c_peer, tokens, cotangent, out_weight, peer_out, up_weight, peer_up, up_row, peer_up_row, down_weight, peer_down, vecs
    )
    jobs, dx, sums = backward(
        levels, lens,
        (
            h_own, h_peer, gp_own, gp_peer, glow, mid, grad_second, first_in, c_own, c_peer, q_own, q_peer, k_own, k_peer, v_own, v_peer, tokens, qkv_weight, peer_qkv, sums,
            up_weight, peer_up, down_weight, peer_down, out_weight, peer_out, vecs,
        ),
    )
    inner = 1 << levels
    if n_dp > inner:
        groups = [[i + inner * g for g in range(n_dp // inner)] for i in range(inner)]
        jobs, sums = lax.psum((jobs, sums), "dp", axis_index_groups=groups)
    grad_tokens, grad_qkv, grad_qv_bias, grad_out, grad_up, grad_up_bias, grad_down, *vectors = unpack(jobs, dx, sums, up_bias.shape[0])
    return (
        layer_out, grad_tokens, grad_qkv, grad_qv_bias, grad_out, vectors[0], vectors[1], vectors[2],
        grad_up, grad_up_bias, grad_down, vectors[3], vectors[4], vectors[5],
    )


def solution(mesh):
    tokens = P(("dp", "tensor"), None)
    columns = P(None, "tensor")
    cube = P(None, None, "tensor")
    split = P("tensor", None)
    return jax.shard_map(
        body,
        mesh=mesh,
        in_specs=(tokens, P("dp"), cube, columns, split, P(), P(), P(), columns, P("tensor"), split, P(), P(), P(), tokens),
        out_specs=(tokens, tokens, cube, columns, split, P(), P(), P(), columns, P("tensor"), split, P(), P(), P()),
        check_vma=False,
    )
```

```python
import functools

import jax
import jax.numpy as jnp
from jax import lax
from jax.experimental import pallas as pl
from jax.experimental.pallas import tpu as pltpu
from jax.sharding import PartitionSpec as P

HD = 64
EPS = 1e-06
BF = jnp.bfloat16
F32 = jnp.float32
NEG = -1000000000.0
JR, JC = 256, 384


def dot(a, b):
    return lax.dot_general(a, b, (((1,), (0,)), ((), ())), preferred_element_type=F32)


def dot_nt(a, b):
    return lax.dot_general(a, b, (((1,), (1,)), ((), ())), preferred_element_type=F32)


def dot_tn(a, b):
    return lax.dot_general(a, b, (((0,), (0,)), ((), ())), preferred_element_type=F32)


def half_masks(shape, dim):
    low = lax.broadcasted_iota(jnp.int32, shape, dim) % (2 * HD) < HD
    return low


def attn_kernel(qb, lens_ref, x_ref, w_ref, b_ref, q_ref, k_ref, v_ref, c_ref):
    length = lens_ref[pl.program_id(0)]
    x = x_ref[...]
    rows, width = q_ref.shape
    scale = HD ** (-0.5)
    q_ref[...] = (dot(x, w_ref[0]) + b_ref[0:1, :]).astype(BF) * jnp.asarray(scale, BF)
    k_ref[...] = dot(x, w_ref[1]).astype(BF)
    v_ref[...] = (dot(x, w_ref[2]) + b_ref[1:2, :]).astype(BF)
    for pair in range(width // 128):
        lanes = slice(pair * 128, pair * 128 + 128)
        k = k_ref[:, lanes]
        v_t = v_ref[:, lanes].T
        for block in range(rows // qb):
            span = slice(block * qb, block * qb + qb)
            q = q_ref[span, lanes]
            low = half_masks(q.shape, 1)
            zero = jnp.zeros_like(q)
            parts = []
            for head in range(2):
                q_head = jnp.where(low, q, zero) if head == 0 else jnp.where(low, zero, q)
                s = dot_nt(k, q_head)
                is_valid = lax.broadcasted_iota(jnp.int32, s.shape, 0) < length
                s = jnp.where(is_valid, s, NEG)
                top = jnp.max(s, axis=0, keepdims=True)
                e = jnp.exp(s - top)
                total = jnp.sum(e, axis=0, keepdims=True)
                c_t = dot(v_t[head * HD:(head + 1) * HD], e.astype(BF))
                parts.append(c_t * (1.0 / total))
            c_ref[span, lanes] = jnp.concatenate(parts, axis=0).T.astype(BF)


def attention(lens, x, weight, bias, qb=512):
    rows, depth = x.shape
    seqs = lens.shape[0]
    seq_len = rows // seqs
    width = weight.shape[2]
    row_spec = pl.BlockSpec((seq_len, width), lambda s, _: (s, 0))
    out = jax.ShapeDtypeStruct((rows, width), BF)
    flops = 2 * rows * depth * width * 3 + 4 * rows * seq_len * width
    return pl.pallas_call(
        functools.partial(attn_kernel, qb),
        out_shape=(out, out, out, out),
        grid_spec=pltpu.PrefetchScalarGridSpec(
            num_scalar_prefetch=1,
            grid=(seqs,),
            in_specs=[
                pl.BlockSpec((seq_len, depth), lambda s, _: (s, 0)),
                pl.BlockSpec(weight.shape, lambda s, _: (0, 0, 0)),
                pl.BlockSpec(bias.shape, lambda s, _: (0, 0)),
            ],
            out_specs=[row_spec] * 4,
        ),
        compiler_params=pltpu.CompilerParams(vmem_limit_bytes=56 << 20),
        cost_estimate=pl.CostEstimate(flops=flops * 3, bytes_accessed=12 << 20, transcendentals=rows * seq_len * width // HD),
        name="attend",
    )(lens, x, weight, bias)


def norm_stats(rows_in):
    centre = rows_in - jnp.mean(rows_in, axis=-1, keepdims=True)
    spread = jnp.mean(centre * centre, axis=-1, keepdims=True)
    root = lax.rsqrt(spread + EPS)
    return centre * root, root


def norm_back(grad, normed, root):
    first = jnp.mean(grad, axis=-1, keepdims=True)
    second = jnp.mean(grad * normed, axis=-1, keepdims=True)
    return root * (grad - first - normed * second)


def gelu_both(u):
    z = jnp.abs(u) * (0.5 ** 0.5)
    t = 1.0 / (1.0 + 0.3275911 * z)
    poly = 1.061405429 * t - 1.453152027
    poly = poly * t + 1.421413741
    poly = poly * t - 0.284496736
    poly = poly * t + 0.254829592
    bell = jnp.exp(-0.5 * (u * u))
    tail = 0.5 * (poly * t) * bell
    phi_cdf = jnp.where(u < 0.0, tail, 1.0 - tail)
    return u * phi_cdf, phi_cdf + u * (bell * 0.3989422804014327)


def ffn_kernel(
    chunk,
    c_own, c_peer, x_ref, cot_ref, wo_own, wo_peer, wu_own, wu_peer, bu_own, bu_peer, wd_own, wd_peer, vec_ref,
    out_ref, h_own, h_peer, gp_own, gp_peer, mid_ref, glow_ref, gs_ref, fin_ref, small_ref,
):
    step = pl.program_id(0)
    wide = wu_own.shape[1]
    out_bias, gain1, shift1, down_bias, gain2, shift2 = (vec_ref[i:i + 1, :] for i in range(6))

    @pl.when(step == 0)
    def _():
        small_ref[...] = jnp.zeros_like(small_ref)

    def colsum(index, value):
        small_ref[index:index + 1, :] += jnp.sum(value, axis=0, keepdims=True)

    attn_sum = dot(c_own[...], wo_own[...]) + dot(c_peer[...], wo_peer[...])
    first_in = x_ref[...].astype(F32) + attn_sum + out_bias
    fin_ref[...] = first_in
    n1, _ = norm_stats(first_in)
    first_out = n1 * gain1 + shift1
    middle = first_out.astype(BF)
    mid_ref[...] = middle
    ffn_sum = jnp.zeros_like(first_out)
    for wu, bu, wd, h_ref, gp_ref in ((wu_own, bu_own, wd_own, h_own, gp_own), (wu_peer, bu_peer, wd_peer, h_peer, gp_peer)):
        for at in range(0, wide, chunk):
            cols = slice(at, at + chunk)
            u = dot(middle, wu[:, cols]) + bu[:, cols]
            act, slope = gelu_both(u)
            act = act.astype(BF)
            h_ref[:, cols] = act
            gp_ref[:, cols] = slope.astype(BF)
            ffn_sum = ffn_sum + dot(act, wd[cols, :])
    n2, root2 = norm_stats(first_out + ffn_sum + down_bias)
    out_ref[...] = n2 * gain2 + shift2
    cot = cot_ref[...].astype(F32)
    colsum(4, cot * n2)
    colsum(5, cot)
    grad_second = norm_back(cot * gain2, n2, root2)
    colsum(3, grad_second)
    glow_ref[...] = grad_second.astype(BF)
    gs_ref[...] = grad_second


def ffn(c_own, c_peer, x, cot, wo_own, wo_peer, wu_own, wu_peer, bu_own, bu_peer, wd_own, wd_peer, vecs, tile=256):
    rows, depth = x.shape
    half = c_own.shape[1]
    wide = wu_own.shape[1]
    chunk = depth

    def tiled(cols):
        return pl.BlockSpec((tile, cols), lambda i: (i, 0))

    def fixed(shape):
        return pl.BlockSpec(shape, lambda i: (0, 0), pipeline_mode=pl.Buffered(1))

    def sds(cols, dtype):
        return jax.ShapeDtypeStruct((rows, cols), dtype)

    fixed_in = (wo_own, wo_peer, wu_own, wu_peer, bu_own, bu_peer, wd_own, wd_peer, vecs)
    return pl.pallas_call(
        functools.partial(ffn_kernel, chunk),
        grid=(rows // tile,),
        out_shape=(
            sds(depth, F32), sds(wide, BF), sds(wide, BF), sds(wide, BF), sds(wide, BF),
            sds(depth, BF), sds(depth, BF), sds(depth, F32), sds(depth, F32),
            jax.ShapeDtypeStruct((16, depth), F32),
        ),
        in_specs=[tiled(half), tiled(half), tiled(depth), tiled(depth)] + [fixed(a.shape) for a in fixed_in],
        out_specs=[
            tiled(depth), tiled(wide), tiled(wide), tiled(wide), tiled(wide),
            tiled(depth), tiled(depth), tiled(depth), tiled(depth),
            pl.BlockSpec((16, depth), lambda i: (0, 0)),
        ],
        compiler_params=pltpu.CompilerParams(vmem_limit_bytes=60 << 20),
        cost_estimate=pl.CostEstimate(flops=rows * depth * (4 * 2 * wide + 4 * depth), bytes_accessed=48 << 20, transcendentals=rows * wide * 2),
        name="feed",
    )(c_own, c_peer, x, cot, *fixed_in)


LAGS = (1, 3, 5, 7, 9, 12, 14, 16, 19)
GROUPS = 12
BLOCKS = 1
JOBS = 3 * GROUPS


def back_kernel(
    levels,
    lens_ref, h_own, h_peer, gp_own, gp_peer, glow_in, mid_in, gs_in, fin_in, c_own, c_peer, q_own, q_peer, k_own, k_peer, v_own, v_peer, x_in, w_own, w_peer, small_in,
    wu_own, wu_peer, wd_own, wd_peer, wo_own, wo_peer, vec_in,
    job_out, dx_out, small_out,
    buf, ring, prec, rbuf, blocks, glow, mid, flow, ctx, qv, kv, vv, dov, wv, wdb, acc, fin, vec, dq, dk, dv, dxs, small, small_sum, small_send, small_recv,
    load_sem, blk_sem, wt_sem, core_send, core_recv, hop_send, hop_recv, out_sem, dx_sem, small_sem, sum_send, sum_recv,
):
    dp = lax.axis_index("dp")
    core = lax.axis_index("tensor")
    half = ctx.shape[1] // 2
    rows, depth = glow.shape
    seqs = lens_ref.shape[0]
    seq_len = rows // seqs
    pairs = qv.shape[1] // 128
    scale = HD ** (-0.5)
    other = (dp, 1 - core)

    def partner(level, job):
        flip = job & 1
        shift = (flip, 2, 1 - flip, 3)[level]
        bit = (dp >> shift) & 1
        return bit, (dp ^ (1 << shift), core)

    def loads():
        return (
            (glow_in, glow, 0), (mid_in, mid, 1), (c_own, ctx.at[:, :half], 2), (c_peer, ctx.at[:, half:], 3), (gs_in, acc, 4),
            (q_own, qv.at[:, :half], 5), (q_peer, qv.at[:, half:], 6), (k_own, kv.at[:, :half], 7), (k_peer, kv.at[:, half:], 8),
            (v_own, vv.at[:, :half], 9), (v_peer, vv.at[:, half:], 10), (fin_in, fin, 11), (x_in, mid, 12), (w_own, wv.at[0], 13), (w_peer, wv.at[1], 14), (small_in, small, 15),
            (vec_in, vec, 16), (wo_own, wdb.at[0, 0], 17), (wo_peer, wdb.at[0, 1], 18),
        )

    def load(index):
        src, dst, sem = loads()[index]
        return pltpu.make_async_copy(src, dst, load_sem.at[sem])

    def block_copies(src_own, src_peer, index, slot):
        cols = pl.ds(pl.multiple_of(index * JC, 128), JC)
        return (
            pltpu.make_async_copy(src_own.at[:, cols], blocks.at[slot, 0], blk_sem.at[slot, 0]),
            pltpu.make_async_copy(src_peer.at[:, cols], blocks.at[slot, 1], blk_sem.at[slot, 1]),
        )

    def start_blocks(index):
        @pl.when(index < 4)
        def _():
            for copy in block_copies(h_own, h_peer, index, (index & 1)):
                copy.start()

        @pl.when((index >= 4) & (index < 8))
        def _():
            for copy in block_copies(gp_own, gp_peer, index - 4, (index & 1)):
                copy.start()

    def weight_copies(index, side):
        slot = (index & 1)
        span = pl.ds(pl.multiple_of(index * JC, 128), JC)
        up, down = ((wu_own, wd_own), (wu_peer, wd_peer))[side]
        return (
            pltpu.make_async_copy(up.at[:, span], wv.at[side, slot], wt_sem.at[0, slot, side]),
            pltpu.make_async_copy(down.at[span], wdb.at[slot, side], wt_sem.at[1, slot, side]),
        )

    def start_weights(index):
        for side in range(2):
            for copy in weight_copies(index, side):
                copy.start()

    def core_copy(job):
        return pltpu.make_async_remote_copy(
            src_ref=ring.at[job - 9 * (job * 57 >> 9)], dst_ref=prec.at[job], send_sem=core_send.at[job], recv_sem=core_recv.at[job],
            device_id=other, device_id_type=pl.DeviceIdType.MESH,
        )

    def offsets(job):
        spots = [0]
        for level in range(levels):
            bit, _ = partner(level, job)
            spots.append(spots[-1] + (bit << ((JR >> (level + 1)).bit_length() - 1)))
        return spots

    def hop(job, stage):
        if stage < levels:
            level = stage
            size = JR >> (level + 1)
            bit, device = partner(level, job)
            at = pl.multiple_of(offsets(job)[level] + (1 - bit) * size, 16)
            src = buf.at[job, pl.ds(at, size)]
            begin = JR - (JR >> level)
            dst = rbuf.at[job, begin:begin + size]
        else:
            level = 2 * levels - 1 - stage
            size = JR >> (level + 1)
            bit, device = partner(level, job)
            at = pl.multiple_of(offsets(job)[level + 1], 16)
            src = prec.at[job, pl.ds(at, size)]
            dst = prec.at[job, pl.ds(at, size)]
        return pltpu.make_async_remote_copy(
            src_ref=src, dst_ref=dst, send_sem=hop_send.at[stage, job], recv_sem=hop_recv.at[stage, job],
            device_id=device, device_id_type=pl.DeviceIdType.MESH,
        )

    def stage_op(stage, job):
        if stage == 0:
            core_copy(job).wait_recv()
            buf[job] = buf[job] + prec[job]
            hop(job, 0).start()
            return
        before = hop(job, stage - 1)
        before.wait_recv()
        before.wait_send()
        if stage <= levels:
            level = stage - 1
            size = JR >> stage
            at = pl.multiple_of(offsets(job)[stage], 16)
            begin = JR - (JR >> level)
            keep = buf[job, pl.ds(at, size)] + rbuf[job, begin:begin + size]
            target = prec if stage == levels else buf
            target[job, pl.ds(at, size)] = keep
        if stage < 2 * levels:
            hop(job, stage).start()
        else:
            pltpu.make_async_copy(prec.at[job], job_out.at[job], out_sem.at[job]).start()

    def emit_side(group, which, pieces):
        for i, (top, bottom) in enumerate(pieces):
            job = group * 3 + i
            target = buf.at[job] if which == 0 else ring.at[job - 9 * (job * 57 >> 9)]
            cut = top.shape[0]
            target[:cut, :] = top.astype(BF)
            if bottom is not None:
                target[cut:, :] = bottom.astype(BF)
            if which == 1:
                core_copy(job).start()

    def emit(group, own, peer):
        emit_side(group, 0, own)
        emit_side(group, 1, peer)

    def free_ring(group):
        @pl.when(group >= 3)
        def _():
            for i in range(3):
                core_copy((group - 3) * 3 + i).wait_send()

    def slabs(block):
        return [(block[i * 128:(i + 1) * 128, :JC], block[i * 128:(i + 1) * 128, JC:]) for i in range(3)]

    def tall(block):
        return [(block[i * JR:(i + 1) * JR], None) for i in range(3)]

    def down_phase(index):
        @pl.when(index == 0)
        def _():
            load(0).wait()

        for copy in block_copies(h_own, h_peer, index, (index & 1)):
            copy.wait()
        free_ring(index)
        right = glow[...]
        slot = (index & 1)
        emit(index, slabs(dot_tn(blocks[slot, 0], right)), slabs(dot_tn(blocks[slot, 1], right)))
        start_blocks(index + 2)

    def up_phase(index, side):
        slot = (index & 1)
        if side == 0:
            @pl.when(index == 0)
            def _():
                for i in (1, 4, 15):
                    load(i).wait()

            free_ring(index + 4)
        block_copies(gp_own, gp_peer, index, slot)[side].wait()
        for copy in weight_copies(index, side):
            copy.wait()
        grad_up = (dot_nt(glow[...], wdb[slot, side]) * blocks[slot, side].astype(F32)).astype(BF)
        total = jnp.sum(grad_up.astype(F32), axis=0, keepdims=True)
        for row in range(2):
            @pl.when(index // 2 == row)
            def _():
                lanes = pl.ds(pl.multiple_of(((index & 1)) * JC, 128), JC)
                small[8 + 2 * side + row:9 + 2 * side + row, lanes] = total
        emit_side(index + 4, side, tall(dot_tn(mid[...], grad_up)))
        acc[...] = acc[...] + dot_nt(grad_up, wv[side, slot])
        if side == 1:
            start_blocks(index + 6)

            @pl.when(index < 2)
            def _():
                start_weights(index + 2)

            @pl.when(index == 2)
            def _():
                load(17).start()
                load(18).start()

            @pl.when(index == 3)
            def _():
                for i in (12, 13, 14):
                    load(i).start()

    def norm_phase(index):
        @pl.when(index == 0)
        def _():
            for i in (11, 16, 17, 18):
                load(i).wait()
            small[0:3, :] = jnp.zeros((3, depth), F32)

        gain1 = vec[1:2, :]

        def piece(i, carry):
            span = pl.ds(pl.multiple_of(index * (rows // 2) + i * JR, JR), JR)
            n1, root1 = norm_stats(fin[span, :])
            grad = acc[span, :]
            small[1:2, :] += jnp.sum(grad * n1, axis=0, keepdims=True)
            small[2:3, :] += jnp.sum(grad, axis=0, keepdims=True)
            grad_first = norm_back(grad * gain1, n1, root1)
            small[0:1, :] += jnp.sum(grad_first, axis=0, keepdims=True)
            acc[span, :] = grad_first
            low = grad_first.astype(BF)
            flow[span, :] = low
            dov[span, :half] = dot_nt(low, wdb[0, 0]).astype(BF)
            dov[span, half:] = dot_nt(low, wdb[0, 1]).astype(BF)
            return carry

        lax.fori_loop(0, rows // 2 // JR, piece, 0)

    def out_phase():
        for i in (2, 3):
            load(i).wait()
        free_ring(8)
        right = flow[...]
        emit(8, slabs(dot_tn(ctx[:, :half], right)), slabs(dot_tn(ctx[:, half:], right)))

    def add_bias(pair, offset, value):
        total = jnp.sum(value.astype(F32), axis=0, keepdims=True)
        for side in range(2):
            @pl.when(pair // (pairs // 2) == side)
            def _():
                lanes = pl.ds(pl.multiple_of(offset + (pair - side * (pairs // 2)) * 128, 128), 128)
                small[12 + side:13 + side, lanes] += total

    def sum_hop(stage):
        if stage == 0:
            src, device = small_send, other
        else:
            src, device = small_sum.at[stage - 1], partner(stage - 1, 0)[1]
        return pltpu.make_async_remote_copy(
            src_ref=src, dst_ref=small_recv.at[stage], send_sem=sum_send.at[stage], recv_sem=sum_recv.at[stage],
            device_id=device, device_id_type=pl.DeviceIdType.MESH,
        )

    def sum_phase(stage):
        if stage == 0:
            small_send[0:8, :] = small[0:8, :]
            small_send[8:10, :] = small[10:12, :]
            small_send[10:11, :] = small[13:14, :]
            small_send[11:16, :] = jnp.zeros((5, depth), F32)
        else:
            sum_hop(stage - 1).wait_recv()
            sum_hop(stage - 1).wait_send()
            if stage == 1:
                got = small_recv[0]
                small_sum[0, 0:8, :] = small[0:8, :] + got[0:8, :]
                small_sum[0, 8:10, :] = small[8:10, :] + got[8:10, :]
                small_sum[0, 10:11, :] = small[12:13, :] + got[10:11, :]
                small_sum[0, 11:16, :] = jnp.zeros((5, depth), F32)
            else:
                small_sum[stage - 1] = small_sum[stage - 2] + small_recv[stage - 1]
        if stage <= levels:
            sum_hop(stage).start()
        else:
            pltpu.make_async_copy(small_sum.at[levels], small_out, small_sem).start()

    def attend_phase(unit):
        @pl.when(unit == 0)
        def _():
            for i in range(5, 11):
                load(i).wait()
            small[12:14, :] = jnp.zeros((2, depth), F32)

        inner = unit % (2 * seqs)
        seq = inner % seqs
        pair = unit // (2 * seqs) + (inner // seqs) * (pairs // 2)
        length = lens_ref[seq]
        span = pl.ds(pl.multiple_of(seq * seq_len, seq_len), seq_len)
        lanes = pl.ds(pl.multiple_of(pair * 128, 128), 128)
        k = kv[span, lanes]
        v = vv[span, lanes]
        k_t = k.T
        low = half_masks((1, 128), 1)
        qb = seq_len // BLOCKS
        grad_k = jnp.zeros((seq_len, 128), F32)
        grad_v = jnp.zeros((seq_len, 128), F32)
        for block in range(BLOCKS):
            part = pl.ds(pl.multiple_of(seq * seq_len + block * qb, qb), qb)
            q = qv[part, lanes]
            do = dov[part, lanes]
            grad_q = []
            for head in range(2):
                pick = low if head == 0 else jnp.logical_not(low)
                q_head = jnp.where(pick, q, jnp.zeros_like(q))
                do_head = jnp.where(pick, do, jnp.zeros_like(do))
                s = dot_nt(k, q_head)
                is_valid = lax.broadcasted_iota(jnp.int32, s.shape, 0) < length
                s = jnp.where(is_valid, s, NEG)
                e = jnp.exp(s - jnp.max(s, axis=0, keepdims=True))
                weights = e * (1.0 / jnp.sum(e, axis=0, keepdims=True))
                grad_probs = dot_nt(v, do_head)
                grad_v = grad_v + dot(weights.astype(BF), do_head)
                row_terms = jnp.sum(weights * grad_probs, axis=0, keepdims=True)
                grad_s = (weights * (grad_probs - row_terms)).astype(BF)
                grad_k = grad_k + dot(grad_s, q_head)
                grad_q.append(dot(k_t[head * HD:(head + 1) * HD], grad_s) * scale)
            grad_q = jnp.concatenate(grad_q, axis=0).T.astype(BF)
            dq[part, lanes] = grad_q
            add_bias(pair, 0, grad_q)
        grad_v = grad_v.astype(BF)
        dk[span, lanes] = grad_k.astype(BF)
        dv[span, lanes] = grad_v
        add_bias(pair, half, grad_v)

    def proj_phase(index):
        @pl.when(index == 0)
        def _():
            load(12).wait()

        free_ring(index + 9)
        left = mid[...]
        for side in range(2):
            lanes = pl.ds(pl.multiple_of(side * half + index * 128, 128), 128)
            right = jnp.concatenate([dq[:, lanes], dk[:, lanes], dv[:, lanes]], axis=1)
            emit_side(index + 9, side, tall(dot_tn(left, right)))

    def dx_copy(index):
        span = pl.ds(pl.multiple_of(index * JR, JR), JR)
        return pltpu.make_async_copy(dxs.at[(index & 1)], dx_out.at[span], dx_sem.at[(index & 1)])

    def dx_phase(index):
        @pl.when(index == 0)
        def _():
            load(13).wait()
            load(14).wait()

        @pl.when(index >= 2)
        def _():
            dx_copy(index - 2).wait()

        span = pl.ds(pl.multiple_of(index * JR, JR), JR)
        total = jnp.zeros((JR, depth), F32)
        for side in range(2):
            cols = slice(side * half, side * half + half)
            part = jnp.zeros((JR, depth), F32)
            for i, grad in enumerate((dq, dk, dv)):
                part = part + dot_nt(grad[span, cols], wv[side, i])
            total = total + part
        dxs[(index & 1)] = total + acc[span, :]
        dx_copy(index).start()

    barrier = pltpu.get_barrier_semaphore()
    pl.semaphore_signal(barrier, inc=1, device_id=other, device_id_type=pl.DeviceIdType.MESH)
    for level in range(levels):
        pl.semaphore_signal(barrier, inc=1, device_id=partner(level, 0)[1], device_id_type=pl.DeviceIdType.MESH)
    load(0).start()
    start_blocks(0)
    start_blocks(1)
    load(1).start()
    start_weights(0)
    start_weights(1)
    for i in (4, 15, 11, 16, 2, 3, 5, 6, 7, 8, 9, 10):
        load(i).start()
    pl.semaphore_wait(barrier, levels + 1)

    norm_at = 4 + 2 * 4
    first = norm_at + 2 + 1
    turn = 3 * seqs
    after = first + turn * (pairs // 2)
    end = max(JOBS + LAGS[2 * levels], after + 2 * levels + 4)

    def comm(step, low, high):
        for stage in range(2 * levels, -1, -1):
            job = step - LAGS[stage]
            most, least = high - LAGS[stage], low - LAGS[stage]
            if most < 0 or least >= JOBS:
                continue
            if least >= 0 and most < JOBS:
                stage_op(stage, job)
            else:
                @pl.when((job >= 0) & (job < JOBS))
                def _():
                    stage_op(stage, job)

    def down_part(t, carry):
        comm(t, 0, 3)
        down_phase(t)
        return carry

    def up_part(i, carry):
        for side in range(2):
            comm(4 + 2 * i + side, 4, norm_at - 1)
            up_phase(i, side)
        return carry

    def norm_part(i, carry):
        comm(norm_at + i, norm_at, norm_at + 1)
        norm_phase(i)
        return carry

    def head_part(p, carry):
        def unit_part(u, inner):
            t = first + turn * p + (u >> 1) * 3 + (u & 1)
            comm(t, first, after - 1)
            attend_phase(p * (2 * seqs) + u)

            @pl.when((u & 1) == 1)
            def _():
                comm(t + 1, first, after - 1)

            return inner

        lax.fori_loop(0, 2 * seqs, unit_part, 0)
        proj_phase(p)
        return carry

    def last_part(t, carry):
        comm(t, after, end - 1)

        @pl.when(t < after + rows // JR)
        def _():
            dx_phase(t - after)

        for stage in range(levels + 2):
            @pl.when(t == after + 1 + 2 * stage)
            def _():
                sum_phase(stage)

        return carry

    lax.fori_loop(0, 4, down_part, 0)
    lax.fori_loop(0, 4, up_part, 0)
    lax.fori_loop(0, 2, norm_part, 0)
    comm(jnp.int32(first - 1), first - 1, first - 1)
    out_phase()
    lax.fori_loop(0, pairs // 2, head_part, 0)
    lax.fori_loop(after, end, last_part, 0)
    for group in (GROUPS - 3, GROUPS - 2, GROUPS - 1):
        for i in range(3):
            core_copy(group * 3 + i).wait_send()
    dx_copy(rows // JR - 2).wait()
    dx_copy(rows // JR - 1).wait()

    def finish(job, carry):
        pltpu.make_async_copy(prec.at[job], job_out.at[job], out_sem.at[job]).wait()
        return carry

    lax.fori_loop(0, JOBS, finish, 0)
    pltpu.make_async_copy(small_sum.at[levels], small_out, small_sem).wait()


def backward(levels, lens, arrays):
    glow, c_own = arrays[4], arrays[8]
    rows, depth = glow.shape
    half = c_own.shape[1]
    hbm = pl.BlockSpec(memory_space=pl.ANY)
    square = pltpu.VMEM((rows, depth), BF)
    dma = pltpu.SemaphoreType.DMA
    return pl.pallas_call(
        functools.partial(back_kernel, levels),
        out_shape=(
            jax.ShapeDtypeStruct((JOBS, JR, JC), BF),
            jax.ShapeDtypeStruct((rows, depth), F32),
            jax.ShapeDtypeStruct((16, depth), F32),
        ),
        in_specs=[pl.BlockSpec(memory_space=pltpu.SMEM)] + [hbm] * len(arrays),
        out_specs=(hbm, hbm, hbm),
        scratch_shapes=[
            pltpu.VMEM((JOBS, JR, JC), BF), pltpu.VMEM((9, JR, JC), BF), pltpu.VMEM((JOBS, JR, JC), BF),
            pltpu.VMEM((JOBS, JR - (JR >> levels), JC), BF), pltpu.VMEM((2, 2, rows, JC), BF),
            square, square, square, square, square, square, square, square,
            pltpu.VMEM((2, 3, depth, half), BF), pltpu.VMEM((2, 2, JC, depth), BF), pltpu.VMEM((rows, depth), F32), pltpu.VMEM((rows, depth), F32), pltpu.VMEM((8, depth), F32), square, square, square,
            pltpu.VMEM((2, JR, depth), F32), pltpu.VMEM((16, depth), F32),
            pltpu.VMEM((levels + 1, 16, depth), F32), pltpu.VMEM((16, depth), F32), pltpu.VMEM((levels + 1, 16, depth), F32),
            dma((19,)), dma((2, 2)), dma((2, 2, 2)), dma((JOBS,)), dma((JOBS,)), dma((2 * levels, JOBS)), dma((2 * levels, JOBS)), dma((JOBS,)), dma((2,)), dma(()), dma((levels + 1,)), dma((levels + 1,)),
        ],
        compiler_params=pltpu.CompilerParams(vmem_limit_bytes=67043328, collective_id=1, has_side_effects=True),
        cost_estimate=pl.CostEstimate(flops=60 << 30, bytes_accessed=64 << 20, transcendentals=8 << 20),
        name="backward",
    )(lens, *arrays)


def unpack_kernel(jobs_ref, dx_ref, small_ref, tok_ref, qkv_ref, qvb_ref, out_ref, up_ref, upb_ref, down_ref, *vec_refs):
    step = pl.program_id(0)
    depth = small_ref.shape[1]

    def unslab(target):
        for i in range(3):
            rows = slice(i * 128, i * 128 + 128)
            target[rows, :JC] = jobs_ref[i, :128, :].astype(F32)
            target[rows, JC:] = jobs_ref[i, 128:, :].astype(F32)

    def tall(store):
        for i in range(3):
            store(i, jobs_ref[i].astype(F32))

    @pl.when(step < 4)
    def _():
        unslab(down_ref)
        tok_ref[...] = dx_ref[...]

    @pl.when((step >= 4) & (step < 8))
    def _():
        for i in range(3):
            up_ref[i * JR:(i + 1) * JR, :] = jobs_ref[i].astype(F32)

    @pl.when(step == 8)
    def _():
        unslab(out_ref)
        for i, ref in enumerate(vec_refs):
            ref[...] = small_ref[i]
        upb_ref[:depth] = small_ref[8]
        upb_ref[depth:] = small_ref[9]
        qvb_ref[0:1, :] = small_ref[10:11, :JC]
        qvb_ref[1:2, :] = small_ref[10:11, JC:]

    @pl.when(step >= 9)
    def _():
        for i in range(3):
            for c in range(3):
                qkv_ref[c, i * JR:(i + 1) * JR, :] = jobs_ref[i, :, c * 128:c * 128 + 128].astype(F32)


def unpack(jobs, dx, small, wide):
    rows, depth = dx.shape

    def rows_at(i):
        return (jnp.minimum(i, 3), 0)

    quarter = pl.BlockSpec((rows // 4, depth), rows_at)

    def whole(shape):
        return pl.BlockSpec(shape, lambda i: (0, 0))

    def flat(size):
        return pl.BlockSpec((size,), lambda i: (0,))

    vec = jax.ShapeDtypeStruct((depth,), F32)
    return pl.pallas_call(
        unpack_kernel,
        grid=(GROUPS,),
        out_shape=(
            jax.ShapeDtypeStruct((rows, depth), F32), jax.ShapeDtypeStruct((3, depth, JC), F32), jax.ShapeDtypeStruct((2, JC), F32),
            jax.ShapeDtypeStruct((JC, depth), F32), jax.ShapeDtypeStruct((depth, wide), F32), jax.ShapeDtypeStruct((wide,), F32),
            jax.ShapeDtypeStruct((wide, depth), F32), vec, vec, vec, vec, vec, vec,
        ),
        in_specs=[pl.BlockSpec((3, JR, JC), lambda i: (i, 0, 0)), quarter, whole((16, depth))],
        out_specs=[
            quarter, pl.BlockSpec((3, depth, 128), lambda i: (0, 0, jnp.clip(i - 9, 0, 2))), whole((2, JC)), whole((JC, depth)),
            pl.BlockSpec((depth, JC), lambda i: (0, jnp.clip(i - 4, 0, 3))), flat(wide), pl.BlockSpec((JC, depth), rows_at),
        ] + [flat(depth)] * 6,
        compiler_params=pltpu.CompilerParams(vmem_limit_bytes=62 << 20),
        name="unpack",
    )(jobs, dx, small)


def body(tokens, lengths, qkv_weight, qv_bias, out_weight, out_bias, first_gain, first_shift, up_weight, up_bias, down_weight, down_bias, second_gain, second_shift, cotangent):
    n_tensor = lax.axis_size("tensor")
    n_dp = lax.axis_size("dp")
    core = lax.axis_index("tensor")
    seqs = lengths.shape[0] // n_tensor
    lens = lax.dynamic_slice(lengths, (core * seqs,), (seqs,))
    levels = 4

    def swap(value):
        return lax.ppermute(value, "tensor", [(0, 1), (1, 0)])

    up_row = up_bias.reshape(1, -1)
    peer_qkv, peer_qv_bias = swap(qkv_weight), swap(qv_bias)
    peer_out, peer_up, peer_up_row, peer_down = swap(out_weight), swap(up_weight), swap(up_row), swap(down_weight)
    q_own, k_own, v_own, c_own = attention(lens, tokens, qkv_weight, qv_bias)
    q_peer, k_peer, v_peer, c_peer = attention(lens, tokens, peer_qkv, peer_qv_bias)
    vecs = jnp.stack([out_bias, first_gain, first_shift, down_bias, second_gain, second_shift, out_bias, out_bias])
    layer_out, h_own, h_peer, gp_own, gp_peer, mid, glow, grad_second, first_in, sums = ffn(
        c_own, c_peer, tokens, cotangent, out_weight, peer_out, up_weight, peer_up, up_row, peer_up_row, down_weight, peer_down, vecs
    )
    jobs, dx, sums = backward(
        levels, lens,
        (
            h_own, h_peer, gp_own, gp_peer, glow, mid, grad_second, first_in, c_own, c_peer, q_own, q_peer, k_own, k_peer, v_own, v_peer, tokens, qkv_weight, peer_qkv, sums,
            up_weight, peer_up, down_weight, peer_down, out_weight, peer_out, vecs,
        ),
    )
    inner = 1 << levels
    if n_dp > inner:
        groups = [[i + inner * g for g in range(n_dp // inner)] for i in range(inner)]
        jobs, sums = lax.psum((jobs, sums), "dp", axis_index_groups=groups)
    grad_tokens, grad_qkv, grad_qv_bias, grad_out, grad_up, grad_up_bias, grad_down, *vectors = unpack(jobs, dx, sums, up_bias.shape[0])
    return (
        layer_out, grad_tokens, grad_qkv, grad_qv_bias, grad_out, vectors[0], vectors[1], vectors[2],
        grad_up, grad_up_bias, grad_down, vectors[3], vectors[4], vectors[5],
    )


def solution(mesh):
    tokens = P(("dp", "tensor"), None)
    columns = P(None, "tensor")
    cube = P(None, None, "tensor")
    split = P("tensor", None)
    return jax.shard_map(
        body,
        mesh=mesh,
        in_specs=(tokens, P("dp"), cube, columns, split, P(), P(), P(), columns, P("tensor"), split, P(), P(), P(), tokens),
        out_specs=(tokens, tokens, cube, columns, split, P(), P(), P(), columns, P("tensor"), split, P(), P(), P()),
        check_vma=False,
    )
```

```python
import functools

import jax
import jax.numpy as jnp
from jax import lax
from jax.experimental import pallas as pl
from jax.experimental.pallas import tpu as pltpu
from jax.sharding import PartitionSpec as P

HD = 64
EPS = 1e-06
BF = jnp.bfloat16
F32 = jnp.float32
NEG = -1000000000.0
JR, JC = 256, 384


def dot(a, b):
    return lax.dot_general(a, b, (((1,), (0,)), ((), ())), preferred_element_type=F32)


def dot_nt(a, b):
    return lax.dot_general(a, b, (((1,), (1,)), ((), ())), preferred_element_type=F32)


def dot_tn(a, b):
    return lax.dot_general(a, b, (((0,), (0,)), ((), ())), preferred_element_type=F32)


def half_masks(shape, dim):
    low = lax.broadcasted_iota(jnp.int32, shape, dim) % (2 * HD) < HD
    return low


def attn_kernel(qb, lens_ref, x_ref, w_ref, b_ref, q_ref, k_ref, v_ref, c_ref):
    length = lens_ref[pl.program_id(0)]
    x = x_ref[...]
    rows, width = q_ref.shape
    scale = HD ** (-0.5)
    q_ref[...] = (dot(x, w_ref[0]) + b_ref[0:1, :]).astype(BF) * jnp.asarray(scale, BF)
    k_ref[...] = dot(x, w_ref[1]).astype(BF)
    v_ref[...] = (dot(x, w_ref[2]) + b_ref[1:2, :]).astype(BF)
    hide = jnp.where(lax.broadcasted_iota(jnp.int32, (rows, 1), 0) < length, 0.0, NEG)
    for pair in range(width // 128):
        lanes = slice(pair * 128, pair * 128 + 128)
        k = k_ref[:, lanes]
        v_t = v_ref[:, lanes].T
        for block in range(rows // qb):
            span = slice(block * qb, block * qb + qb)
            q = q_ref[span, lanes]
            low = half_masks(q.shape, 1)
            zero = jnp.zeros_like(q)
            parts = []
            for head in range(2):
                q_head = jnp.where(low, q, zero) if head == 0 else jnp.where(low, zero, q)
                s = dot_nt(k, q_head)
                s = s + hide
                top = jnp.max(s, axis=0, keepdims=True)
                e = jnp.exp(s - top)
                total = jnp.sum(e, axis=0, keepdims=True)
                c_t = dot(v_t[head * HD:(head + 1) * HD], e.astype(BF))
                parts.append(c_t * (1.0 / total))
            c_ref[span, lanes] = jnp.concatenate(parts, axis=0).T.astype(BF)


def attention(lens, x, weight, bias, qb=512):
    rows, depth = x.shape
    seqs = lens.shape[0]
    seq_len = rows // seqs
    width = weight.shape[2]
    row_spec = pl.BlockSpec((seq_len, width), lambda s, _: (s, 0))
    out = jax.ShapeDtypeStruct((rows, width), BF)
    flops = 2 * rows * depth * width * 3 + 4 * rows * seq_len * width
    return pl.pallas_call(
        functools.partial(attn_kernel, qb),
        out_shape=(out, out, out, out),
        grid_spec=pltpu.PrefetchScalarGridSpec(
            num_scalar_prefetch=1,
            grid=(seqs,),
            in_specs=[
                pl.BlockSpec((seq_len, depth), lambda s, _: (s, 0)),
                pl.BlockSpec(weight.shape, lambda s, _: (0, 0, 0)),
                pl.BlockSpec(bias.shape, lambda s, _: (0, 0)),
            ],
            out_specs=[row_spec] * 4,
        ),
        compiler_params=pltpu.CompilerParams(vmem_limit_bytes=56 << 20),
        cost_estimate=pl.CostEstimate(flops=flops * 3, bytes_accessed=12 << 20, transcendentals=rows * seq_len * width // HD),
        name="attend",
    )(lens, x, weight, bias)


def norm_stats(rows_in):
    centre = rows_in - jnp.mean(rows_in, axis=-1, keepdims=True)
    spread = jnp.mean(centre * centre, axis=-1, keepdims=True)
    root = lax.rsqrt(spread + EPS)
    return centre * root, root


def norm_back(grad, normed, root):
    first = jnp.mean(grad, axis=-1, keepdims=True)
    second = jnp.mean(grad * normed, axis=-1, keepdims=True)
    return root * (grad - first - normed * second)


def gelu_both(u):
    z = jnp.abs(u) * (0.5 ** 0.5)
    t = 1.0 / (1.0 + 0.3275911 * z)
    poly = 1.061405429 * t - 1.453152027
    poly = poly * t + 1.421413741
    poly = poly * t - 0.284496736
    poly = poly * t + 0.254829592
    bell = jnp.exp(-0.5 * (u * u))
    tail = 0.5 * (poly * t) * bell
    phi_cdf = jnp.where(u < 0.0, tail, 1.0 - tail)
    return u * phi_cdf, phi_cdf + u * (bell * 0.3989422804014327)


def ffn_kernel(
    chunk,
    c_own, c_peer, x_ref, cot_ref, wo_own_in, wo_peer_in, wu_own_in, wu_peer_in, bu_own, bu_peer, wd_own_in, wd_peer_in, vec_ref,
    out_ref, h_own, h_peer, gp_own, gp_peer, mid_ref, glow_ref, gs_ref, fin_ref, small_ref,
    wo_own, wo_peer, wu_own, wu_peer, wd_own, wd_peer, sem,
):
    step = pl.program_id(0)
    pieces = ((wo_own_in, wo_own), (wo_peer_in, wo_peer), (wu_own_in, wu_own), (wd_own_in, wd_own), (wu_peer_in, wu_peer), (wd_peer_in, wd_peer))
    copies = [pltpu.make_async_copy(src, dst, sem.at[i]) for i, (src, dst) in enumerate(pieces)]

    @pl.when(step == 0)
    def _():
        for copy in copies:
            copy.start()

    def arrived(group):
        @pl.when(step == 0)
        def _():
            for copy in copies[2 * group:2 * group + 2]:
                copy.wait()

    wide = wu_own.shape[1]
    out_bias, gain1, shift1, down_bias, gain2, shift2 = (vec_ref[i:i + 1, :] for i in range(6))

    @pl.when(step == 0)
    def _():
        small_ref[...] = jnp.zeros_like(small_ref)

    def colsum(index, value):
        small_ref[index:index + 1, :] += jnp.sum(value, axis=0, keepdims=True)

    arrived(0)
    attn_sum = dot(c_own[...], wo_own[...]) + dot(c_peer[...], wo_peer[...])
    first_in = x_ref[...].astype(F32) + attn_sum + out_bias
    fin_ref[...] = first_in
    n1, _ = norm_stats(first_in)
    first_out = n1 * gain1 + shift1
    middle = first_out.astype(BF)
    mid_ref[...] = middle
    ffn_sum = jnp.zeros_like(first_out)
    for group, (wu, bu, wd, h_ref, gp_ref) in enumerate(((wu_own, bu_own, wd_own, h_own, gp_own), (wu_peer, bu_peer, wd_peer, h_peer, gp_peer))):
        arrived(group + 1)
        for at in range(0, wide, chunk):
            cols = slice(at, at + chunk)
            u = dot(middle, wu[:, cols]) + bu[:, cols]
            act, slope = gelu_both(u)
            act = act.astype(BF)
            h_ref[:, cols] = act
            gp_ref[:, cols] = slope.astype(BF)
            ffn_sum = ffn_sum + dot(act, wd[cols, :])
    n2, root2 = norm_stats(first_out + ffn_sum + down_bias)
    out_ref[...] = n2 * gain2 + shift2
    cot = cot_ref[...].astype(F32)
    colsum(4, cot * n2)
    colsum(5, cot)
    grad_second = norm_back(cot * gain2, n2, root2)
    colsum(3, grad_second)
    glow_ref[...] = grad_second.astype(BF)
    gs_ref[...] = grad_second


def ffn(c_own, c_peer, x, cot, wo_own, wo_peer, wu_own, wu_peer, bu_own, bu_peer, wd_own, wd_peer, vecs, tile=256):
    rows, depth = x.shape
    half = c_own.shape[1]
    wide = wu_own.shape[1]
    chunk = depth

    def tiled(cols):
        return pl.BlockSpec((tile, cols), lambda i: (i, 0))

    def fixed(shape):
        return pl.BlockSpec(shape, lambda i: (0, 0), pipeline_mode=pl.Buffered(1))

    def sds(cols, dtype):
        return jax.ShapeDtypeStruct((rows, cols), dtype)

    hbm = pl.BlockSpec(memory_space=pl.ANY)
    fixed_in = (wo_own, wo_peer, wu_own, wu_peer, bu_own, bu_peer, wd_own, wd_peer, vecs)
    return pl.pallas_call(
        functools.partial(ffn_kernel, chunk),
        grid=(rows // tile,),
        out_shape=(
            sds(depth, F32), sds(wide, BF), sds(wide, BF), sds(wide, BF), sds(wide, BF),
            sds(depth, BF), sds(depth, BF), sds(depth, F32), sds(depth, F32),
            jax.ShapeDtypeStruct((16, depth), F32),
        ),
        in_specs=[tiled(half), tiled(half), tiled(depth), tiled(depth)] + [hbm if a.dtype == BF else fixed(a.shape) for a in fixed_in],
        out_specs=[
            tiled(depth), tiled(wide), tiled(wide), tiled(wide), tiled(wide),
            tiled(depth), tiled(depth), tiled(depth), tiled(depth),
            pl.BlockSpec((16, depth), lambda i: (0, 0)),
        ],
        scratch_shapes=[pltpu.VMEM(a.shape, BF) for a in (wo_own, wo_peer, wu_own, wu_peer, wd_own, wd_peer)] + [pltpu.SemaphoreType.DMA((6,))],
        compiler_params=pltpu.CompilerParams(vmem_limit_bytes=60 << 20),
        cost_estimate=pl.CostEstimate(flops=rows * depth * (4 * 2 * wide + 4 * depth), bytes_accessed=48 << 20, transcendentals=rows * wide * 2),
        name="feed",
    )(c_own, c_peer, x, cot, *fixed_in)


LAGS = (1, 3, 5, 7, 9, 12, 14, 16, 19)
GROUPS = 12
BLOCKS = 1
JOBS = 3 * GROUPS


def back_kernel(
    levels,
    lens_ref, h_own, h_peer, gp_own, gp_peer, glow_in, mid_in, gs_in, fin_in, c_own, c_peer, q_own, q_peer, k_own, k_peer, v_own, v_peer, x_in, w_own, w_peer, small_in,
    wu_own, wu_peer, wd_own, wd_peer, wo_own, wo_peer, vec_in,
    job_out, dx_out, small_out,
    buf, ring, prec, rbuf, blocks, glow, mid, flow, ctx, qv, kv, vv, dov, wv, wdb, acc, fin, vec, dq, dk, dv, dxs, small, small_sum, small_send, small_recv,
    load_sem, blk_sem, wt_sem, core_send, core_recv, hop_send, hop_recv, out_sem, dx_sem, small_sem, sum_send, sum_recv,
):
    dp = lax.axis_index("dp")
    core = lax.axis_index("tensor")
    half = ctx.shape[1] // 2
    rows, depth = glow.shape
    seqs = lens_ref.shape[0]
    seq_len = rows // seqs
    pairs = qv.shape[1] // 128
    scale = HD ** (-0.5)
    other = (dp, 1 - core)

    def partner(level, job):
        flip = job & 1
        shift = (flip, 2, 1 - flip, 3)[level]
        bit = (dp >> shift) & 1
        return bit, (dp ^ (1 << shift), core)

    def loads():
        return (
            (glow_in, glow, 0), (mid_in, mid, 1), (c_own, ctx.at[:, :half], 2), (c_peer, ctx.at[:, half:], 3), (gs_in, acc, 4),
            (q_own, qv.at[:, :half], 5), (q_peer, qv.at[:, half:], 6), (k_own, kv.at[:, :half], 7), (k_peer, kv.at[:, half:], 8),
            (v_own, vv.at[:, :half], 9), (v_peer, vv.at[:, half:], 10), (fin_in, fin, 11), (x_in, mid, 12), (w_own, wv.at[0], 13), (w_peer, wv.at[1], 14), (small_in, small, 15),
            (vec_in, vec, 16), (wo_own, wdb.at[0, 0], 17), (wo_peer, wdb.at[0, 1], 18),
        )

    def load(index):
        src, dst, sem = loads()[index]
        return pltpu.make_async_copy(src, dst, load_sem.at[sem])

    def block_copies(src_own, src_peer, index, slot):
        cols = pl.ds(pl.multiple_of(index * JC, 128), JC)
        return (
            pltpu.make_async_copy(src_own.at[:, cols], blocks.at[slot, 0], blk_sem.at[slot, 0]),
            pltpu.make_async_copy(src_peer.at[:, cols], blocks.at[slot, 1], blk_sem.at[slot, 1]),
        )

    def start_blocks(index):
        @pl.when(index < 4)
        def _():
            for copy in block_copies(h_own, h_peer, index, (index & 1)):
                copy.start()

        @pl.when((index >= 4) & (index < 8))
        def _():
            for copy in block_copies(gp_own, gp_peer, index - 4, (index & 1)):
                copy.start()

    def weight_copies(index, side):
        slot = (index & 1)
        span = pl.ds(pl.multiple_of(index * JC, 128), JC)
        up, down = ((wu_own, wd_own), (wu_peer, wd_peer))[side]
        return (
            pltpu.make_async_copy(up.at[:, span], wv.at[side, slot], wt_sem.at[0, slot, side]),
            pltpu.make_async_copy(down.at[span], wdb.at[slot, side], wt_sem.at[1, slot, side]),
        )

    def start_weights(index):
        for side in range(2):
            for copy in weight_copies(index, side):
                copy.start()

    def core_copy(job):
        return pltpu.make_async_remote_copy(
            src_ref=ring.at[job - 9 * (job * 57 >> 9)], dst_ref=prec.at[job], send_sem=core_send.at[job], recv_sem=core_recv.at[job],
            device_id=other, device_id_type=pl.DeviceIdType.MESH,
        )

    def offsets(job):
        spots = [0]
        for level in range(levels):
            bit, _ = partner(level, job)
            spots.append(spots[-1] + (bit << ((JR >> (level + 1)).bit_length() - 1)))
        return spots

    def hop(job, stage):
        if stage < levels:
            level = stage
            size = JR >> (level + 1)
            bit, device = partner(level, job)
            at = pl.multiple_of(offsets(job)[level] + (1 - bit) * size, 16)
            src = buf.at[job, pl.ds(at, size)]
            begin = JR - (JR >> level)
            dst = rbuf.at[job, begin:begin + size]
        else:
            level = 2 * levels - 1 - stage
            size = JR >> (level + 1)
            bit, device = partner(level, job)
            at = pl.multiple_of(offsets(job)[level + 1], 16)
            src = prec.at[job, pl.ds(at, size)]
            dst = prec.at[job, pl.ds(at, size)]
        return pltpu.make_async_remote_copy(
            src_ref=src, dst_ref=dst, send_sem=hop_send.at[stage, job], recv_sem=hop_recv.at[stage, job],
            device_id=device, device_id_type=pl.DeviceIdType.MESH,
        )

    def stage_op(stage, job):
        if stage == 0:
            core_copy(job).wait_recv()
            buf[job] = buf[job] + prec[job]
            hop(job, 0).start()
            return
        before = hop(job, stage - 1)
        before.wait_recv()
        before.wait_send()
        if stage <= levels:
            level = stage - 1
            size = JR >> stage
            at = pl.multiple_of(offsets(job)[stage], 16)
            begin = JR - (JR >> level)
            keep = buf[job, pl.ds(at, size)] + rbuf[job, begin:begin + size]
            target = prec if stage == levels else buf
            target[job, pl.ds(at, size)] = keep
        if stage < 2 * levels:
            hop(job, stage).start()
        else:
            pltpu.make_async_copy(prec.at[job], job_out.at[job], out_sem.at[job]).start()

    def emit_side(group, which, pieces):
        for i, (top, bottom) in enumerate(pieces):
            job = group * 3 + i
            target = buf.at[job] if which == 0 else ring.at[job - 9 * (job * 57 >> 9)]
            cut = top.shape[0]
            target[:cut, :] = top.astype(BF)
            if bottom is not None:
                target[cut:, :] = bottom.astype(BF)
            if which == 1:
                core_copy(job).start()

    def emit(group, own, peer):
        emit_side(group, 0, own)
        emit_side(group, 1, peer)

    def free_ring(group):
        @pl.when(group >= 3)
        def _():
            for i in range(3):
                core_copy((group - 3) * 3 + i).wait_send()

    def slabs(block):
        return [(block[i * 128:(i + 1) * 128, :JC], block[i * 128:(i + 1) * 128, JC:]) for i in range(3)]

    def tall(block):
        return [(block[i * JR:(i + 1) * JR], None) for i in range(3)]

    def down_phase(index):
        @pl.when(index == 0)
        def _():
            load(0).wait()

        for copy in block_copies(h_own, h_peer, index, (index & 1)):
            copy.wait()
        free_ring(index)
        right = glow[...]
        slot = (index & 1)
        emit(index, slabs(dot_tn(blocks[slot, 0], right)), slabs(dot_tn(blocks[slot, 1], right)))
        start_blocks(index + 2)

    def up_phase(index, side):
        slot = (index & 1)
        if side == 0:
            @pl.when(index == 0)
            def _():
                for i in (1, 4, 15):
                    load(i).wait()

            free_ring(index + 4)
        block_copies(gp_own, gp_peer, index, slot)[side].wait()
        for copy in weight_copies(index, side):
            copy.wait()
        grad_up = (dot_nt(glow[...], wdb[slot, side]) * blocks[slot, side].astype(F32)).astype(BF)
        total = jnp.sum(grad_up.astype(F32), axis=0, keepdims=True)
        for row in range(2):
            @pl.when(index // 2 == row)
            def _():
                lanes = pl.ds(pl.multiple_of(((index & 1)) * JC, 128), JC)
                small[8 + 2 * side + row:9 + 2 * side + row, lanes] = total
        blocks[slot, side] = grad_up
        emit_side(index + 4, side, tall(dot_tn(mid[...], grad_up)))

    def first_phase(index):
        slot = index & 1
        acc[...] = acc[...] + (dot_nt(blocks[slot, 0], wv[0, slot]) + dot_nt(blocks[slot, 1], wv[1, slot]))
        start_blocks(index + 6)

        @pl.when(index < 2)
        def _():
            start_weights(index + 2)

        @pl.when(index == 2)
        def _():
            load(17).start()
            load(18).start()

        @pl.when(index == 3)
        def _():
            for i in (12, 13, 14):
                load(i).start()

    def norm_phase(index):
        @pl.when(index == 0)
        def _():
            for i in (11, 16, 17, 18):
                load(i).wait()
            small[0:3, :] = jnp.zeros((3, depth), F32)

        gain1 = vec[1:2, :]

        def piece(i, carry):
            span = pl.ds(pl.multiple_of(index * (rows // 2) + i * JR, JR), JR)
            n1, root1 = norm_stats(fin[span, :])
            grad = acc[span, :]
            small[1:2, :] += jnp.sum(grad * n1, axis=0, keepdims=True)
            small[2:3, :] += jnp.sum(grad, axis=0, keepdims=True)
            grad_first = norm_back(grad * gain1, n1, root1)
            small[0:1, :] += jnp.sum(grad_first, axis=0, keepdims=True)
            acc[span, :] = grad_first
            low = grad_first.astype(BF)
            flow[span, :] = low
            dov[span, :half] = dot_nt(low, wdb[0, 0]).astype(BF)
            dov[span, half:] = dot_nt(low, wdb[0, 1]).astype(BF)
            return carry

        lax.fori_loop(0, rows // 2 // JR, piece, 0)

    def out_phase():
        for i in (2, 3):
            load(i).wait()
        free_ring(8)
        right = flow[...]
        emit(8, slabs(dot_tn(ctx[:, :half], right)), slabs(dot_tn(ctx[:, half:], right)))

    def add_bias(pair, offset, value):
        total = jnp.sum(value.astype(F32), axis=0, keepdims=True)
        for side in range(2):
            @pl.when(pair // (pairs // 2) == side)
            def _():
                lanes = pl.ds(pl.multiple_of(offset + (pair - side * (pairs // 2)) * 128, 128), 128)
                small[12 + side:13 + side, lanes] += total

    def sum_hop(stage):
        if stage == 0:
            src, device = small_send, other
        else:
            src, device = small_sum.at[stage - 1], partner(stage - 1, 0)[1]
        return pltpu.make_async_remote_copy(
            src_ref=src, dst_ref=small_recv.at[stage], send_sem=sum_send.at[stage], recv_sem=sum_recv.at[stage],
            device_id=device, device_id_type=pl.DeviceIdType.MESH,
        )

    def sum_phase(stage):
        if stage == 0:
            small_send[0:8, :] = small[0:8, :]
            small_send[8:10, :] = small[10:12, :]
            small_send[10:11, :] = small[13:14, :]
            small_send[11:16, :] = jnp.zeros((5, depth), F32)
        else:
            sum_hop(stage - 1).wait_recv()
            sum_hop(stage - 1).wait_send()
            if stage == 1:
                got = small_recv[0]
                small_sum[0, 0:8, :] = small[0:8, :] + got[0:8, :]
                small_sum[0, 8:10, :] = small[8:10, :] + got[8:10, :]
                small_sum[0, 10:11, :] = small[12:13, :] + got[10:11, :]
                small_sum[0, 11:16, :] = jnp.zeros((5, depth), F32)
            else:
                small_sum[stage - 1] = small_sum[stage - 2] + small_recv[stage - 1]
        if stage <= levels:
            sum_hop(stage).start()
        else:
            pltpu.make_async_copy(small_sum.at[levels], small_out, small_sem).start()

    def attend_phase(unit):
        @pl.when(unit == 0)
        def _():
            for i in range(5, 11):
                load(i).wait()
            small[12:14, :] = jnp.zeros((2, depth), F32)

        inner = unit % (2 * seqs)
        seq = inner % seqs
        pair = unit // (2 * seqs) + (inner // seqs) * (pairs // 2)
        length = lens_ref[seq]
        span = pl.ds(pl.multiple_of(seq * seq_len, seq_len), seq_len)
        lanes = pl.ds(pl.multiple_of(pair * 128, 128), 128)
        k = kv[span, lanes]
        v = vv[span, lanes]
        k_t = k.T
        hide = jnp.where(lax.broadcasted_iota(jnp.int32, (seq_len, 1), 0) < length, 0.0, NEG)
        low = half_masks((1, 128), 1)
        qb = seq_len // BLOCKS
        grad_k = jnp.zeros((seq_len, 128), F32)
        grad_v = jnp.zeros((seq_len, 128), F32)
        for block in range(BLOCKS):
            part = pl.ds(pl.multiple_of(seq * seq_len + block * qb, qb), qb)
            q = qv[part, lanes]
            do = dov[part, lanes]
            grad_q = []
            for head in range(2):
                pick = low if head == 0 else jnp.logical_not(low)
                q_head = jnp.where(pick, q, jnp.zeros_like(q))
                do_head = jnp.where(pick, do, jnp.zeros_like(do))
                s = dot_nt(k, q_head)
                s = s + hide
                e = jnp.exp(s - jnp.max(s, axis=0, keepdims=True))
                weights = e * (1.0 / jnp.sum(e, axis=0, keepdims=True))
                grad_probs = dot_nt(v, do_head)
                grad_v = grad_v + dot(weights.astype(BF), do_head)
                row_terms = jnp.sum(weights * grad_probs, axis=0, keepdims=True)
                grad_s = (weights * (grad_probs - row_terms)).astype(BF)
                grad_k = grad_k + dot(grad_s, q_head)
                grad_q.append(dot(k_t[head * HD:(head + 1) * HD], grad_s) * scale)
            grad_q = jnp.concatenate(grad_q, axis=0).T.astype(BF)
            dq[part, lanes] = grad_q
            add_bias(pair, 0, grad_q)
        grad_v = grad_v.astype(BF)
        dk[span, lanes] = grad_k.astype(BF)
        dv[span, lanes] = grad_v
        add_bias(pair, half, grad_v)

    def proj_phase(index):
        @pl.when(index == 0)
        def _():
            load(12).wait()

        free_ring(index + 9)
        left = mid[...]
        for side in range(2):
            lanes = pl.ds(pl.multiple_of(side * half + index * 128, 128), 128)
            right = jnp.concatenate([dq[:, lanes], dk[:, lanes], dv[:, lanes]], axis=1)
            emit_side(index + 9, side, tall(dot_tn(left, right)))

    def dx_copy(index):
        span = pl.ds(pl.multiple_of(index * JR, JR), JR)
        return pltpu.make_async_copy(dxs.at[(index & 1)], dx_out.at[span], dx_sem.at[(index & 1)])

    def dx_phase(index):
        @pl.when(index == 0)
        def _():
            load(13).wait()
            load(14).wait()

        @pl.when(index >= 2)
        def _():
            dx_copy(index - 2).wait()

        span = pl.ds(pl.multiple_of(index * JR, JR), JR)
        total = jnp.zeros((JR, depth), F32)
        for side in range(2):
            cols = slice(side * half, side * half + half)
            part = jnp.zeros((JR, depth), F32)
            for i, grad in enumerate((dq, dk, dv)):
                part = part + dot_nt(grad[span, cols], wv[side, i])
            total = total + part
        dxs[(index & 1)] = total + acc[span, :]
        dx_copy(index).start()

    barrier = pltpu.get_barrier_semaphore()
    pl.semaphore_signal(barrier, inc=1, device_id=other, device_id_type=pl.DeviceIdType.MESH)
    for level in range(levels):
        pl.semaphore_signal(barrier, inc=1, device_id=partner(level, 0)[1], device_id_type=pl.DeviceIdType.MESH)
    load(0).start()
    start_blocks(0)
    start_blocks(1)
    load(1).start()
    start_weights(0)
    start_weights(1)
    for i in (4, 15, 11, 16, 2, 3, 5, 6, 7, 8, 9, 10):
        load(i).start()
    pl.semaphore_wait(barrier, levels + 1)

    norm_at = 4 + 3 * 4
    first = norm_at + 2 + 1
    turn = 3 * seqs
    after = first + turn * (pairs // 2)
    early = JOBS - 3
    gap = max(after - 1 - early, 0)
    end = max(JOBS + gap + LAGS[2 * levels], after + 2 * levels + 4)

    def comm(step, low, high):
        for stage in range(2 * levels, -1, -1):
            slot = step - LAGS[stage]
            most, least = high - LAGS[stage], low - LAGS[stage]
            if most < 0:
                continue
            if most < early:
                job, here = slot, slot >= 0
            else:
                job = slot - jnp.where(slot >= early, gap, 0)
                here = (slot >= 0) & ((slot < early) | (job >= early)) & (job < JOBS)
            if least >= 0 and most < early:
                stage_op(stage, job)
            else:
                @pl.when(here)
                def _():
                    stage_op(stage, job)

    def down_part(t, carry):
        comm(t, 0, 3)
        down_phase(t)
        return carry

    def up_part(i, carry):
        for side in range(2):
            comm(4 + 3 * i + side, 4, norm_at - 1)
            up_phase(i, side)
        comm(6 + 3 * i, 4, norm_at - 1)
        first_phase(i)
        return carry

    def norm_part(i, carry):
        comm(norm_at + i, norm_at, norm_at + 1)
        norm_phase(i)
        return carry

    def head_part(p, carry):
        def unit_part(u, inner):
            t = first + turn * p + (u >> 1) * 3 + (u & 1)
            comm(t, first, after - 1)
            attend_phase(p * (2 * seqs) + u)

            @pl.when((u & 1) == 1)
            def _():
                comm(t + 1, first, after - 1)

            return inner

        lax.fori_loop(0, 2 * seqs, unit_part, 0)
        proj_phase(p)
        return carry

    def last_part(t, carry):
        comm(t, after, end - 1)

        @pl.when(t < after + rows // JR)
        def _():
            dx_phase(t - after)

        for stage in range(levels + 2):
            @pl.when(t == after + 1 + 2 * stage)
            def _():
                sum_phase(stage)

        return carry

    lax.fori_loop(0, 4, down_part, 0)
    lax.fori_loop(0, 4, up_part, 0)
    lax.fori_loop(0, 2, norm_part, 0)
    comm(jnp.int32(first - 1), first - 1, first - 1)
    out_phase()
    lax.fori_loop(0, pairs // 2, head_part, 0)
    lax.fori_loop(after, end, last_part, 0)
    for group in (GROUPS - 3, GROUPS - 2, GROUPS - 1):
        for i in range(3):
            core_copy(group * 3 + i).wait_send()
    dx_copy(rows // JR - 2).wait()
    dx_copy(rows // JR - 1).wait()

    def finish(job, carry):
        pltpu.make_async_copy(prec.at[job], job_out.at[job], out_sem.at[job]).wait()
        return carry

    lax.fori_loop(0, JOBS, finish, 0)
    pltpu.make_async_copy(small_sum.at[levels], small_out, small_sem).wait()


def backward(levels, lens, arrays):
    glow, c_own = arrays[4], arrays[8]
    rows, depth = glow.shape
    half = c_own.shape[1]
    hbm = pl.BlockSpec(memory_space=pl.ANY)
    square = pltpu.VMEM((rows, depth), BF)
    dma = pltpu.SemaphoreType.DMA
    return pl.pallas_call(
        functools.partial(back_kernel, levels),
        out_shape=(
            jax.ShapeDtypeStruct((JOBS, JR, JC), BF),
            jax.ShapeDtypeStruct((rows, depth), F32),
            jax.ShapeDtypeStruct((16, depth), F32),
        ),
        in_specs=[pl.BlockSpec(memory_space=pltpu.SMEM)] + [hbm] * len(arrays),
        out_specs=(hbm, hbm, hbm),
        scratch_shapes=[
            pltpu.VMEM((JOBS, JR, JC), BF), pltpu.VMEM((9, JR, JC), BF), pltpu.VMEM((JOBS, JR, JC), BF),
            pltpu.VMEM((JOBS, JR - (JR >> levels), JC), BF), pltpu.VMEM((2, 2, rows, JC), BF),
            square, square, square, square, square, square, square, square,
            pltpu.VMEM((2, 3, depth, half), BF), pltpu.VMEM((2, 2, JC, depth), BF), pltpu.VMEM((rows, depth), F32), pltpu.VMEM((rows, depth), F32), pltpu.VMEM((8, depth), F32), square, square, square,
            pltpu.VMEM((2, JR, depth), F32), pltpu.VMEM((16, depth), F32),
            pltpu.VMEM((levels + 1, 16, depth), F32), pltpu.VMEM((16, depth), F32), pltpu.VMEM((levels + 1, 16, depth), F32),
            dma((19,)), dma((2, 2)), dma((2, 2, 2)), dma((JOBS,)), dma((JOBS,)), dma((2 * levels, JOBS)), dma((2 * levels, JOBS)), dma((JOBS,)), dma((2,)), dma(()), dma((levels + 1,)), dma((levels + 1,)),
        ],
        compiler_params=pltpu.CompilerParams(vmem_limit_bytes=67043328, collective_id=1, has_side_effects=True),
        cost_estimate=pl.CostEstimate(flops=60 << 30, bytes_accessed=64 << 20, transcendentals=8 << 20),
        name="backward",
    )(lens, *arrays)


def unpack_kernel(jobs_ref, dx_ref, small_ref, tok_ref, qkv_ref, qvb_ref, out_ref, up_ref, upb_ref, down_ref, *vec_refs):
    step = pl.program_id(0)
    depth = small_ref.shape[1]

    def unslab(target):
        for i in range(3):
            rows = slice(i * 128, i * 128 + 128)
            target[rows, :JC] = jobs_ref[i, :128, :].astype(F32)
            target[rows, JC:] = jobs_ref[i, 128:, :].astype(F32)

    def tall(store):
        for i in range(3):
            store(i, jobs_ref[i].astype(F32))

    @pl.when(step < 4)
    def _():
        unslab(down_ref)
        tok_ref[...] = dx_ref[...]

    @pl.when((step >= 4) & (step < 8))
    def _():
        for i in range(3):
            up_ref[i * JR:(i + 1) * JR, :] = jobs_ref[i].astype(F32)

    @pl.when(step == 8)
    def _():
        unslab(out_ref)
        for i, ref in enumerate(vec_refs):
            ref[...] = small_ref[i]
        upb_ref[:depth] = small_ref[8]
        upb_ref[depth:] = small_ref[9]
        qvb_ref[0:1, :] = small_ref[10:11, :JC]
        qvb_ref[1:2, :] = small_ref[10:11, JC:]

    @pl.when(step >= 9)
    def _():
        for i in range(3):
            for c in range(3):
                qkv_ref[c, i * JR:(i + 1) * JR, :] = jobs_ref[i, :, c * 128:c * 128 + 128].astype(F32)


def unpack(jobs, dx, small, wide):
    rows, depth = dx.shape

    def rows_at(i):
        return (jnp.minimum(i, 3), 0)

    quarter = pl.BlockSpec((rows // 4, depth), rows_at)

    def whole(shape):
        return pl.BlockSpec(shape, lambda i: (0, 0))

    def flat(size):
        return pl.BlockSpec((size,), lambda i: (0,))

    vec = jax.ShapeDtypeStruct((depth,), F32)
    return pl.pallas_call(
        unpack_kernel,
        grid=(GROUPS,),
        out_shape=(
            jax.ShapeDtypeStruct((rows, depth), F32), jax.ShapeDtypeStruct((3, depth, JC), F32), jax.ShapeDtypeStruct((2, JC), F32),
            jax.ShapeDtypeStruct((JC, depth), F32), jax.ShapeDtypeStruct((depth, wide), F32), jax.ShapeDtypeStruct((wide,), F32),
            jax.ShapeDtypeStruct((wide, depth), F32), vec, vec, vec, vec, vec, vec,
        ),
        in_specs=[pl.BlockSpec((3, JR, JC), lambda i: (i, 0, 0)), quarter, whole((16, depth))],
        out_specs=[
            quarter, pl.BlockSpec((3, depth, 128), lambda i: (0, 0, jnp.clip(i - 9, 0, 2))), whole((2, JC)), whole((JC, depth)),
            pl.BlockSpec((depth, JC), lambda i: (0, jnp.clip(i - 4, 0, 3))), flat(wide), pl.BlockSpec((JC, depth), rows_at),
        ] + [flat(depth)] * 6,
        compiler_params=pltpu.CompilerParams(vmem_limit_bytes=62 << 20),
        name="unpack",
    )(jobs, dx, small)


def body(tokens, lengths, qkv_weight, qv_bias, out_weight, out_bias, first_gain, first_shift, up_weight, up_bias, down_weight, down_bias, second_gain, second_shift, cotangent):
    n_tensor = lax.axis_size("tensor")
    n_dp = lax.axis_size("dp")
    core = lax.axis_index("tensor")
    seqs = lengths.shape[0] // n_tensor
    lens = lax.dynamic_slice(lengths, (core * seqs,), (seqs,))
    levels = 4

    def swap(value):
        return lax.ppermute(value, "tensor", [(0, 1), (1, 0)])

    up_row = up_bias.reshape(1, -1)
    peer_qkv, peer_qv_bias = swap(qkv_weight), swap(qv_bias)
    peer_out, peer_up, peer_up_row, peer_down = swap(out_weight), swap(up_weight), swap(up_row), swap(down_weight)
    q_own, k_own, v_own, c_own = attention(lens, tokens, qkv_weight, qv_bias)
    q_peer, k_peer, v_peer, c_peer = attention(lens, tokens, peer_qkv, peer_qv_bias)
    vecs = jnp.stack([out_bias, first_gain, first_shift, down_bias, second_gain, second_shift, out_bias, out_bias])
    layer_out, h_own, h_peer, gp_own, gp_peer, mid, glow, grad_second, first_in, sums = ffn(
        c_own, c_peer, tokens, cotangent, out_weight, peer_out, up_weight, peer_up, up_row, peer_up_row, down_weight, peer_down, vecs
    )
    jobs, dx, sums = backward(
        levels, lens,
        (
            h_own, h_peer, gp_own, gp_peer, glow, mid, grad_second, first_in, c_own, c_peer, q_own, q_peer, k_own, k_peer, v_own, v_peer, tokens, qkv_weight, peer_qkv, sums,
            up_weight, peer_up, down_weight, peer_down, out_weight, peer_out, vecs,
        ),
    )
    inner = 1 << levels
    if n_dp > inner:
        groups = [[i + inner * g for g in range(n_dp // inner)] for i in range(inner)]
        jobs, sums = lax.psum((jobs, sums), "dp", axis_index_groups=groups)
    grad_tokens, grad_qkv, grad_qv_bias, grad_out, grad_up, grad_up_bias, grad_down, *vectors = unpack(jobs, dx, sums, up_bias.shape[0])
    return (
        layer_out, grad_tokens, grad_qkv, grad_qv_bias, grad_out, vectors[0], vectors[1], vectors[2],
        grad_up, grad_up_bias, grad_down, vectors[3], vectors[4], vectors[5],
    )


def solution(mesh):
    tokens = P(("dp", "tensor"), None)
    columns = P(None, "tensor")
    cube = P(None, None, "tensor")
    split = P("tensor", None)
    return jax.shard_map(
        body,
        mesh=mesh,
        in_specs=(tokens, P("dp"), cube, columns, split, P(), P(), P(), columns, P("tensor"), split, P(), P(), P(), tokens),
        out_specs=(tokens, tokens, cube, columns, split, P(), P(), P(), columns, P("tensor"), split, P(), P(), P()),
        check_vma=False,
    )
```

```python
import functools

import jax
import jax.numpy as jnp
from jax import lax
from jax.experimental import pallas as pl
from jax.experimental.pallas import tpu as pltpu
from jax.sharding import PartitionSpec as P

HD = 64
EPS = 1e-06
BF = jnp.bfloat16
F32 = jnp.float32
NEG = -1000000000.0
JR, JC = 256, 384


def dot(a, b):
    return lax.dot_general(a, b, (((1,), (0,)), ((), ())), preferred_element_type=F32)


def dot_nt(a, b):
    return lax.dot_general(a, b, (((1,), (1,)), ((), ())), preferred_element_type=F32)


def dot_tn(a, b):
    return lax.dot_general(a, b, (((0,), (0,)), ((), ())), preferred_element_type=F32)


def half_masks(shape, dim):
    low = lax.broadcasted_iota(jnp.int32, shape, dim) % (2 * HD) < HD
    return low


def attn_kernel(qb, lens_ref, x_ref, w_ref, b_ref, q_ref, k_ref, v_ref, c_ref):
    length = lens_ref[pl.program_id(0)]
    x = x_ref[...]
    rows, width = q_ref.shape
    scale = HD ** (-0.5)
    q_ref[...] = (dot(x, w_ref[0]) + b_ref[0:1, :]).astype(BF) * jnp.asarray(scale, BF)
    k_ref[...] = dot(x, w_ref[1]).astype(BF)
    v_ref[...] = (dot(x, w_ref[2]) + b_ref[1:2, :]).astype(BF)
    hide = jnp.where(lax.broadcasted_iota(jnp.int32, (rows, 1), 0) < length, 0.0, NEG)
    for pair in range(width // 128):
        lanes = slice(pair * 128, pair * 128 + 128)
        k = k_ref[:, lanes]
        v_t = v_ref[:, lanes].T
        for block in range(rows // qb):
            span = slice(block * qb, block * qb + qb)
            q = q_ref[span, lanes]
            low = half_masks(q.shape, 1)
            zero = jnp.zeros_like(q)
            parts = []
            for head in range(2):
                q_head = jnp.where(low, q, zero) if head == 0 else jnp.where(low, zero, q)
                s = dot_nt(k, q_head)
                s = s + hide
                top = jnp.max(s, axis=0, keepdims=True)
                e = jnp.exp(s - top)
                total = jnp.sum(e, axis=0, keepdims=True)
                c_t = dot(v_t[head * HD:(head + 1) * HD], e.astype(BF))
                parts.append(c_t * (1.0 / total))
            c_ref[span, lanes] = jnp.concatenate(parts, axis=0).T.astype(BF)


def attention(lens, x, weight, bias, qb=512):
    rows, depth = x.shape
    seqs = lens.shape[0]
    seq_len = rows // seqs
    width = weight.shape[2]
    row_spec = pl.BlockSpec((seq_len, width), lambda s, _: (s, 0))
    out = jax.ShapeDtypeStruct((rows, width), BF)
    flops = 2 * rows * depth * width * 3 + 4 * rows * seq_len * width
    return pl.pallas_call(
        functools.partial(attn_kernel, qb),
        out_shape=(out, out, out, out),
        grid_spec=pltpu.PrefetchScalarGridSpec(
            num_scalar_prefetch=1,
            grid=(seqs,),
            in_specs=[
                pl.BlockSpec((seq_len, depth), lambda s, _: (s, 0)),
                pl.BlockSpec(weight.shape, lambda s, _: (0, 0, 0)),
                pl.BlockSpec(bias.shape, lambda s, _: (0, 0)),
            ],
            out_specs=[row_spec] * 4,
        ),
        compiler_params=pltpu.CompilerParams(vmem_limit_bytes=56 << 20),
        cost_estimate=pl.CostEstimate(flops=flops * 3, bytes_accessed=12 << 20, transcendentals=rows * seq_len * width // HD),
        name="attend",
    )(lens, x, weight, bias)


def norm_stats(rows_in):
    centre = rows_in - jnp.mean(rows_in, axis=-1, keepdims=True)
    spread = jnp.mean(centre * centre, axis=-1, keepdims=True)
    root = lax.rsqrt(spread + EPS)
    return centre * root, root


def norm_back(grad, normed, root):
    first = jnp.mean(grad, axis=-1, keepdims=True)
    second = jnp.mean(grad * normed, axis=-1, keepdims=True)
    return root * (grad - first - normed * second)


def gelu_both(u):
    z = jnp.abs(u) * (0.5 ** 0.5)
    t = 1.0 / (1.0 + 0.3275911 * z)
    poly = 1.061405429 * t - 1.453152027
    poly = poly * t + 1.421413741
    poly = poly * t - 0.284496736
    poly = poly * t + 0.254829592
    bell = jnp.exp(-0.5 * (u * u))
    tail = 0.5 * (poly * t) * bell
    phi_cdf = jnp.where(u < 0.0, tail, 1.0 - tail)
    return u * phi_cdf, phi_cdf + u * (bell * 0.3989422804014327)


def ffn_kernel(
    chunk,
    c_own, c_peer, x_ref, cot_ref, wo_own_in, wo_peer_in, wu_own_in, wu_peer_in, bu_own, bu_peer, wd_own_in, wd_peer_in, vec_ref,
    out_ref, h_own, h_peer, gp_own, gp_peer, mid_ref, glow_ref, gs_ref, fin_ref, small_ref,
    wo_own, wo_peer, wu_own, wu_peer, wd_own, wd_peer, sem,
):
    step = pl.program_id(0)
    pieces = ((wo_own_in, wo_own), (wo_peer_in, wo_peer), (wu_own_in, wu_own), (wd_own_in, wd_own), (wu_peer_in, wu_peer), (wd_peer_in, wd_peer))
    copies = [pltpu.make_async_copy(src, dst, sem.at[i]) for i, (src, dst) in enumerate(pieces)]

    @pl.when(step == 0)
    def _():
        for copy in copies:
            copy.start()

    def arrived(group):
        @pl.when(step == 0)
        def _():
            for copy in copies[2 * group:2 * group + 2]:
                copy.wait()

    wide = wu_own.shape[1]
    out_bias, gain1, shift1, down_bias, gain2, shift2 = (vec_ref[i:i + 1, :] for i in range(6))

    @pl.when(step == 0)
    def _():
        small_ref[...] = jnp.zeros_like(small_ref)

    def colsum(index, value):
        small_ref[index:index + 1, :] += jnp.sum(value, axis=0, keepdims=True)

    arrived(0)
    attn_sum = dot(c_own[...], wo_own[...]) + dot(c_peer[...], wo_peer[...])
    first_in = x_ref[...].astype(F32) + attn_sum + out_bias
    fin_ref[...] = first_in
    n1, _ = norm_stats(first_in)
    first_out = n1 * gain1 + shift1
    middle = first_out.astype(BF)
    mid_ref[...] = middle
    ffn_sum = jnp.zeros_like(first_out)
    for group, (wu, bu, wd, h_ref, gp_ref) in enumerate(((wu_own, bu_own, wd_own, h_own, gp_own), (wu_peer, bu_peer, wd_peer, h_peer, gp_peer))):
        arrived(group + 1)
        for at in range(0, wide, chunk):
            cols = slice(at, at + chunk)
            u = dot(middle, wu[:, cols]) + bu[:, cols]
            act, slope = gelu_both(u)
            act = act.astype(BF)
            h_ref[:, cols] = act
            gp_ref[:, cols] = slope.astype(BF)
            ffn_sum = ffn_sum + dot(act, wd[cols, :])
    n2, root2 = norm_stats(first_out + ffn_sum + down_bias)
    out_ref[...] = n2 * gain2 + shift2
    cot = cot_ref[...].astype(F32)
    colsum(4, cot * n2)
    colsum(5, cot)
    grad_second = norm_back(cot * gain2, n2, root2)
    colsum(3, grad_second)
    glow_ref[...] = grad_second.astype(BF)
    gs_ref[...] = grad_second


def ffn(c_own, c_peer, x, cot, wo_own, wo_peer, wu_own, wu_peer, bu_own, bu_peer, wd_own, wd_peer, vecs, tile=256):
    rows, depth = x.shape
    half = c_own.shape[1]
    wide = wu_own.shape[1]
    chunk = depth

    def tiled(cols):
        return pl.BlockSpec((tile, cols), lambda i: (i, 0))

    def fixed(shape):
        return pl.BlockSpec(shape, lambda i: (0, 0), pipeline_mode=pl.Buffered(1))

    def sds(cols, dtype):
        return jax.ShapeDtypeStruct((rows, cols), dtype)

    hbm = pl.BlockSpec(memory_space=pl.ANY)
    fixed_in = (wo_own, wo_peer, wu_own, wu_peer, bu_own, bu_peer, wd_own, wd_peer, vecs)
    return pl.pallas_call(
        functools.partial(ffn_kernel, chunk),
        grid=(rows // tile,),
        out_shape=(
            sds(depth, F32), sds(wide, BF), sds(wide, BF), sds(wide, BF), sds(wide, BF),
            sds(depth, BF), sds(depth, BF), sds(depth, F32), sds(depth, F32),
            jax.ShapeDtypeStruct((16, depth), F32),
        ),
        in_specs=[tiled(half), tiled(half), tiled(depth), tiled(depth)] + [hbm if a.dtype == BF else fixed(a.shape) for a in fixed_in],
        out_specs=[
            tiled(depth), tiled(wide), tiled(wide), tiled(wide), tiled(wide),
            tiled(depth), tiled(depth), tiled(depth), tiled(depth),
            pl.BlockSpec((16, depth), lambda i: (0, 0)),
        ],
        scratch_shapes=[pltpu.VMEM(a.shape, BF) for a in (wo_own, wo_peer, wu_own, wu_peer, wd_own, wd_peer)] + [pltpu.SemaphoreType.DMA((6,))],
        compiler_params=pltpu.CompilerParams(vmem_limit_bytes=60 << 20),
        cost_estimate=pl.CostEstimate(flops=rows * depth * (4 * 2 * wide + 4 * depth), bytes_accessed=48 << 20, transcendentals=rows * wide * 2),
        name="feed",
    )(c_own, c_peer, x, cot, *fixed_in)


LAGS = (1, 3, 5, 7, 9, 12, 14, 16, 19)
GROUPS = 12
BLOCKS = 1
JOBS = 3 * GROUPS


def back_kernel(
    levels,
    lens_ref, h_own, h_peer, gp_own, gp_peer, glow_in, mid_in, gs_in, fin_in, c_own, c_peer, q_own, q_peer, k_own, k_peer, v_own, v_peer, x_in, w_own, w_peer, small_in,
    wu_own, wu_peer, wd_own, wd_peer, wo_own, wo_peer, vec_in,
    job_out, dx_out, small_out,
    buf, ring, prec, rbuf, blocks, glow, mid, flow, ctx, qv, kv, vv, dov, wv, wdb, acc, fin, vec, dq, dk, dv, dxs, small, small_sum, small_send, small_recv,
    load_sem, blk_sem, wt_sem, core_send, core_recv, hop_send, hop_recv, out_sem, dx_sem, small_sem, sum_send, sum_recv,
):
    dp = lax.axis_index("dp")
    core = lax.axis_index("tensor")
    half = ctx.shape[1] // 2
    rows, depth = glow.shape
    seqs = lens_ref.shape[0]
    seq_len = rows // seqs
    pairs = qv.shape[1] // 128
    scale = HD ** (-0.5)
    other = (dp, 1 - core)

    def partner(level, job):
        flip = job & 1
        shift = (flip, 2, 1 - flip, 3)[level]
        bit = (dp >> shift) & 1
        return bit, (dp ^ (1 << shift), core)

    def loads():
        return (
            (glow_in, glow, 0), (mid_in, mid, 1), (c_own, ctx.at[:, :half], 2), (c_peer, ctx.at[:, half:], 3), (gs_in, acc, 4),
            (q_own, qv.at[:, :half], 5), (q_peer, qv.at[:, half:], 6), (k_own, kv.at[:, :half], 7), (k_peer, kv.at[:, half:], 8),
            (v_own, vv.at[:, :half], 9), (v_peer, vv.at[:, half:], 10), (fin_in, fin, 11), (x_in, mid, 12), (w_own, wv.at[0], 13), (w_peer, wv.at[1], 14), (small_in, small, 15),
            (vec_in, vec, 16), (wo_own, wdb.at[0, 0], 17), (wo_peer, wdb.at[0, 1], 18),
        )

    def load(index):
        src, dst, sem = loads()[index]
        return pltpu.make_async_copy(src, dst, load_sem.at[sem])

    def block_copies(src_own, src_peer, index, slot):
        cols = pl.ds(pl.multiple_of(index * JC, 128), JC)
        return (
            pltpu.make_async_copy(src_own.at[:, cols], blocks.at[slot, 0], blk_sem.at[slot, 0]),
            pltpu.make_async_copy(src_peer.at[:, cols], blocks.at[slot, 1], blk_sem.at[slot, 1]),
        )

    def start_blocks(index):
        @pl.when(index < 4)
        def _():
            for copy in block_copies(h_own, h_peer, index, (index & 1)):
                copy.start()

        @pl.when((index >= 4) & (index < 8))
        def _():
            for copy in block_copies(gp_own, gp_peer, index - 4, (index & 1)):
                copy.start()

    def weight_copies(index, side):
        slot = (index & 1)
        span = pl.ds(pl.multiple_of(index * JC, 128), JC)
        up, down = ((wu_own, wd_own), (wu_peer, wd_peer))[side]
        return (
            pltpu.make_async_copy(up.at[:, span], wv.at[side, slot], wt_sem.at[0, slot, side]),
            pltpu.make_async_copy(down.at[span], wdb.at[slot, side], wt_sem.at[1, slot, side]),
        )

    def start_weights(index):
        for side in range(2):
            for copy in weight_copies(index, side):
                copy.start()

    def core_copy(job):
        return pltpu.make_async_remote_copy(
            src_ref=ring.at[job - 9 * (job * 57 >> 9)], dst_ref=prec.at[job], send_sem=core_send.at[job], recv_sem=core_recv.at[job],
            device_id=other, device_id_type=pl.DeviceIdType.MESH,
        )

    def offsets(job):
        spots = [0]
        for level in range(levels):
            bit, _ = partner(level, job)
            spots.append(spots[-1] + (bit << ((JR >> (level + 1)).bit_length() - 1)))
        return spots

    def hop(job, stage):
        if stage < levels:
            level = stage
            size = JR >> (level + 1)
            bit, device = partner(level, job)
            at = pl.multiple_of(offsets(job)[level] + (1 - bit) * size, 16)
            src = buf.at[job, pl.ds(at, size)]
            begin = JR - (JR >> level)
            dst = rbuf.at[job, begin:begin + size]
        else:
            level = 2 * levels - 1 - stage
            size = JR >> (level + 1)
            bit, device = partner(level, job)
            at = pl.multiple_of(offsets(job)[level + 1], 16)
            src = prec.at[job, pl.ds(at, size)]
            dst = prec.at[job, pl.ds(at, size)]
        return pltpu.make_async_remote_copy(
            src_ref=src, dst_ref=dst, send_sem=hop_send.at[stage, job], recv_sem=hop_recv.at[stage, job],
            device_id=device, device_id_type=pl.DeviceIdType.MESH,
        )

    def stage_op(stage, job):
        if stage == 0:
            core_copy(job).wait_recv()
            buf[job] = buf[job] + prec[job]
            hop(job, 0).start()
            return
        before = hop(job, stage - 1)
        before.wait_recv()
        if stage <= levels:
            level = stage - 1
            size = JR >> stage
            at = pl.multiple_of(offsets(job)[stage], 16)
            begin = JR - (JR >> level)
            keep = buf[job, pl.ds(at, size)] + rbuf[job, begin:begin + size]
            target = prec if stage == levels else buf
            target[job, pl.ds(at, size)] = keep
        if stage < 2 * levels:
            hop(job, stage).start()
        else:
            pltpu.make_async_copy(prec.at[job], job_out.at[job], out_sem.at[job]).start()
        before.wait_send()

    def emit_side(group, which, pieces):
        for i, (top, bottom) in enumerate(pieces):
            job = group * 3 + i
            target = buf.at[job] if which == 0 else ring.at[job - 9 * (job * 57 >> 9)]
            cut = top.shape[0]
            target[:cut, :] = top.astype(BF)
            if bottom is not None:
                target[cut:, :] = bottom.astype(BF)
            if which == 1:
                core_copy(job).start()

    def emit(group, own, peer):
        emit_side(group, 1, peer)
        emit_side(group, 0, own)

    def free_ring(group):
        @pl.when(group >= 3)
        def _():
            for i in range(3):
                core_copy((group - 3) * 3 + i).wait_send()

    def slabs(block):
        return [(block[i * 128:(i + 1) * 128, :JC], block[i * 128:(i + 1) * 128, JC:]) for i in range(3)]

    def tall(block):
        return [(block[i * JR:(i + 1) * JR], None) for i in range(3)]

    def down_phase(index):
        @pl.when(index == 0)
        def _():
            load(0).wait()

        for copy in block_copies(h_own, h_peer, index, (index & 1)):
            copy.wait()
        free_ring(index)
        right = glow[...]
        slot = (index & 1)
        emit(index, slabs(dot_tn(blocks[slot, 0], right)), slabs(dot_tn(blocks[slot, 1], right)))
        start_blocks(index + 2)

    def up_phase(index, side):
        slot = (index & 1)
        if side == 0:
            @pl.when(index == 0)
            def _():
                for i in (1, 4, 15):
                    load(i).wait()

            free_ring(index + 4)
        block_copies(gp_own, gp_peer, index, slot)[side].wait()
        for copy in weight_copies(index, side):
            copy.wait()
        grad_up = (dot_nt(glow[...], wdb[slot, side]) * blocks[slot, side].astype(F32)).astype(BF)
        total = jnp.sum(grad_up.astype(F32), axis=0, keepdims=True)
        for row in range(2):
            @pl.when(index // 2 == row)
            def _():
                lanes = pl.ds(pl.multiple_of(((index & 1)) * JC, 128), JC)
                small[8 + 2 * side + row:9 + 2 * side + row, lanes] = total
        blocks[slot, side] = grad_up
        emit_side(index + 4, side, tall(dot_tn(mid[...], grad_up)))

    def first_phase(index):
        slot = index & 1
        acc[...] = acc[...] + (dot_nt(blocks[slot, 0], wv[0, slot]) + dot_nt(blocks[slot, 1], wv[1, slot]))
        start_blocks(index + 6)

        @pl.when(index < 2)
        def _():
            start_weights(index + 2)

        @pl.when(index == 2)
        def _():
            load(17).start()
            load(18).start()

        @pl.when(index == 3)
        def _():
            for i in (12, 13, 14):
                load(i).start()

    def norm_phase(index):
        @pl.when(index == 0)
        def _():
            for i in (11, 16, 17, 18):
                load(i).wait()
            small[0:3, :] = jnp.zeros((3, depth), F32)

        gain1 = vec[1:2, :]

        def piece(i, carry):
            span = pl.ds(pl.multiple_of(index * (rows // 2) + i * JR, JR), JR)
            n1, root1 = norm_stats(fin[span, :])
            grad = acc[span, :]
            small[1:2, :] += jnp.sum(grad * n1, axis=0, keepdims=True)
            small[2:3, :] += jnp.sum(grad, axis=0, keepdims=True)
            grad_first = norm_back(grad * gain1, n1, root1)
            small[0:1, :] += jnp.sum(grad_first, axis=0, keepdims=True)
            acc[span, :] = grad_first
            low = grad_first.astype(BF)
            flow[span, :] = low
            dov[span, :half] = dot_nt(low, wdb[0, 0]).astype(BF)
            dov[span, half:] = dot_nt(low, wdb[0, 1]).astype(BF)
            return carry

        lax.fori_loop(0, rows // 2 // JR, piece, 0)

    def out_phase():
        for i in (2, 3):
            load(i).wait()
        free_ring(8)
        right = flow[...]
        emit(8, slabs(dot_tn(ctx[:, :half], right)), slabs(dot_tn(ctx[:, half:], right)))

    def add_bias(pair, offset, value):
        total = jnp.sum(value.astype(F32), axis=0, keepdims=True)
        for side in range(2):
            @pl.when(pair // (pairs // 2) == side)
            def _():
                lanes = pl.ds(pl.multiple_of(offset + (pair - side * (pairs // 2)) * 128, 128), 128)
                small[12 + side:13 + side, lanes] += total

    def sum_hop(stage):
        if stage == 0:
            src, device = small_send, other
        else:
            src, device = small_sum.at[stage - 1], partner(stage - 1, 0)[1]
        return pltpu.make_async_remote_copy(
            src_ref=src, dst_ref=small_recv.at[stage], send_sem=sum_send.at[stage], recv_sem=sum_recv.at[stage],
            device_id=device, device_id_type=pl.DeviceIdType.MESH,
        )

    def sum_phase(stage):
        if stage == 0:
            small_send[0:8, :] = small[0:8, :]
            small_send[8:10, :] = small[10:12, :]
            small_send[10:11, :] = small[13:14, :]
            small_send[11:16, :] = jnp.zeros((5, depth), F32)
        else:
            sum_hop(stage - 1).wait_recv()
            sum_hop(stage - 1).wait_send()
            if stage == 1:
                got = small_recv[0]
                small_sum[0, 0:8, :] = small[0:8, :] + got[0:8, :]
                small_sum[0, 8:10, :] = small[8:10, :] + got[8:10, :]
                small_sum[0, 10:11, :] = small[12:13, :] + got[10:11, :]
                small_sum[0, 11:16, :] = jnp.zeros((5, depth), F32)
            else:
                small_sum[stage - 1] = small_sum[stage - 2] + small_recv[stage - 1]
        if stage <= levels:
            sum_hop(stage).start()
        else:
            pltpu.make_async_copy(small_sum.at[levels], small_out, small_sem).start()

    def attend_phase(unit):
        @pl.when(unit == 0)
        def _():
            for i in range(5, 11):
                load(i).wait()
            small[12:14, :] = jnp.zeros((2, depth), F32)

        inner = unit % (2 * seqs)
        seq = inner % seqs
        pair = unit // (2 * seqs) + (inner // seqs) * (pairs // 2)
        length = lens_ref[seq]
        span = pl.ds(pl.multiple_of(seq * seq_len, seq_len), seq_len)
        lanes = pl.ds(pl.multiple_of(pair * 128, 128), 128)
        k = kv[span, lanes]
        v = vv[span, lanes]
        k_t = k.T
        hide = jnp.where(lax.broadcasted_iota(jnp.int32, (seq_len, 1), 0) < length, 0.0, NEG)
        low = half_masks((1, 128), 1)
        qb = seq_len // BLOCKS
        grad_k = jnp.zeros((seq_len, 128), F32)
        grad_v = jnp.zeros((seq_len, 128), F32)
        for block in range(BLOCKS):
            part = pl.ds(pl.multiple_of(seq * seq_len + block * qb, qb), qb)
            q = qv[part, lanes]
            do = dov[part, lanes]
            grad_q = []
            for head in range(2):
                pick = low if head == 0 else jnp.logical_not(low)
                q_head = jnp.where(pick, q, jnp.zeros_like(q))
                do_head = jnp.where(pick, do, jnp.zeros_like(do))
                s = dot_nt(k, q_head)
                s = s + hide
                e = jnp.exp(s - jnp.max(s, axis=0, keepdims=True))
                weights = e * (1.0 / jnp.sum(e, axis=0, keepdims=True))
                grad_probs = dot_nt(v, do_head)
                grad_v = grad_v + dot(weights.astype(BF), do_head)
                row_terms = jnp.sum(weights * grad_probs, axis=0, keepdims=True)
                grad_s = (weights * (grad_probs - row_terms)).astype(BF)
                grad_k = grad_k + dot(grad_s, q_head)
                grad_q.append(dot(k_t[head * HD:(head + 1) * HD], grad_s) * scale)
            grad_q = jnp.concatenate(grad_q, axis=0).T.astype(BF)
            dq[part, lanes] = grad_q
            add_bias(pair, 0, grad_q)
        grad_v = grad_v.astype(BF)
        dk[span, lanes] = grad_k.astype(BF)
        dv[span, lanes] = grad_v
        add_bias(pair, half, grad_v)

    def proj_phase(index):
        @pl.when(index == 0)
        def _():
            load(12).wait()

        free_ring(index + 9)
        left = mid[...]
        for side in (1, 0):
            lanes = pl.ds(pl.multiple_of(side * half + index * 128, 128), 128)
            right = jnp.concatenate([dq[:, lanes], dk[:, lanes], dv[:, lanes]], axis=1)
            emit_side(index + 9, side, tall(dot_tn(left, right)))

    def dx_copy(index):
        span = pl.ds(pl.multiple_of(index * JR, JR), JR)
        return pltpu.make_async_copy(dxs.at[(index & 1)], dx_out.at[span], dx_sem.at[(index & 1)])

    def dx_phase(index):
        @pl.when(index == 0)
        def _():
            load(13).wait()
            load(14).wait()

        @pl.when(index >= 2)
        def _():
            dx_copy(index - 2).wait()

        span = pl.ds(pl.multiple_of(index * JR, JR), JR)
        total = jnp.zeros((JR, depth), F32)
        for side in range(2):
            cols = slice(side * half, side * half + half)
            part = jnp.zeros((JR, depth), F32)
            for i, grad in enumerate((dq, dk, dv)):
                part = part + dot_nt(grad[span, cols], wv[side, i])
            total = total + part
        dxs[(index & 1)] = total + acc[span, :]
        dx_copy(index).start()

    barrier = pltpu.get_barrier_semaphore()
    pl.semaphore_signal(barrier, inc=1, device_id=other, device_id_type=pl.DeviceIdType.MESH)
    for level in range(levels):
        pl.semaphore_signal(barrier, inc=1, device_id=partner(level, 0)[1], device_id_type=pl.DeviceIdType.MESH)
    load(0).start()
    start_blocks(0)
    start_blocks(1)
    load(1).start()
    start_weights(0)
    start_weights(1)
    for i in (4, 15, 11, 16, 2, 3, 5, 6, 7, 8, 9, 10):
        load(i).start()
    pl.semaphore_wait(barrier, levels + 1)

    norm_at = 4 + 3 * 4
    first = norm_at + 2 + 1
    turn = 3 * seqs
    after = first + turn * (pairs // 2)
    early = JOBS - 3
    gap = max(after - 1 - early, 0)
    end = max(JOBS + gap + LAGS[2 * levels], after + 2 * levels + 4)

    def comm(step, low, high):
        for stage in range(2 * levels, -1, -1):
            slot = step - LAGS[stage]
            most, least = high - LAGS[stage], low - LAGS[stage]
            if most < 0:
                continue
            if most < early:
                job, here = slot, slot >= 0
            else:
                job = slot - jnp.where(slot >= early, gap, 0)
                here = (slot >= 0) & ((slot < early) | (job >= early)) & (job < JOBS)
            if least >= 0 and most < early:
                stage_op(stage, job)
            else:
                @pl.when(here)
                def _():
                    stage_op(stage, job)

    def down_part(t, carry):
        comm(t, 0, 3)
        down_phase(t)
        return carry

    def up_part(i, carry):
        for side in range(2):
            comm(4 + 3 * i + side, 4, norm_at - 1)
            up_phase(i, side)
        comm(6 + 3 * i, 4, norm_at - 1)
        first_phase(i)
        return carry

    def norm_part(i, carry):
        comm(norm_at + i, norm_at, norm_at + 1)
        norm_phase(i)
        return carry

    def head_part(p, carry):
        def unit_part(u, inner):
            t = first + turn * p + (u >> 1) * 3 + (u & 1)
            comm(t, first, after - 1)
            attend_phase(p * (2 * seqs) + u)

            @pl.when((u & 1) == 1)
            def _():
                comm(t + 1, first, after - 1)

            return inner

        lax.fori_loop(0, 2 * seqs, unit_part, 0)
        proj_phase(p)
        return carry

    def last_part(t, carry):
        comm(t, after, end - 1)

        @pl.when(t < after + rows // JR)
        def _():
            dx_phase(t - after)

        for stage in range(levels + 2):
            @pl.when(t == after + 1 + 2 * stage)
            def _():
                sum_phase(stage)

        return carry

    lax.fori_loop(0, 4, down_part, 0)
    lax.fori_loop(0, 4, up_part, 0)
    lax.fori_loop(0, 2, norm_part, 0)
    comm(jnp.int32(first - 1), first - 1, first - 1)
    out_phase()
    lax.fori_loop(0, pairs // 2, head_part, 0)
    lax.fori_loop(after, end, last_part, 0)
    for group in (GROUPS - 3, GROUPS - 2, GROUPS - 1):
        for i in range(3):
            core_copy(group * 3 + i).wait_send()
    dx_copy(rows // JR - 2).wait()
    dx_copy(rows // JR - 1).wait()

    def finish(job, carry):
        pltpu.make_async_copy(prec.at[job], job_out.at[job], out_sem.at[job]).wait()
        return carry

    lax.fori_loop(0, JOBS, finish, 0)
    pltpu.make_async_copy(small_sum.at[levels], small_out, small_sem).wait()


def backward(levels, lens, arrays):
    glow, c_own = arrays[4], arrays[8]
    rows, depth = glow.shape
    half = c_own.shape[1]
    hbm = pl.BlockSpec(memory_space=pl.ANY)
    square = pltpu.VMEM((rows, depth), BF)
    dma = pltpu.SemaphoreType.DMA
    return pl.pallas_call(
        functools.partial(back_kernel, levels),
        out_shape=(
            jax.ShapeDtypeStruct((JOBS, JR, JC), BF),
            jax.ShapeDtypeStruct((rows, depth), F32),
            jax.ShapeDtypeStruct((16, depth), F32),
        ),
        in_specs=[pl.BlockSpec(memory_space=pltpu.SMEM)] + [hbm] * len(arrays),
        out_specs=(hbm, hbm, hbm),
        scratch_shapes=[
            pltpu.VMEM((JOBS, JR, JC), BF), pltpu.VMEM((9, JR, JC), BF), pltpu.VMEM((JOBS, JR, JC), BF),
            pltpu.VMEM((JOBS, JR - (JR >> levels), JC), BF), pltpu.VMEM((2, 2, rows, JC), BF),
            square, square, square, square, square, square, square, square,
            pltpu.VMEM((2, 3, depth, half), BF), pltpu.VMEM((2, 2, JC, depth), BF), pltpu.VMEM((rows, depth), F32), pltpu.VMEM((rows, depth), F32), pltpu.VMEM((8, depth), F32), square, square, square,
            pltpu.VMEM((2, JR, depth), F32), pltpu.VMEM((16, depth), F32),
            pltpu.VMEM((levels + 1, 16, depth), F32), pltpu.VMEM((16, depth), F32), pltpu.VMEM((levels + 1, 16, depth), F32),
            dma((19,)), dma((2, 2)), dma((2, 2, 2)), dma((JOBS,)), dma((JOBS,)), dma((2 * levels, JOBS)), dma((2 * levels, JOBS)), dma((JOBS,)), dma((2,)), dma(()), dma((levels + 1,)), dma((levels + 1,)),
        ],
        compiler_params=pltpu.CompilerParams(vmem_limit_bytes=67043328, collective_id=1, has_side_effects=True),
        cost_estimate=pl.CostEstimate(flops=60 << 30, bytes_accessed=64 << 20, transcendentals=8 << 20),
        name="backward",
    )(lens, *arrays)


def unpack_kernel(jobs_ref, dx_ref, small_ref, tok_ref, qkv_ref, qvb_ref, out_ref, up_ref, upb_ref, down_ref, *vec_refs):
    step = pl.program_id(0)
    depth = small_ref.shape[1]

    def unslab(target):
        for i in range(3):
            rows = slice(i * 128, i * 128 + 128)
            target[rows, :JC] = jobs_ref[i, :128, :].astype(F32)
            target[rows, JC:] = jobs_ref[i, 128:, :].astype(F32)

    def tall(store):
        for i in range(3):
            store(i, jobs_ref[i].astype(F32))

    @pl.when(step < 4)
    def _():
        unslab(down_ref)
        tok_ref[...] = dx_ref[...]

    @pl.when((step >= 4) & (step < 8))
    def _():
        for i in range(3):
            up_ref[i * JR:(i + 1) * JR, :] = jobs_ref[i].astype(F32)

    @pl.when(step == 8)
    def _():
        unslab(out_ref)
        for i, ref in enumerate(vec_refs):
            ref[...] = small_ref[i]
        upb_ref[:depth] = small_ref[8]
        upb_ref[depth:] = small_ref[9]
        qvb_ref[0:1, :] = small_ref[10:11, :JC]
        qvb_ref[1:2, :] = small_ref[10:11, JC:]

    @pl.when(step >= 9)
    def _():
        for i in range(3):
            for c in range(3):
                qkv_ref[c, i * JR:(i + 1) * JR, :] = jobs_ref[i, :, c * 128:c * 128 + 128].astype(F32)


def unpack(jobs, dx, small, wide):
    rows, depth = dx.shape

    def rows_at(i):
        return (jnp.minimum(i, 3), 0)

    quarter = pl.BlockSpec((rows // 4, depth), rows_at)

    def whole(shape):
        return pl.BlockSpec(shape, lambda i: (0, 0))

    def flat(size):
        return pl.BlockSpec((size,), lambda i: (0,))

    vec = jax.ShapeDtypeStruct((depth,), F32)
    return pl.pallas_call(
        unpack_kernel,
        grid=(GROUPS,),
        out_shape=(
            jax.ShapeDtypeStruct((rows, depth), F32), jax.ShapeDtypeStruct((3, depth, JC), F32), jax.ShapeDtypeStruct((2, JC), F32),
            jax.ShapeDtypeStruct((JC, depth), F32), jax.ShapeDtypeStruct((depth, wide), F32), jax.ShapeDtypeStruct((wide,), F32),
            jax.ShapeDtypeStruct((wide, depth), F32), vec, vec, vec, vec, vec, vec,
        ),
        in_specs=[pl.BlockSpec((3, JR, JC), lambda i: (i, 0, 0)), quarter, whole((16, depth))],
        out_specs=[
            quarter, pl.BlockSpec((3, depth, 128), lambda i: (0, 0, jnp.clip(i - 9, 0, 2))), whole((2, JC)), whole((JC, depth)),
            pl.BlockSpec((depth, JC), lambda i: (0, jnp.clip(i - 4, 0, 3))), flat(wide), pl.BlockSpec((JC, depth), rows_at),
        ] + [flat(depth)] * 6,
        compiler_params=pltpu.CompilerParams(vmem_limit_bytes=62 << 20),
        name="unpack",
    )(jobs, dx, small)


def body(tokens, lengths, qkv_weight, qv_bias, out_weight, out_bias, first_gain, first_shift, up_weight, up_bias, down_weight, down_bias, second_gain, second_shift, cotangent):
    n_tensor = lax.axis_size("tensor")
    n_dp = lax.axis_size("dp")
    core = lax.axis_index("tensor")
    seqs = lengths.shape[0] // n_tensor
    lens = lax.dynamic_slice(lengths, (core * seqs,), (seqs,))
    levels = 4

    def swap(value):
        return lax.ppermute(value, "tensor", [(0, 1), (1, 0)])

    up_row = up_bias.reshape(1, -1)
    peer_qkv, peer_qv_bias = swap(qkv_weight), swap(qv_bias)
    peer_out, peer_up, peer_up_row, peer_down = swap(out_weight), swap(up_weight), swap(up_row), swap(down_weight)
    q_own, k_own, v_own, c_own = attention(lens, tokens, qkv_weight, qv_bias)
    q_peer, k_peer, v_peer, c_peer = attention(lens, tokens, peer_qkv, peer_qv_bias)
    vecs = jnp.stack([out_bias, first_gain, first_shift, down_bias, second_gain, second_shift, out_bias, out_bias])
    layer_out, h_own, h_peer, gp_own, gp_peer, mid, glow, grad_second, first_in, sums = ffn(
        c_own, c_peer, tokens, cotangent, out_weight, peer_out, up_weight, peer_up, up_row, peer_up_row, down_weight, peer_down, vecs
    )
    jobs, dx, sums = backward(
        levels, lens,
        (
            h_own, h_peer, gp_own, gp_peer, glow, mid, grad_second, first_in, c_own, c_peer, q_own, q_peer, k_own, k_peer, v_own, v_peer, tokens, qkv_weight, peer_qkv, sums,
            up_weight, peer_up, down_weight, peer_down, out_weight, peer_out, vecs,
        ),
    )
    inner = 1 << levels
    if n_dp > inner:
        groups = [[i + inner * g for g in range(n_dp // inner)] for i in range(inner)]
        jobs, sums = lax.psum((jobs, sums), "dp", axis_index_groups=groups)
    grad_tokens, grad_qkv, grad_qv_bias, grad_out, grad_up, grad_up_bias, grad_down, *vectors = unpack(jobs, dx, sums, up_bias.shape[0])
    return (
        layer_out, grad_tokens, grad_qkv, grad_qv_bias, grad_out, vectors[0], vectors[1], vectors[2],
        grad_up, grad_up_bias, grad_down, vectors[3], vectors[4], vectors[5],
    )


def solution(mesh):
    tokens = P(("dp", "tensor"), None)
    columns = P(None, "tensor")
    cube = P(None, None, "tensor")
    split = P("tensor", None)
    return jax.shard_map(
        body,
        mesh=mesh,
        in_specs=(tokens, P("dp"), cube, columns, split, P(), P(), P(), columns, P("tensor"), split, P(), P(), P(), tokens),
        out_specs=(tokens, tokens, cube, columns, split, P(), P(), P(), columns, P("tensor"), split, P(), P(), P()),
        check_vma=False,
    )
```
